32 devices in a mesh: dp: 4 (over x, core), tm: 8 (over z, y).
Axes of the slice: x: 2, y: 2, z: 4, core: 2. Of those that a mesh axis runs over, the one named last changes fastest.
Arguments:
- latent: float32 [4, 64, 4096], P('dp', None, 'tm'), may hold values from -40 to 40
- target: float32 [4, 8192], P('dp', 'tm'), may hold values from -20 to 20
- up_kernel: float32 [4, 32, 64], replicated, may hold values from -0.5 to 0.5
- inner_kernel: float32 [3, 16, 32], replicated, may hold values from -0.625 to 0.625
- outer_kernel: float32 [32, 16], replicated, may hold values from -1.5 to 1.5
- out_kernel: float32 [7, 32], replicated, may hold values from -0.375 to 0.375
Outputs:
- latent_grad: float32 [4, 64, 4096], P('dp', None, 'tm')
- up_update: float32 [4, 32, 64], replicated
- inner_update: float32 [3, 16, 32], replicated
- outer_update: float32 [32, 16], replicated
- out_update: float32 [7, 32], replicated
The draws below stay inside these ranges and needn't reach their ends.
All inputs are finite; a program needn't handle non-finite values.
Results may differ from the reference program's by a relative error of at most 0.0003.
Values sent between devices are 32-bit elements; how exact they have to be, the bound alone decides.
No kernel may reach another device: no remote copies, remote signals or barrier semaphores. Data moves between devices by JAX's collectives and lax.ppermute only.
A program may use at most 64 MiB of HBM per device.

```python
import jax
import jax.numpy as jnp
from jax import lax

CH = 64
MELS = 64
WIN_COARSE = 1024
WIN_FINE = 256
CLIPS = 4
TIME = 8192
FRAMES = 4096
PARAMS = 10464


def draw_latent(key, part):
    noise_key, clip_key, block_key = jax.random.split(jax.random.fold_in(key, 11), 3)
    positions = jnp.arange(FRAMES, dtype=jnp.float32) / FRAMES
    gaussian = jax.random.truncated_normal(noise_key, -4.0, 4.0, (CLIPS, CH, FRAMES), jnp.float32)
    rising = 1.0 + positions
    blocks_scale = jnp.exp(jax.random.uniform(block_key, (CLIPS, 1, FRAMES // 16), jnp.float32, jnp.log(0.5), jnp.log(2.5)))
    clip_scale = jnp.exp(jax.random.uniform(clip_key, (CLIPS, 1, 1), jnp.float32, jnp.log(0.5), jnp.log(2.0)))
    return gaussian * rising * clip_scale * jnp.repeat(blocks_scale, 16, axis=2)


def draw_target(key, part):
    noise_key, block_key = jax.random.split(jax.random.fold_in(key, 23), 2)
    positions = jnp.arange(TIME, dtype=jnp.float32) / TIME
    gaussian = jax.random.truncated_normal(noise_key, -4.0, 4.0, (CLIPS, TIME), jnp.float32)
    rising = 1.0 + positions
    blocks_scale = jnp.exp(jax.random.uniform(block_key, (CLIPS, TIME // 128), jnp.float32, jnp.log(0.5), jnp.log(2.5)))
    return gaussian * rising * jnp.repeat(blocks_scale, 128, axis=1)


def normal_values(own_key, dims, spread, most, kind=jnp.bfloat16):
    drawn = spread * jax.random.normal(own_key, dims, jnp.float32)
    return jnp.clip(drawn, min=-most, max=most).astype(kind)


def setup_inputs(seed: int = 0) -> dict:
    keys = jax.random.split(jax.random.key(seed), 7)
    return {
        "latent": draw_latent(jax.random.fold_in(keys[6], 71), 0),
        "target": draw_target(jax.random.fold_in(keys[6], 71), 0),
        "up_kernel": normal_values(keys[2], (4, CH // 2, CH), (2 * CH) ** -0.5, 0.5, jnp.float32),
        "inner_kernel": normal_values(keys[3], (3, CH // 4, CH // 2), (3 * CH // 2) ** -0.5, 0.625, jnp.float32),
        "outer_kernel": normal_values(keys[4], (CH // 2, CH // 4), (CH // 4) ** -0.5, 1.5, jnp.float32),
        "out_kernel": normal_values(keys[5], (7, CH // 2), (7 * CH // 2) ** -0.5, 0.375, jnp.float32),
    }


LOSS_WEIGHTS = (0.25, 0.5, 0.5)

def product(form, left, right):
    return jnp.einsum(form, left, right, precision=lax.Precision.HIGHEST, preferred_element_type=jnp.float32)

def mel_bank(window, mel_count):
    half_window = window // 2
    top_mel = 2595.0 * jnp.log10(1.0 + 12000.0 / 700.0)
    points = (jnp.arange(mel_count + 1, dtype=jnp.float32) + 1.0) / (mel_count + 2.0) * top_mel
    centers = 700.0 * (jnp.power(10.0, points / 2595.0) - 1.0) / 12000.0 * half_window
    spacing = jnp.maximum(centers[1:] - centers[:-1], 1.0)
    places = jnp.arange(half_window, dtype=jnp.float32)[:, None]
    return jnp.maximum(0.0, 1.0 - jnp.abs(places - centers[None, :mel_count]) / spacing[None, :])

def dft_table(window):
    half_window = window // 2
    sample = jnp.arange(window, dtype=jnp.int32)[:, None]
    freq_index = jnp.arange(half_window, dtype=jnp.int32)[None, :]
    angles = (sample * freq_index % window).astype(jnp.float32) * (2.0 * jnp.pi / window)
    hann_taper = 0.5 - 0.5 * jnp.cos(sample.astype(jnp.float32) * (2.0 * jnp.pi / window))
    return jnp.concatenate([hann_taper * jnp.cos(angles), -hann_taper * jnp.sin(angles)], axis=1)

def framed(signal, window, frame_count):
    hop_size = window // 4
    blocks = signal[..., :(frame_count + 3) * hop_size].reshape(signal.shape[:-1] + (frame_count + 3, hop_size))
    return jnp.concatenate([blocks[..., offset:offset + frame_count, :] for offset in range(4)], axis=-1)

def mel_energy(signal, window, frame_count):
    frames = framed(signal, window, frame_count)
    spectra = product('...nf,fk->...nk', frames, dft_table(window))
    half_window = window // 2
    energy = spectra[..., :half_window] ** 2 + spectra[..., half_window:] ** 2
    return product('...nk,km->...nm', energy, mel_bank(window, MELS))

def spectral_loss(signal, target_mel, window, frame_count):
    level = jnp.sqrt(mel_energy(signal, window, frame_count) + 1.0)
    return jnp.sum((level - jnp.sqrt(target_mel + 1.0)) ** 2)

def upsample(values, kernel, stride):
    lagged = jnp.pad(values[:, :-1], ((0, 0), (1, 0)))
    phases = product('pij,jm->imp', kernel[:stride], values) + product('pij,jm->imp', kernel[stride:], lagged)
    return phases.reshape(phases.shape[0], -1)

def convolve(values, kernel):
    tap_count = kernel.shape[0]
    half_taps = tap_count // 2
    length = values.shape[-1]
    padded = jnp.pad(values, ((0, 0), (half_taps, half_taps)))
    summed = product('oi,il->ol', kernel[0], padded[:, :length])
    for offset in range(1, tap_count):
        summed = summed + product('oi,il->ol', kernel[offset], padded[:, offset:offset + length])
    return summed

def residual_unit(values, inner_kernel, outer_kernel):
    hidden = jax.nn.elu(convolve(jax.nn.elu(values), inner_kernel))
    return values + product('oi,il->ol', outer_kernel, hidden)

def decode(latent_clip, weights):
    up_kernel, inner_kernel, outer_kernel, out_kernel = weights
    values = upsample(jax.nn.elu(latent_clip), up_kernel, 2)
    values = residual_unit(values, inner_kernel, outer_kernel)
    return convolve(jax.nn.elu(values), out_kernel[:, None, :])[0]

def reference(latent, target, up_kernel, inner_kernel, outer_kernel, out_kernel):
    weights = (up_kernel, inner_kernel, outer_kernel, out_kernel)
    time_length = target.shape[1]

    def clip_step(totals, clip_pair):
        latent_clip, target_clip = clip_pair
        waveform, pullback = jax.vjp(decode, latent_clip, weights)
        gradients = [2.0 * (waveform - target_clip)]
        for window in (WIN_COARSE, WIN_FINE):
            hop_size = window // 4
            frame_count = time_length // hop_size
            target_mel = mel_energy(jnp.pad(target_clip, (0, 3 * hop_size)), window, frame_count)

            def scale_loss(signal):
                return spectral_loss(jnp.pad(signal, (0, 3 * hop_size)), target_mel, window, frame_count)
            gradients.append(jax.grad(scale_loss)(waveform))
        balanced = jnp.zeros_like(waveform)
        for weight_value, member in zip(LOSS_WEIGHTS, gradients):
            balanced = balanced + member * (weight_value / jnp.sqrt(jnp.mean(member * member) + 1e-06))
        grad_latent, grad_weights = pullback(balanced)
        return (jax.tree.map(jnp.add, totals, grad_weights), grad_latent)
    totals, latent_grad = lax.scan(clip_step, jax.tree.map(jnp.zeros_like, weights), (latent, target))
    squares = sum((jnp.sum(member * member) for member in totals))
    factor = jnp.minimum(1.0, 1.0 / jnp.sqrt(squares / PARAMS + 1e-06))
    return (latent_grad, totals[0] * factor, totals[1] * factor, totals[2] * factor, totals[3] * factor)
```

```python
import jax
import jax.numpy as jnp
import numpy as np
from jax import lax
from jax.experimental import pallas as pl
from jax.experimental.pallas import tpu as pltpu
from jax.sharding import PartitionSpec as P

MELS = 64
WIN_COARSE = 1024
WIN_FINE = 256
LOSS_WEIGHTS = (0.25, 0.5, 0.5)
LANES = 128
BLOCK = 2 * LANES
STREAMS = 3
F32 = jnp.float32
BF16 = jnp.bfloat16
VMEM = pltpu.MemorySpace.VMEM


def hi_lo(table):
    high = table.astype(np.float32).astype(BF16)
    low = (table - high.astype(np.float64)).astype(np.float32).astype(BF16)
    return high, low


def mel_table(window):
    half = window // 2
    top = 2595.0 * np.log10(1.0 + 12000.0 / 700.0)
    points = (np.arange(MELS + 1) + 1.0) / (MELS + 2.0) * top
    centers = 700.0 * (10.0 ** (points / 2595.0) - 1.0) / 12000.0 * half
    spacing = np.maximum(centers[1:] - centers[:-1], 1.0)
    places = np.arange(half)[:, None]
    return np.maximum(0.0, 1.0 - np.abs(places - centers[None, :MELS]) / spacing[None, :])


def tables():
    order = np.concatenate([np.arange(0, BLOCK, 2), np.arange(1, BLOCK, 2)])
    p = np.arange(LANES)
    cos, sin = [], []
    for rho in range(4):
        angle = 2.0 * np.pi / WIN_COARSE * ((order[:, None] * (4 * p + rho)[None, :]) % WIN_COARSE)
        cos.append(np.cos(angle))
        sin.append(np.sin(angle))
    even = np.concatenate(
        [np.concatenate([cos[0], -sin[0]], 1), np.concatenate([cos[2], -sin[2]], 1)], 0
    )
    odd = np.concatenate(
        [
            np.concatenate([cos[1], -sin[1], cos[3], -sin[3]], 1),
            np.concatenate([-sin[1], -cos[1], sin[3], cos[3]], 1),
        ],
        0,
    )
    angle = 2.0 * np.pi / WIN_FINE * ((order[:, None] * p[None, :]) % WIN_FINE)
    taper = 0.5 - 0.5 * np.cos(2.0 * np.pi / WIN_FINE * order)[:, None]
    fine = np.concatenate([taper * np.cos(angle), -taper * np.sin(angle)], 1)
    coarse_mel = mel_table(WIN_COARSE)
    coarse_mel = np.concatenate([coarse_mel[rho::4] for rho in (0, 2, 1, 3)], 0)
    fine_mel = mel_table(WIN_FINE)
    hann = 0.5 - 0.5 * np.cos(2.0 * np.pi / WIN_COARSE * np.arange(WIN_COARSE))
    hann = hann.reshape(4, BLOCK)[:, order].astype(np.float32)
    hann = np.concatenate([hann, np.zeros_like(hann)], 0)
    deal = np.zeros((BLOCK, BLOCK), np.float32)
    deal[order, np.arange(BLOCK)] = 1.0
    out = [hann, deal.astype(BF16)]
    for table in (even, odd, fine, coarse_mel, fine_mel):
        out += list(hi_lo(table))
    return out


def split(x):
    high = x.astype(BF16)
    return high, (x - high.astype(F32)).astype(BF16)


def stacked(x):
    high = x.astype(BF16).astype(F32)
    return jnp.concatenate([high, x - high], axis=0).astype(BF16)


def dot(left, right, transposed=False):
    dims = (((1,), (1 if transposed else 0,)), ((), ()))
    return lax.dot_general(left, right, dims, preferred_element_type=F32)


def dot3(left, right_high, right_low, transposed=False):
    rows = left.shape[0]
    both = stacked(left)
    first = dot(both, right_high, transposed)
    second = dot(left.astype(BF16), right_low, transposed)
    return first[:rows] + first[rows:] + second


def dot3x(left, right, transposed=False):
    return dot3(left, *split(right), transposed)


def elu_pair(x):
    slope = jnp.exp(jnp.minimum(x, 0.0))
    return jnp.where(x > 0, x, slope - 1.0), slope


def moved(x, by):
    return pltpu.roll(x, by % x.shape[1], 1)


def main_kernel(sizes, *refs):
    (own_ref, first_ref, second_ref, up_ref, inner_ref, outer_ref, out_ref) = refs[:7]
    (hann_ref, deal_ref, even_h, even_l, odd_h, odd_l, fine_h, fine_l) = refs[7:15]
    (cmel_h, cmel_l, fmel_h, fmel_l) = refs[15:19]
    payload_ref, grads_ref = refs[19:21]
    (lat, act, slope_a, a_h, a_l, slope_u, e_h, e_l, slope_c, h_h, h_l, slope_m, g_h, g_l) = refs[21:35]
    (square, wup, kfwd, wblock, shifted, wave_b, targ_b, lanes_b) = refs[35:43]
    channels, half, hidden, frames = sizes
    wide = 3 * frames
    own_blocks = frames // LANES
    index = lax.axis_index("tm")
    count = lax.axis_size("tm")
    odd_place = lax.rem(index, 2) == 1

    first, second = first_ref[...], second_ref[...]
    left_buf = jnp.where(odd_place, first, second)
    right_buf = jnp.where(odd_place, second, first)
    lat[:, 0:frames] = left_buf[:channels]
    lat[:, frames : 2 * frames] = own_ref[0:channels, :]
    lat[:, 2 * frames :] = right_buf[:channels]
    per_row = frames // BLOCK
    for side, rows in enumerate((left_buf, own_ref[...], right_buf)):
        for row in range(2):
            for piece in range(per_row):
                targ_b[pl.ds(side * own_blocks + row * per_row + piece, 1), :] = rows[
                    channels + row : channels + row + 1, piece * BLOCK : (piece + 1) * BLOCK
                ]

    place = lax.broadcasted_iota(jnp.int32, (1, wide), 1) + (index - 1) * frames
    mask = ((place >= 0) & (place < count * frames)).astype(F32)

    for r in range(2):
        wup[r * half : (r + 1) * half, 0:channels] = up_ref[r]
        wup[r * half : (r + 1) * half, channels : 2 * channels] = up_ref[r + 2]
    kfwd[...] = jnp.zeros_like(kfwd)
    square[...] = jnp.zeros_like(square)
    for j in range(3):
        kfwd[0:hidden, j * half : (j + 1) * half] = inner_ref[j]
        kfwd[hidden : 2 * hidden, (j + 1) * half : (j + 2) * half] = inner_ref[j]
        square[(2 - j) * hidden : (3 - j) * hidden, 0:half] = inner_ref[j]
        square[(3 - j) * hidden : (4 - j) * hidden, half : 2 * half] = inner_ref[j]
    back_inner = jnp.transpose(square[...])[0 : 2 * half, 0 : 4 * hidden]
    square[...] = jnp.zeros_like(square)
    square[0:half, 0:hidden] = outer_ref[...]
    square[half : 2 * half, hidden : 2 * hidden] = outer_ref[...]
    outer_fwd = square[0 : 2 * half, 0 : 2 * hidden]
    outer_back = jnp.transpose(square[...])[0 : 2 * hidden, 0 : 2 * half]
    square[...] = jnp.zeros_like(square)
    square[1:8, 0:half] = out_ref[...]
    square[0:7, half : 2 * half] = out_ref[...]
    out_fwd = square[0:8, 0 : 2 * half]
    out_back = jnp.transpose(square[...])[0 : 2 * half, 0:8]
    square[...] = jnp.zeros_like(square)
    for r in range(4):
        square[r * half : (r + 1) * half, 0:channels] = up_ref[r]
    up_back = jnp.transpose(square[...])[0:channels, :]

    activated, slope = elu_pair(lat[...])
    slope_a[...] = slope
    high, low = split(activated)
    a_h[0:channels], a_l[0:channels] = high, low
    high, low = split(moved(activated, 1))
    a_h[channels:], a_l[channels:] = high, low
    upper = dot3(wup[...], a_h[...], a_l[...]) * mask
    rect, slope = elu_pair(upper)
    act[...] = upper
    slope_u[...] = slope
    before, after = moved(rect[half:], 1), moved(rect[:half], -1)
    for at, piece in enumerate((before, rect, after)):
        rows = piece.shape[0]
        start = (0, half, 3 * half)[at]
        high, low = split(piece)
        e_h[start : start + rows], e_l[start : start + rows] = high, low
    inner_out = dot3(kfwd[...], e_h[...], e_l[...])
    hid, slope = elu_pair(inner_out)
    slope_c[...] = slope
    high, low = split(hid)
    h_h[...], h_l[...] = high, low
    mixed = (act[...] + dot3(outer_fwd, h_h[...], h_l[...])) * mask
    rect, slope = elu_pair(mixed)
    slope_m[...] = slope
    high, low = split(rect)
    g_h[...], g_l[...] = high, low
    taps = dot3(out_fwd, g_h[...], g_l[...])
    plus1, plus2, minus1, minus2 = (moved(taps, by) for by in (1, 2, -1, -2))
    wave = [
        (plus2[0:1] + plus1[2:3] + taps[4:5] + minus1[6:7]) * mask,
        (plus1[1:2] + taps[3:4] + minus1[5:6] + minus2[7:8]) * mask,
    ]

    for b in range(3 * own_blocks):
        for r in range(2):
            wave_b[b : b + 1, r * LANES : (r + 1) * LANES] = wave[r][:, b * LANES : (b + 1) * LANES]
    whole = targ_b[...]
    high = whole.astype(BF16)
    rest = whole - high.astype(F32)
    middle = rest.astype(BF16)
    last = (rest - middle.astype(F32)).astype(BF16)
    deal = deal_ref[...]
    targ_b[...] = dot(high, deal) + dot(middle, deal) + dot(last, deal)

    row_count = own_blocks + 4
    start = own_blocks - 3
    parts = []
    for j in range(4):
        rows = jnp.concatenate(
            [wave_b[pl.ds(start + j, row_count), :], targ_b[pl.ds(start + j, row_count), :]], 0
        )
        parts.append(rows * hann_ref[j : j + 1, :])
    even_sum, odd_sum = parts[0] + parts[2], parts[1] + parts[3]
    turned = jnp.concatenate([parts[0] - parts[2], parts[1] - parts[3]], axis=1)
    spec0 = dot3(even_sum + odd_sum, even_h[0:BLOCK], even_l[0:BLOCK])
    spec2 = dot3(even_sum - odd_sum, even_h[BLOCK:], even_l[BLOCK:])
    spec1 = dot3(turned, odd_h[...], odd_l[...])
    real = jnp.concatenate(
        [spec0[:, :LANES], spec2[:, :LANES], spec1[:, :LANES], spec1[:, BLOCK : BLOCK + LANES]], 1
    )
    imag = jnp.concatenate(
        [spec0[:, LANES:], spec2[:, LANES:], spec1[:, LANES:BLOCK], spec1[:, BLOCK + LANES :]], 1
    )
    mel = dot3(real * real + imag * imag, cmel_h[...], cmel_l[...])
    level = jnp.sqrt(mel + 1.0)
    level_wave = level[:row_count]
    frame = lax.broadcasted_iota(jnp.int32, (row_count, MELS), 0) + index * own_blocks - 3
    slope = jnp.where(frame >= 0, (level_wave - level[row_count:]) / level_wave, 0.0)
    push = 2.0 * dot3(slope, cmel_h[...], cmel_l[...], True)
    real, imag = real[:row_count] * push, imag[:row_count] * push
    back0 = dot3(
        jnp.concatenate([real[:, :LANES], imag[:, :LANES]], 1), even_h[0:BLOCK], even_l[0:BLOCK], True
    )
    back2 = dot3(
        jnp.concatenate([real[:, LANES:BLOCK], imag[:, LANES:BLOCK]], 1),
        even_h[BLOCK:],
        even_l[BLOCK:],
        True,
    )
    back1 = dot3(
        jnp.concatenate(
            [
                real[:, BLOCK : BLOCK + LANES],
                imag[:, BLOCK : BLOCK + LANES],
                real[:, BLOCK + LANES :],
                imag[:, BLOCK + LANES :],
            ],
            1,
        ),
        odd_h[...],
        odd_l[...],
        True,
    )
    plus, minus = back0 + back2, back0 - back2
    backs = [
        plus + back1[:, :BLOCK],
        minus + back1[:, BLOCK:],
        plus - back1[:, :BLOCK],
        minus - back1[:, BLOCK:],
    ]
    coarse = jnp.zeros((own_blocks, BLOCK), F32)
    for j in range(4):
        coarse = coarse + (backs[j] * hann_ref[j : j + 1, :])[3 - j : 3 - j + own_blocks]

    hop = LANES // 4
    lane = lax.broadcasted_iota(jnp.int32, (1, LANES), 1)
    start = own_blocks - 1
    for which, source in enumerate((wave_b, targ_b)):
        for s in range(4):
            base = (which * 4 + s) * row_count
            for r in range(2):
                here = source[pl.ds(start, row_count), r * LANES : (r + 1) * LANES]
                if s:
                    there = source[pl.ds(start + 1, row_count), r * LANES : (r + 1) * LANES]
                    here = jnp.where(
                        lane < LANES - s * hop,
                        pltpu.roll(here, LANES - s * hop, 1),
                        pltpu.roll(there, LANES - s * hop, 1),
                    )
                shifted[base : base + row_count, r * LANES : (r + 1) * LANES] = here
    spec = dot3(shifted[...], fine_h[...], fine_l[...])
    real, imag = spec[:, :LANES], spec[:, LANES:]
    mel = dot3(real * real + imag * imag, fmel_h[...], fmel_l[...])
    level = jnp.sqrt(mel + 1.0)
    fine_rows = 4 * row_count
    level_wave = level[:fine_rows]
    row = lax.broadcasted_iota(jnp.int32, (fine_rows, MELS), 0)
    frame = (lax.rem(row, row_count) - 1 + index * own_blocks) * 4 + row // row_count
    slope = jnp.where(frame >= 0, (level_wave - level[fine_rows:]) / level_wave, 0.0)
    push = 2.0 * dot3(slope, fmel_h[...], fmel_l[...], True)
    back = dot3(
        jnp.concatenate([real[:fine_rows] * push, imag[:fine_rows] * push], 1),
        fine_h[...],
        fine_l[...],
        True,
    )
    fine = []
    for r in range(2):
        total = jnp.zeros((own_blocks, LANES), F32)
        for s in range(4):
            piece = back[s * row_count : (s + 1) * row_count, r * LANES : (r + 1) * LANES]
            if s:
                piece = pltpu.roll(piece, s * hop, 1)
                total = total + jnp.where(
                    lane >= s * hop, piece[1 : 1 + own_blocks], piece[0:own_blocks]
                )
            else:
                total = total + piece[1 : 1 + own_blocks]
        fine.append(total)
    fine = jnp.concatenate(fine, axis=1)

    own_rows = pl.ds(own_blocks, own_blocks)
    timed = 2.0 * (wave_b[own_rows, :] - targ_b[own_rows, :])

    window = frames + 2 * LANES
    at = slice(frames - LANES, 2 * frames + LANES)
    mask = mask[:, at]
    totals = []
    edges = []
    for i, stream in enumerate((timed, coarse, fine)):
        totals.append(jnp.sum(stream * stream))
        lanes_b[i] = jnp.zeros((8, window), F32)
        for b in range(own_blocks):
            for r in range(2):
                lanes_b[i, r : r + 1, (b + 1) * LANES : (b + 2) * LANES] = stream[
                    b : b + 1, r * LANES : (r + 1) * LANES
                ]
        evens, odds = lanes_b[i, 0:1, :], lanes_b[i, 1:2, :]
        for k in range(8):
            source = odds if k % 2 else evens
            lanes_b[i, k : k + 1, :] = moved(source, -((4 - k) // 2))
        view = lanes_b[i]
        grad_mixed = dot3x(out_back, view) * slope_m[:, at] * mask
        mixed_h, mixed_l = split(grad_mixed)
        grad_inner = dot3(outer_back, mixed_h, mixed_l) * slope_c[:, at]
        spread = jnp.concatenate(
            [moved(grad_inner[hidden:], 1), grad_inner, moved(grad_inner[:hidden], -1)], 0
        )
        grad_upper = (grad_mixed + dot3x(back_inner, spread) * slope_u[:, at]) * mask
        both = jnp.concatenate([grad_upper, moved(grad_upper, -1)], 0)
        grads = dot3x(up_back, both) * slope_a[:, at] * mask
        grads_ref[i * channels : (i + 1) * channels, :] = grads[:, LANES : LANES + frames]
        before = jnp.transpose(grads[:, 0:LANES])[LANES - 8 :]
        after = jnp.transpose(grads[:, LANES + frames :])[:8]
        edges.append(jnp.concatenate([before, after], axis=1))
        payload_ref[i * 2 * half : (i + 1) * 2 * half, :] = dot3(
            grad_upper, a_h[:, at], a_l[:, at], True
        )
        kern = dot3(grad_inner, e_h[:, at], e_l[:, at], True)
        base = STREAMS * 2 * half + i * hidden
        payload_ref[base : base + hidden, 0 : 3 * half] = (
            kern[:hidden, : 3 * half] + kern[hidden:, half:]
        )
        mix = dot(h_h[:, at], mixed_h, True) + dot(h_l[:, at], mixed_h, True) + dot(h_h[:, at], mixed_l, True)
        payload_ref[base : base + hidden, 3 * half : 4 * half] = (
            mix[:hidden, :half] + mix[hidden:, half:]
        )
        taps = dot3(view, g_h[:, at], g_l[:, at], True)
        wblock[0:7, i * half : (i + 1) * half] = taps[1:8, :half] + taps[0:7, half:]
    base = STREAMS * (2 * half + hidden)
    lane = lax.broadcasted_iota(jnp.int32, (1, half), 1)
    sums = jnp.where(lane == 0, totals[0], jnp.where(lane == 1, totals[1], totals[2]))
    wblock[7:8, :] = jnp.zeros((1, 4 * half), F32)
    wblock[0:7, STREAMS * half :] = jnp.zeros((7, half), F32)
    wblock[7:8, STREAMS * half :] = sums
    payload_ref[base : base + 8, :] = wblock[...]
    payload_ref[base + 8 :, :] = jnp.concatenate(edges, axis=0)


def combine_kernel(sizes, mine_ref, theirs_ref, weights_ref, aux_ref):
    half, hidden, samples = sizes
    rows = STREAMS * (2 * half + hidden)
    total = mine_ref[0 : rows + 8, :] + theirs_ref[0 : rows + 8, :]
    line = total[rows + 7 : rows + 8, :]
    lane = lax.broadcasted_iota(jnp.int32, line.shape, 1) - STREAMS * half
    wanted = jnp.where(lane == 0, LOSS_WEIGHTS[0], jnp.where(lane == 1, LOSS_WEIGHTS[1], LOSS_WEIGHTS[2]))
    line = wanted / jnp.sqrt(line / samples + 1e-06)
    scale = [
        jnp.sum(jnp.where(lane == i, line, 0.0), axis=1, keepdims=True) for i in range(STREAMS)
    ]
    up = sum(total[i * 2 * half : (i + 1) * 2 * half] * scale[i] for i in range(STREAMS))
    base = STREAMS * 2 * half
    inner = sum(total[base + i * hidden : base + (i + 1) * hidden] * scale[i] for i in range(STREAMS))
    last = total[rows : rows + 8]
    out = sum(
        (pltpu.roll(last, (4 - i) * half % (4 * half), 1) if i else last) * scale[i]
        for i in range(STREAMS)
    )
    place = lax.broadcasted_iota(jnp.int32, out.shape, 0)
    lane = lax.broadcasted_iota(jnp.int32, out.shape, 1)
    weights_ref[0 : 2 * half, :] = up
    weights_ref[2 * half : 2 * half + hidden, :] = inner
    weights_ref[2 * half + hidden :, :] = jnp.where((place < 7) & (lane < half), out, 0.0)
    index = lax.axis_index("tm")
    step = lax.axis_size("tm") // 2
    low = lax.rem(index, step)
    edge_lane = lax.broadcasted_iota(jnp.int32, (1, LANES), 1)
    swap = ((low == 0) & (edge_lane >= LANES // 2)) | ((low == step - 1) & (edge_lane < LANES // 2))
    edges = jnp.where(swap, theirs_ref[rows + 8 :, :], mine_ref[rows + 8 :, :])
    aux_ref[0:8, :] = sum(edges[8 * i : 8 * i + 8] * scale[i] for i in range(STREAMS))
    for i in range(STREAMS):
        aux_ref[8 + i : 9 + i, :] = jnp.broadcast_to(scale[i], (1, LANES))


def latent_kernel(channels, grads_ref, aux_ref, square, grad_ref):
    frames = grads_ref.shape[1]
    total = sum(
        grads_ref[i * channels : (i + 1) * channels, :] * aux_ref[8 + i : 9 + i, 0:1]
        for i in range(STREAMS)
    )
    grad_ref[0] = total
    square[...] = jnp.zeros_like(square)
    square[0:8, 0:channels] = aux_ref[0:8, channels:]
    square[LANES - 8 :, channels:] = aux_ref[0:8, 0:channels]
    turned = jnp.transpose(square[...])
    grad_ref[0, :, 0:LANES] = grad_ref[0, :, 0:LANES] + turned[0:channels]
    grad_ref[0, :, frames - LANES :] = grad_ref[0, :, frames - LANES :] + turned[channels:]


def final_kernel(sizes, mine_ref, theirs_ref, up_ref, inner_ref, outer_ref, out_ref, square):
    channels, half, hidden, params = sizes
    total = mine_ref[...] + theirs_ref[...]
    squares = jnp.sum(total * total)
    factor = jnp.minimum(1.0, 1.0 / jnp.sqrt(jnp.full((1, 1), squares / params + 1e-06, F32)))
    total = total * factor
    for r in range(2):
        up_ref[r] = total[r * half : (r + 1) * half, 0:channels]
        up_ref[r + 2] = total[r * half : (r + 1) * half, channels:]
    inner = total[2 * half : 2 * half + hidden]
    for j in range(3):
        inner_ref[j] = inner[:, j * half : (j + 1) * half]
    square[...] = jnp.zeros_like(square)
    square[0:hidden, :] = inner
    outer_ref[...] = jnp.transpose(square[...])[3 * half :, 0:hidden]
    out_ref[...] = total[2 * half + hidden : 2 * half + hidden + 7, 0:half]


def in_vmem(count):
    return [pl.BlockSpec(memory_space=VMEM)] * count


def local(latent, target, up_kernel, inner_kernel, outer_kernel, out_kernel):
    assert latent.shape[0] == 1
    channels, frames = latent.shape[1:]
    half, hidden = outer_kernel.shape
    wide = 3 * frames
    window = frames + 2 * LANES
    blocks = frames // LANES
    count = lax.axis_size("tm")
    samples = target.shape[1] * count
    params = sum(x.size for x in (up_kernel, inner_kernel, outer_kernel, out_kernel))

    own = jnp.concatenate([latent[0], target.reshape(2, frames)], axis=0)
    pairs = [(i, i ^ 1) for i in range(count) if i ^ 1 < count]
    first = lax.ppermute(own, "tm", pairs)
    pairs = [(i, i + 1 if i % 2 else i - 1) for i in range(count)]
    second = lax.ppermute(own, "tm", [(a, b) for a, b in pairs if 0 <= b < count])

    constants = tables()
    rows = STREAMS * (2 * half + hidden)
    scratch = [
        pltpu.VMEM((channels, wide), F32),
        pltpu.VMEM((2 * half, wide), F32),
        pltpu.VMEM((channels, wide), F32),
        pltpu.VMEM((2 * channels, wide), BF16),
        pltpu.VMEM((2 * channels, wide), BF16),
        pltpu.VMEM((2 * half, wide), F32),
        pltpu.VMEM((4 * half, wide), BF16),
        pltpu.VMEM((4 * half, wide), BF16),
        pltpu.VMEM((2 * hidden, wide), F32),
        pltpu.VMEM((2 * hidden, wide), BF16),
        pltpu.VMEM((2 * hidden, wide), BF16),
        pltpu.VMEM((2 * half, wide), F32),
        pltpu.VMEM((2 * half, wide), BF16),
        pltpu.VMEM((2 * half, wide), BF16),
        pltpu.VMEM((LANES, LANES), F32),
        pltpu.VMEM((2 * half, 2 * channels), F32),
        pltpu.VMEM((2 * hidden, 4 * half), F32),
        pltpu.VMEM((8, 4 * half), F32),
        pltpu.VMEM((8 * (blocks + 4), BLOCK), F32),
        pltpu.VMEM((3 * blocks, BLOCK), F32),
        pltpu.VMEM((3 * blocks, BLOCK), F32),
        pltpu.VMEM((STREAMS, 8, window), F32),
    ]
    sizes = (channels, half, hidden, frames)
    payload, grads = pl.pallas_call(
        lambda *refs: main_kernel(sizes, *refs),
        out_shape=(
            jax.ShapeDtypeStruct((rows + 8 + 8 * STREAMS, LANES), F32),
            jax.ShapeDtypeStruct((STREAMS * channels, frames), F32),
        ),
        in_specs=in_vmem(7 + len(constants)),
        out_specs=tuple(in_vmem(2)),
        scratch_shapes=scratch,
        name="decode_and_losses",
    )(own, first, second, up_kernel, inner_kernel, outer_kernel, out_kernel, *constants)

    index = lax.axis_index("tm")
    line = lax.broadcasted_iota(jnp.int32, payload.shape, 0)
    lane = lax.broadcasted_iota(jnp.int32, payload.shape, 1)
    step = 1
    while True:
        theirs = lax.ppermute(payload, "tm", [(i, i ^ step) for i in range(count)])
        if 2 * step == count:
            break
        low = index % step
        swap = ((low == 0) & (lane >= LANES // 2)) | ((low == step - 1) & (lane < LANES // 2))
        payload = jnp.where(
            line < rows + 8, payload + theirs, jnp.where(swap, theirs, payload)
        )
        step *= 2

    weights, aux = pl.pallas_call(
        lambda *refs: combine_kernel((half, hidden, samples), *refs),
        out_shape=(
            jax.ShapeDtypeStruct((2 * half + hidden + 8, LANES), F32),
            jax.ShapeDtypeStruct((16, LANES), F32),
        ),
        in_specs=in_vmem(2),
        out_specs=tuple(in_vmem(2)),
        name="combine",
    )(payload, theirs)
    latent_grad = pl.pallas_call(
        lambda grads_ref, aux_ref, out, square: latent_kernel(channels, grads_ref, aux_ref, square, out),
        out_shape=jax.ShapeDtypeStruct(latent.shape, F32),
        in_specs=in_vmem(2),
        out_specs=in_vmem(1)[0],
        scratch_shapes=[pltpu.VMEM((LANES, LANES), F32)],
        name="latent",
    )(grads, aux)

    count = lax.axis_size("dp")
    step = 1
    while True:
        theirs = lax.ppermute(weights, "dp", [(i, i ^ step) for i in range(count)])
        if 2 * step == count:
            break
        weights = weights + theirs
        step *= 2
    updates = pl.pallas_call(
        lambda *refs: final_kernel((channels, half, hidden, params), *refs),
        out_shape=tuple(
            jax.ShapeDtypeStruct(x.shape, F32)
            for x in (up_kernel, inner_kernel, outer_kernel, out_kernel)
        ),
        in_specs=in_vmem(2),
        out_specs=tuple(in_vmem(4)),
        scratch_shapes=[pltpu.VMEM((LANES, LANES), F32)],
        name="final",
    )(weights, theirs)
    return (latent_grad, *updates)


def solution(mesh):
    for axis in ("dp", "tm"):
        size = mesh.shape[axis]
        assert size > 1 and size & (size - 1) == 0
    placed = (P("dp", None, "tm"), P("dp", "tm"), P(), P(), P(), P())
    return jax.shard_map(
        local,
        mesh=mesh,
        in_specs=placed,
        out_specs=(P("dp", None, "tm"), P(), P(), P(), P()),
        check_vma=False,
    )
```

```python
import jax
import jax.numpy as jnp
import numpy as np
from jax import lax
from jax.experimental import pallas as pl
from jax.experimental.pallas import tpu as pltpu
from jax.sharding import PartitionSpec as P

MELS = 64
WIN_COARSE = 1024
WIN_FINE = 256
LOSS_WEIGHTS = (0.25, 0.5, 0.5)
LANES = 128
BLOCK = 2 * LANES
STREAMS = 3
F32 = jnp.float32
BF16 = jnp.bfloat16
VMEM = pltpu.MemorySpace.VMEM


def hi_lo(table):
    high = table.astype(np.float32).astype(BF16)
    low = (table - high.astype(np.float64)).astype(np.float32).astype(BF16)
    return high, low


def mel_table(window):
    half = window // 2
    top = 2595.0 * np.log10(1.0 + 12000.0 / 700.0)
    points = (np.arange(MELS + 1) + 1.0) / (MELS + 2.0) * top
    centers = 700.0 * (10.0 ** (points / 2595.0) - 1.0) / 12000.0 * half
    spacing = np.maximum(centers[1:] - centers[:-1], 1.0)
    places = np.arange(half)[:, None]
    return np.maximum(0.0, 1.0 - np.abs(places - centers[None, :MELS]) / spacing[None, :])


def tables():
    order = np.concatenate([np.arange(0, BLOCK, 2), np.arange(1, BLOCK, 2)])
    p = np.arange(LANES)
    cos, sin = [], []
    for rho in range(4):
        angle = 2.0 * np.pi / WIN_COARSE * ((order[:, None] * (4 * p + rho)[None, :]) % WIN_COARSE)
        cos.append(np.cos(angle))
        sin.append(np.sin(angle))
    even = np.concatenate(
        [np.concatenate([cos[0], -sin[0]], 1), np.concatenate([cos[2], -sin[2]], 1)], 0
    )
    odd = np.concatenate(
        [
            np.concatenate([cos[1], -sin[1], cos[3], -sin[3]], 1),
            np.concatenate([-sin[1], -cos[1], sin[3], cos[3]], 1),
        ],
        0,
    )
    angle = 2.0 * np.pi / WIN_FINE * ((order[:, None] * p[None, :]) % WIN_FINE)
    taper = 0.5 - 0.5 * np.cos(2.0 * np.pi / WIN_FINE * order)[:, None]
    fine = np.concatenate([taper * np.cos(angle), -taper * np.sin(angle)], 1)
    coarse_mel = mel_table(WIN_COARSE)
    coarse_mel = np.concatenate([coarse_mel[rho::4] for rho in (0, 2, 1, 3)], 0)
    fine_mel = mel_table(WIN_FINE)
    hann = 0.5 - 0.5 * np.cos(2.0 * np.pi / WIN_COARSE * np.arange(WIN_COARSE))
    hann = hann.reshape(4, BLOCK)[:, order].astype(np.float32)
    hann = np.concatenate([hann, np.zeros_like(hann)], 0)
    deal = np.zeros((BLOCK, BLOCK), np.float32)
    deal[order, np.arange(BLOCK)] = 1.0
    even, odd, fine = hi_lo(even), hi_lo(odd), hi_lo(fine)
    banks = hi_lo(coarse_mel) + hi_lo(fine_mel)
    return (
        hann,
        np.concatenate([deal.astype(BF16), *even, *fine], 0),
        np.concatenate(odd, 0),
        np.concatenate(banks, 0),
    )


def split(x):
    high = x.astype(BF16)
    return high, (x - high.astype(F32)).astype(BF16)


def stacked(x):
    high = x.astype(BF16).astype(F32)
    return jnp.concatenate([high, x - high], axis=0).astype(BF16)


def dot(left, right, transposed=False):
    dims = (((1,), (1 if transposed else 0,)), ((), ()))
    return lax.dot_general(left, right, dims, preferred_element_type=F32)


def dot3(left, right_high, right_low, transposed=False):
    rows = left.shape[0]
    both = stacked(left)
    first = dot(both, right_high, transposed)
    second = dot(left.astype(BF16), right_low, transposed)
    return first[:rows] + first[rows:] + second


def dot3x(left, right, transposed=False):
    return dot3(left, *split(right), transposed)


def elu_pair(x):
    slope = jnp.exp(jnp.minimum(x, 0.0))
    return jnp.where(x > 0, x, slope - 1.0), slope


def moved(x, by):
    return pltpu.roll(x, by % x.shape[1], 1)


def main_kernel(sizes, *refs):
    (own_ref, first_ref, second_ref, up_ref, inner_ref, outer_ref, out_ref) = refs[:7]
    sources = refs[7:11]
    payload_ref, grads_ref = refs[11:13]
    (lat, act, slope_a, a_h, a_l, slope_u, e_h, e_l, slope_c, h_h, h_l, slope_m, g_h, g_l) = refs[13:27]
    (square, wup, kfwd, wblock, shifted, wave_b, targ_b, lanes_b) = refs[27:35]
    fetched, sems = refs[35:39], refs[39]
    copies = [
        pltpu.make_async_copy(source, space, sems.at[i])
        for i, (source, space) in enumerate(zip(sources, fetched))
    ]
    for copy in copies:
        copy.start()
    hann_ref, square_ref, odd_ref, bank_ref = fetched
    channels, half, hidden, frames = sizes
    wide = 3 * frames
    own_blocks = frames // LANES
    index = lax.axis_index("tm")
    count = lax.axis_size("tm")
    odd_place = lax.rem(index, 2) == 1

    first, second = first_ref[...], second_ref[...]
    left_buf = jnp.where(odd_place, first, second)
    right_buf = jnp.where(odd_place, second, first)
    lat[:, 0:frames] = left_buf[:channels]
    lat[:, frames : 2 * frames] = own_ref[0:channels, :]
    lat[:, 2 * frames :] = right_buf[:channels]
    per_row = frames // BLOCK
    for side, rows in enumerate((left_buf, own_ref[...], right_buf)):
        for row in range(2):
            for piece in range(per_row):
                targ_b[pl.ds(side * own_blocks + row * per_row + piece, 1), :] = rows[
                    channels + row : channels + row + 1, piece * BLOCK : (piece + 1) * BLOCK
                ]

    place = lax.broadcasted_iota(jnp.int32, (1, wide), 1) + (index - 1) * frames
    mask = ((place >= 0) & (place < count * frames)).astype(F32)

    for r in range(2):
        wup[r * half : (r + 1) * half, 0:channels] = up_ref[r]
        wup[r * half : (r + 1) * half, channels : 2 * channels] = up_ref[r + 2]
    kfwd[...] = jnp.zeros_like(kfwd)
    square[...] = jnp.zeros_like(square)
    for j in range(3):
        kfwd[0:hidden, j * half : (j + 1) * half] = inner_ref[j]
        kfwd[hidden : 2 * hidden, (j + 1) * half : (j + 2) * half] = inner_ref[j]
        square[(2 - j) * hidden : (3 - j) * hidden, 0:half] = inner_ref[j]
        square[(3 - j) * hidden : (4 - j) * hidden, half : 2 * half] = inner_ref[j]
    back_inner = jnp.transpose(square[...])[0 : 2 * half, 0 : 4 * hidden]
    square[...] = jnp.zeros_like(square)
    square[0:hidden, 0:half] = outer_ref[...]
    square[hidden : 2 * hidden, half : 2 * half] = outer_ref[...]
    outer_back = square[0 : 2 * hidden, 0 : 2 * half]
    outer_fwd = jnp.transpose(square[...])[0 : 2 * half, 0 : 2 * hidden]
    square[...] = jnp.zeros_like(square)
    square[1:8, 0:half] = out_ref[...]
    square[0:7, half : 2 * half] = out_ref[...]
    out_fwd = square[0:8, 0 : 2 * half]
    out_back = jnp.transpose(square[...])[0 : 2 * half, 0:8]
    square[...] = jnp.zeros_like(square)
    for r in range(4):
        square[r * half : (r + 1) * half, 0:channels] = up_ref[r]
    up_back = jnp.transpose(square[...])[0:channels, :]

    activated, slope = elu_pair(lat[...])
    slope_a[...] = slope
    high, low = split(activated)
    a_h[0:channels], a_l[0:channels] = high, low
    high, low = split(moved(activated, 1))
    a_h[channels:], a_l[channels:] = high, low
    upper = dot3(wup[...], a_h[...], a_l[...]) * mask
    rect, slope = elu_pair(upper)
    act[...] = upper
    slope_u[...] = slope
    before, after = moved(rect[half:], 1), moved(rect[:half], -1)
    for at, piece in enumerate((before, rect, after)):
        rows = piece.shape[0]
        start = (0, half, 3 * half)[at]
        high, low = split(piece)
        e_h[start : start + rows], e_l[start : start + rows] = high, low
    inner_out = dot3(kfwd[...], e_h[...], e_l[...])
    hid, slope = elu_pair(inner_out)
    slope_c[...] = slope
    high, low = split(hid)
    h_h[...], h_l[...] = high, low
    mixed = (act[...] + dot3(outer_fwd, h_h[...], h_l[...])) * mask
    rect, slope = elu_pair(mixed)
    slope_m[...] = slope
    high, low = split(rect)
    g_h[...], g_l[...] = high, low
    taps = dot3(out_fwd, g_h[...], g_l[...])
    plus1, plus2, minus1, minus2 = (moved(taps, by) for by in (1, 2, -1, -2))
    wave = [
        (plus2[0:1] + plus1[2:3] + taps[4:5] + minus1[6:7]) * mask,
        (plus1[1:2] + taps[3:4] + minus1[5:6] + minus2[7:8]) * mask,
    ]

    for b in range(3 * own_blocks):
        for r in range(2):
            wave_b[b : b + 1, r * LANES : (r + 1) * LANES] = wave[r][:, b * LANES : (b + 1) * LANES]
    whole = targ_b[...]
    high = whole.astype(BF16)
    rest = whole - high.astype(F32)
    middle = rest.astype(BF16)
    last = (rest - middle.astype(F32)).astype(BF16)
    for copy in copies:
        copy.wait()
    deal = square_ref[0:BLOCK]
    even_h, even_l, odd_h, odd_l = (
        square_ref.at[pl.ds(BLOCK, 2 * BLOCK)],
        square_ref.at[pl.ds(3 * BLOCK, 2 * BLOCK)],
        odd_ref.at[pl.ds(0, 2 * BLOCK)],
        odd_ref.at[pl.ds(2 * BLOCK, 2 * BLOCK)],
    )
    fine_h, fine_l = square_ref.at[pl.ds(5 * BLOCK, BLOCK)], square_ref.at[pl.ds(6 * BLOCK, BLOCK)]
    cmel_h, cmel_l = bank_ref.at[pl.ds(0, 2 * BLOCK)], bank_ref.at[pl.ds(2 * BLOCK, 2 * BLOCK)]
    fmel_h = bank_ref.at[pl.ds(4 * BLOCK, LANES)]
    fmel_l = bank_ref.at[pl.ds(4 * BLOCK + LANES, LANES)]
    targ_b[...] = dot(high, deal) + dot(middle, deal) + dot(last, deal)

    row_count = own_blocks + 4
    start = own_blocks - 3
    parts = []
    for j in range(4):
        rows = jnp.concatenate(
            [wave_b[pl.ds(start + j, row_count), :], targ_b[pl.ds(start + j, row_count), :]], 0
        )
        parts.append(rows * hann_ref[j : j + 1, :])
    even_sum, odd_sum = parts[0] + parts[2], parts[1] + parts[3]
    turned = jnp.concatenate([parts[0] - parts[2], parts[1] - parts[3]], axis=1)
    spec0 = dot3(even_sum + odd_sum, even_h[0:BLOCK], even_l[0:BLOCK])
    spec2 = dot3(even_sum - odd_sum, even_h[BLOCK:], even_l[BLOCK:])
    spec1 = dot3(turned, odd_h[...], odd_l[...])
    real = jnp.concatenate(
        [spec0[:, :LANES], spec2[:, :LANES], spec1[:, :LANES], spec1[:, BLOCK : BLOCK + LANES]], 1
    )
    imag = jnp.concatenate(
        [spec0[:, LANES:], spec2[:, LANES:], spec1[:, LANES:BLOCK], spec1[:, BLOCK + LANES :]], 1
    )
    mel = dot3(real * real + imag * imag, cmel_h[...], cmel_l[...])
    level = jnp.sqrt(mel + 1.0)
    level_wave = level[:row_count]
    frame = lax.broadcasted_iota(jnp.int32, (row_count, MELS), 0) + index * own_blocks - 3
    slope = jnp.where(frame >= 0, (level_wave - level[row_count:]) / level_wave, 0.0)
    push = 2.0 * dot3(slope, cmel_h[...], cmel_l[...], True)
    real, imag = real[:row_count] * push, imag[:row_count] * push
    back0 = dot3(
        jnp.concatenate([real[:, :LANES], imag[:, :LANES]], 1), even_h[0:BLOCK], even_l[0:BLOCK], True
    )
    back2 = dot3(
        jnp.concatenate([real[:, LANES:BLOCK], imag[:, LANES:BLOCK]], 1),
        even_h[BLOCK:],
        even_l[BLOCK:],
        True,
    )
    back1 = dot3(
        jnp.concatenate(
            [
                real[:, BLOCK : BLOCK + LANES],
                imag[:, BLOCK : BLOCK + LANES],
                real[:, BLOCK + LANES :],
                imag[:, BLOCK + LANES :],
            ],
            1,
        ),
        odd_h[...],
        odd_l[...],
        True,
    )
    plus, minus = back0 + back2, back0 - back2
    backs = [
        plus + back1[:, :BLOCK],
        minus + back1[:, BLOCK:],
        plus - back1[:, :BLOCK],
        minus - back1[:, BLOCK:],
    ]
    coarse = jnp.zeros((own_blocks, BLOCK), F32)
    for j in range(4):
        coarse = coarse + (backs[j] * hann_ref[j : j + 1, :])[3 - j : 3 - j + own_blocks]

    hop = LANES // 4
    lane = lax.broadcasted_iota(jnp.int32, (1, LANES), 1)
    start = own_blocks - 1
    for which, source in enumerate((wave_b, targ_b)):
        for s in range(4):
            base = (which * 4 + s) * row_count
            for r in range(2):
                here = source[pl.ds(start, row_count), r * LANES : (r + 1) * LANES]
                if s:
                    there = source[pl.ds(start + 1, row_count), r * LANES : (r + 1) * LANES]
                    here = jnp.where(
                        lane < LANES - s * hop,
                        pltpu.roll(here, LANES - s * hop, 1),
                        pltpu.roll(there, LANES - s * hop, 1),
                    )
                shifted[base : base + row_count, r * LANES : (r + 1) * LANES] = here
    spec = dot3(shifted[...], fine_h[...], fine_l[...])
    real, imag = spec[:, :LANES], spec[:, LANES:]
    mel = dot3(real * real + imag * imag, fmel_h[...], fmel_l[...])
    level = jnp.sqrt(mel + 1.0)
    fine_rows = 4 * row_count
    level_wave = level[:fine_rows]
    row = lax.broadcasted_iota(jnp.int32, (fine_rows, MELS), 0)
    frame = (lax.rem(row, row_count) - 1 + index * own_blocks) * 4 + row // row_count
    slope = jnp.where(frame >= 0, (level_wave - level[fine_rows:]) / level_wave, 0.0)
    push = 2.0 * dot3(slope, fmel_h[...], fmel_l[...], True)
    back = dot3(
        jnp.concatenate([real[:fine_rows] * push, imag[:fine_rows] * push], 1),
        fine_h[...],
        fine_l[...],
        True,
    )
    fine = []
    for r in range(2):
        total = jnp.zeros((own_blocks, LANES), F32)
        for s in range(4):
            piece = back[s * row_count : (s + 1) * row_count, r * LANES : (r + 1) * LANES]
            if s:
                piece = pltpu.roll(piece, s * hop, 1)
                total = total + jnp.where(
                    lane >= s * hop, piece[1 : 1 + own_blocks], piece[0:own_blocks]
                )
            else:
                total = total + piece[1 : 1 + own_blocks]
        fine.append(total)
    fine = jnp.concatenate(fine, axis=1)

    own_rows = pl.ds(own_blocks, own_blocks)
    timed = 2.0 * (wave_b[own_rows, :] - targ_b[own_rows, :])

    window = frames + 2 * LANES
    at = slice(frames - LANES, 2 * frames + LANES)
    mask = mask[:, at]
    totals = []
    edges = []
    for i, stream in enumerate((timed, coarse, fine)):
        totals.append(jnp.sum(stream * stream))
        lanes_b[i] = jnp.zeros((8, window), F32)
        for b in range(own_blocks):
            for r in range(2):
                lanes_b[i, r : r + 1, (b + 1) * LANES : (b + 2) * LANES] = stream[
                    b : b + 1, r * LANES : (r + 1) * LANES
                ]
        evens, odds = lanes_b[i, 0:1, :], lanes_b[i, 1:2, :]
        for k in range(8):
            source = odds if k % 2 else evens
            lanes_b[i, k : k + 1, :] = moved(source, -((4 - k) // 2))
        view = lanes_b[i]
        grad_mixed = dot3x(out_back, view) * slope_m[:, at] * mask
        mixed_h, mixed_l = split(grad_mixed)
        grad_inner = dot3(outer_back, mixed_h, mixed_l) * slope_c[:, at]
        spread = jnp.concatenate(
            [moved(grad_inner[hidden:], 1), grad_inner, moved(grad_inner[:hidden], -1)], 0
        )
        grad_upper = (grad_mixed + dot3x(back_inner, spread) * slope_u[:, at]) * mask
        both = jnp.concatenate([grad_upper, moved(grad_upper, -1)], 0)
        grads = dot3x(up_back, both) * slope_a[:, at] * mask
        grads_ref[i * channels : (i + 1) * channels, :] = grads[:, LANES : LANES + frames]
        before = jnp.transpose(grads[:, 0:LANES])[LANES - 8 :]
        after = jnp.transpose(grads[:, LANES + frames :])[:8]
        edges.append(jnp.concatenate([before, after], axis=1))
        payload_ref[i * 2 * half : (i + 1) * 2 * half, :] = dot3(
            grad_upper, a_h[:, at], a_l[:, at], True
        )
        kern = dot3(grad_inner, e_h[:, at], e_l[:, at], True)
        base = STREAMS * 2 * half + i * hidden
        payload_ref[base : base + hidden, 0 : 3 * half] = (
            kern[:hidden, : 3 * half] + kern[hidden:, half:]
        )
        mix = dot(h_h[:, at], mixed_h, True) + dot(h_l[:, at], mixed_h, True) + dot(h_h[:, at], mixed_l, True)
        payload_ref[base : base + hidden, 3 * half : 4 * half] = (
            mix[:hidden, :half] + mix[hidden:, half:]
        )
        taps = dot3(view, g_h[:, at], g_l[:, at], True)
        wblock[0:7, i * half : (i + 1) * half] = taps[1:8, :half] + taps[0:7, half:]
    base = STREAMS * (2 * half + hidden)
    lane = lax.broadcasted_iota(jnp.int32, (1, half), 1)
    sums = jnp.where(lane == 0, totals[0], jnp.where(lane == 1, totals[1], totals[2]))
    wblock[7:8, :] = jnp.zeros((1, 4 * half), F32)
    wblock[0:7, STREAMS * half :] = jnp.zeros((7, half), F32)
    wblock[7:8, STREAMS * half :] = sums
    payload_ref[base : base + 8, :] = wblock[...]
    payload_ref[base + 8 :, :] = jnp.concatenate(edges, axis=0)


def combine_kernel(sizes, mine_ref, theirs_ref, weights_ref, aux_ref):
    half, hidden, samples = sizes
    rows = STREAMS * (2 * half + hidden)
    total = mine_ref[0 : rows + 8, :] + theirs_ref[0 : rows + 8, :]
    line = total[rows + 7 : rows + 8, :]
    lane = lax.broadcasted_iota(jnp.int32, line.shape, 1) - STREAMS * half
    wanted = jnp.where(lane == 0, LOSS_WEIGHTS[0], jnp.where(lane == 1, LOSS_WEIGHTS[1], LOSS_WEIGHTS[2]))
    line = wanted / jnp.sqrt(line / samples + 1e-06)
    scale = [
        jnp.sum(jnp.where(lane == i, line, 0.0), axis=1, keepdims=True) for i in range(STREAMS)
    ]
    up = sum(total[i * 2 * half : (i + 1) * 2 * half] * scale[i] for i in range(STREAMS))
    base = STREAMS * 2 * half
    inner = sum(total[base + i * hidden : base + (i + 1) * hidden] * scale[i] for i in range(STREAMS))
    last = total[rows : rows + 8]
    out = sum(
        (pltpu.roll(last, (4 - i) * half % (4 * half), 1) if i else last) * scale[i]
        for i in range(STREAMS)
    )
    place = lax.broadcasted_iota(jnp.int32, out.shape, 0)
    lane = lax.broadcasted_iota(jnp.int32, out.shape, 1)
    weights_ref[0 : 2 * half, :] = up
    weights_ref[2 * half : 2 * half + hidden, :] = inner
    weights_ref[2 * half + hidden :, :] = jnp.where((place < 7) & (lane < half), out, 0.0)
    index = lax.axis_index("tm")
    step = lax.axis_size("tm") // 2
    low = lax.rem(index, step)
    edge_lane = lax.broadcasted_iota(jnp.int32, (1, LANES), 1)
    swap = ((low == 0) & (edge_lane >= LANES // 2)) | ((low == step - 1) & (edge_lane < LANES // 2))
    edges = jnp.where(swap, theirs_ref[rows + 8 :, :], mine_ref[rows + 8 :, :])
    aux_ref[0:8, :] = sum(edges[8 * i : 8 * i + 8] * scale[i] for i in range(STREAMS))
    for i in range(STREAMS):
        aux_ref[8 + i : 9 + i, :] = jnp.broadcast_to(scale[i], (1, LANES))


def latent_kernel(channels, grads_ref, aux_ref, square, grad_ref):
    frames = grads_ref.shape[1]
    total = sum(
        grads_ref[i * channels : (i + 1) * channels, :] * aux_ref[8 + i : 9 + i, 0:1]
        for i in range(STREAMS)
    )
    grad_ref[0] = total
    square[...] = jnp.zeros_like(square)
    square[0:8, 0:channels] = aux_ref[0:8, channels:]
    square[LANES - 8 :, channels:] = aux_ref[0:8, 0:channels]
    turned = jnp.transpose(square[...])
    grad_ref[0, :, 0:LANES] = grad_ref[0, :, 0:LANES] + turned[0:channels]
    grad_ref[0, :, frames - LANES :] = grad_ref[0, :, frames - LANES :] + turned[channels:]


def final_kernel(sizes, mine_ref, theirs_ref, up_ref, inner_ref, outer_ref, out_ref):
    channels, half, hidden, params = sizes
    total = mine_ref[...] + theirs_ref[...]
    squares = jnp.sum(total * total)
    factor = jnp.minimum(1.0, 1.0 / jnp.sqrt(jnp.full((1, 1), squares / params + 1e-06, F32)))
    total = total * factor
    for r in range(2):
        up_ref[r] = total[r * half : (r + 1) * half, 0:channels]
        up_ref[r + 2] = total[r * half : (r + 1) * half, channels:]
    inner = total[2 * half : 2 * half + hidden]
    for j in range(3):
        inner_ref[j] = inner[:, j * half : (j + 1) * half]
    outer_ref[...] = inner[:, 3 * half :]
    out_ref[...] = total[2 * half + hidden : 2 * half + hidden + 7, 0:half]


def pack_kernel(latent_ref, target_ref, own_ref, sems):
    channels, frames = latent_ref.shape[1:]
    copies = [pltpu.make_async_copy(latent_ref.at[0], own_ref.at[pl.ds(0, channels)], sems.at[0])]
    for row in range(2):
        copies.append(
            pltpu.make_async_copy(
                target_ref.at[:, pl.ds(row * frames, frames)],
                own_ref.at[pl.ds(channels + row, 1)],
                sems.at[1 + row],
            )
        )
    for copy in copies:
        copy.start()
    for copy in copies:
        copy.wait()


def run(kernel, out_shape, operands, scratch, name, mebibytes, left=0):
    spec = pl.BlockSpec(memory_space=VMEM)
    kept = len(operands) - left
    hbm = [pltpu.with_memory_space_constraint(x, pltpu.MemorySpace.HBM) for x in operands[kept:]]
    operands = [*operands[:kept], *hbm]
    stay = pl.BlockSpec(memory_space=pltpu.MemorySpace.HBM)
    return pl.pallas_call(
        kernel,
        out_shape=tuple(jax.ShapeDtypeStruct(shape, F32) for shape in out_shape),
        in_specs=[spec] * (len(operands) - left) + [stay] * left,
        out_specs=tuple([spec] * len(out_shape)),
        scratch_shapes=scratch,
        compiler_params=pltpu.CompilerParams(vmem_limit_bytes=mebibytes << 20),
        name=name,
    )(*operands)


def local(latent, target, up_kernel, inner_kernel, outer_kernel, out_kernel):
    assert latent.shape[0] == 1
    channels, frames = latent.shape[1:]
    half, hidden = outer_kernel.shape
    wide = 3 * frames
    window = frames + 2 * LANES
    blocks = frames // LANES
    count = lax.axis_size("tm")
    samples = target.shape[1] * count
    params = sum(x.size for x in (up_kernel, inner_kernel, outer_kernel, out_kernel))

    (own,) = run(pack_kernel, [(channels + 8, frames)], [latent, target], [pltpu.SemaphoreType.DMA((3,))], "pack", 2, 2)
    pairs = [(i, i ^ 1) for i in range(count) if i ^ 1 < count]
    first = lax.ppermute(own, "tm", pairs)
    pairs = [(i, i + 1 if i % 2 else i - 1) for i in range(count)]
    second = lax.ppermute(own, "tm", [(a, b) for a, b in pairs if 0 <= b < count])

    constants = tables()
    rows = STREAMS * (2 * half + hidden)
    scratch = [
        pltpu.VMEM((channels, wide), F32),
        pltpu.VMEM((2 * half, wide), F32),
        pltpu.VMEM((channels, wide), F32),
        pltpu.VMEM((2 * channels, wide), BF16),
        pltpu.VMEM((2 * channels, wide), BF16),
        pltpu.VMEM((2 * half, wide), F32),
        pltpu.VMEM((4 * half, wide), BF16),
        pltpu.VMEM((4 * half, wide), BF16),
        pltpu.VMEM((2 * hidden, wide), F32),
        pltpu.VMEM((2 * hidden, wide), BF16),
        pltpu.VMEM((2 * hidden, wide), BF16),
        pltpu.VMEM((2 * half, wide), F32),
        pltpu.VMEM((2 * half, wide), BF16),
        pltpu.VMEM((2 * half, wide), BF16),
        pltpu.VMEM((LANES, LANES), F32),
        pltpu.VMEM((2 * half, 2 * channels), F32),
        pltpu.VMEM((2 * hidden, 4 * half), F32),
        pltpu.VMEM((8, 4 * half), F32),
        pltpu.VMEM((8 * (blocks + 4), BLOCK), F32),
        pltpu.VMEM((3 * blocks, BLOCK), F32),
        pltpu.VMEM((3 * blocks, BLOCK), F32),
        pltpu.VMEM((STREAMS, 8, window), F32),
        *[pltpu.VMEM(x.shape, x.dtype) for x in constants],
        pltpu.SemaphoreType.DMA((len(constants),)),
    ]
    sizes = (channels, half, hidden, frames)
    payload, grads = run(
        lambda *refs: main_kernel(sizes, *refs),
        [(rows + 8 + 8 * STREAMS, LANES), (STREAMS * channels, frames)],
        [own, first, second, up_kernel, inner_kernel, outer_kernel.T, out_kernel, *constants],
        scratch,
        "decode_and_losses",
        24,
        len(constants),
    )

    index = lax.axis_index("tm")
    line = lax.broadcasted_iota(jnp.int32, payload.shape, 0)
    lane = lax.broadcasted_iota(jnp.int32, payload.shape, 1)
    step = 1
    while True:
        theirs = lax.ppermute(payload, "tm", [(i, i ^ step) for i in range(count)])
        if 2 * step == count:
            break
        low = index % step
        swap = ((low == 0) & (lane >= LANES // 2)) | ((low == step - 1) & (lane < LANES // 2))
        payload = jnp.where(
            line < rows + 8, payload + theirs, jnp.where(swap, theirs, payload)
        )
        step *= 2

    weights, aux = run(
        lambda *refs: combine_kernel((half, hidden, samples), *refs),
        [(2 * half + hidden + 8, LANES), (16, LANES)],
        [payload, theirs],
        [],
        "combine",
        2,
    )
    (latent_grad,) = run(
        lambda grads_ref, aux_ref, out, square: latent_kernel(channels, grads_ref, aux_ref, square, out),
        [latent.shape],
        [grads, aux],
        [pltpu.VMEM((LANES, LANES), F32)],
        "latent",
        2,
    )

    count = lax.axis_size("dp")
    step = 1
    while True:
        theirs = lax.ppermute(weights, "dp", [(i, i ^ step) for i in range(count)])
        if 2 * step == count:
            break
        weights = weights + theirs
        step *= 2
    up, inner, outer, out = run(
        lambda *refs: final_kernel((channels, half, hidden, params), *refs),
        [up_kernel.shape, inner_kernel.shape, outer_kernel.shape[::-1], out_kernel.shape],
        [weights, theirs],
        [],
        "final",
        2,
    )
    return (latent_grad, up, inner, outer.T, out)


def solution(mesh):
    for axis in ("dp", "tm"):
        size = mesh.shape[axis]
        assert size > 1 and size & (size - 1) == 0
    placed = (P("dp", None, "tm"), P("dp", "tm"), P(), P(), P(), P())
    return jax.shard_map(
        local,
        mesh=mesh,
        in_specs=placed,
        out_specs=(P("dp", None, "tm"), P(), P(), P(), P()),
        check_vma=False,
    )
```

```python
import jax
import jax.numpy as jnp
import numpy as np
from jax import lax
from jax.experimental import pallas as pl
from jax.experimental.pallas import tpu as pltpu
from jax.sharding import PartitionSpec as P

MELS = 64
WIN_COARSE = 1024
WIN_FINE = 256
LOSS_WEIGHTS = (0.25, 0.5, 0.5)
LANES = 128
BLOCK = 2 * LANES
STREAMS = 3
MARGIN = LANES // 2
F32 = jnp.float32
BF16 = jnp.bfloat16
VMEM = pltpu.MemorySpace.VMEM


def hi_lo(table):
    high = table.astype(np.float32).astype(BF16)
    low = (table - high.astype(np.float64)).astype(np.float32).astype(BF16)
    return high, low


def mel_table(window):
    half = window // 2
    top = 2595.0 * np.log10(1.0 + 12000.0 / 700.0)
    points = (np.arange(MELS + 1) + 1.0) / (MELS + 2.0) * top
    centers = 700.0 * (10.0 ** (points / 2595.0) - 1.0) / 12000.0 * half
    spacing = np.maximum(centers[1:] - centers[:-1], 1.0)
    places = np.arange(half)[:, None]
    return np.maximum(0.0, 1.0 - np.abs(places - centers[None, :MELS]) / spacing[None, :])


def tables():
    order = np.concatenate([np.arange(0, BLOCK, 2), np.arange(1, BLOCK, 2)])
    p = np.arange(LANES)
    cos, sin = [], []
    for rho in range(4):
        angle = 2.0 * np.pi / WIN_COARSE * ((order[:, None] * (4 * p + rho)[None, :]) % WIN_COARSE)
        cos.append(np.cos(angle))
        sin.append(np.sin(angle))
    even = np.concatenate(
        [np.concatenate([cos[0], -sin[0]], 1), np.concatenate([cos[2], -sin[2]], 1)], 0
    )
    odd = np.concatenate([cos[1], -sin[1], cos[3], -sin[3]], 1)
    angle = 2.0 * np.pi / WIN_FINE * ((order[:, None] * p[None, :]) % WIN_FINE)
    taper = 0.5 - 0.5 * np.cos(2.0 * np.pi / WIN_FINE * order)[:, None]
    fine = np.concatenate([taper * np.cos(angle), -taper * np.sin(angle)], 1)
    coarse_mel = mel_table(WIN_COARSE)
    coarse_mel = np.concatenate([coarse_mel[rho::4] for rho in (0, 2, 1, 3)], 0)
    fine_mel = mel_table(WIN_FINE)
    hann = 0.5 - 0.5 * np.cos(2.0 * np.pi / WIN_COARSE * np.arange(WIN_COARSE))
    hann = hann.reshape(4, BLOCK)[:, order].astype(np.float32)
    hann = np.concatenate([hann, np.zeros_like(hann)], 0)
    deal = np.zeros((BLOCK, BLOCK), np.float32)
    deal[order, np.arange(BLOCK)] = 1.0
    banks = [np.concatenate(hi_lo(x), 1) for x in (coarse_mel, fine_mel)]
    return (
        deal.astype(BF16),
        np.concatenate(hi_lo(even), 0),
        np.concatenate(hi_lo(odd), 0),
        hann,
        np.concatenate(hi_lo(fine), 0),
        np.concatenate(banks, 0),
    )


def split(x):
    high = x.astype(BF16)
    return high, (x - high.astype(F32)).astype(BF16)


def stacked(x):
    high = x.astype(BF16).astype(F32)
    return jnp.concatenate([high, x - high], axis=0).astype(BF16)


def dot(left, right, transposed=False):
    dims = (((1,), (1 if transposed else 0,)), ((), ()))
    return lax.dot_general(left, right, dims, preferred_element_type=F32)


def dot3(left, right_high, right_low, transposed=False):
    rows = left.shape[0]
    both = stacked(left)
    first = dot(both, right_high, transposed)
    second = dot(left.astype(BF16), right_low, transposed)
    return first[:rows] + first[rows:] + second


def to_mel(energy, bank):
    rows = energy.shape[0]
    both = dot(stacked(energy), bank)
    both = both[:rows] + both[rows:]
    return both[:, :MELS] + both[:, MELS:]


def from_mel(push, bank):
    rows = push.shape[0]
    both = dot(stacked(jnp.concatenate([push, push], axis=1)), bank, True)
    return both[:rows] + both[rows:]


def three_wide(weight):
    high = weight.astype(BF16).astype(F32)
    return jnp.concatenate([high, weight - high, high], axis=1).astype(BF16)


def apply(weight3, pair):
    high, low = pair
    return dot(weight3, jnp.concatenate([high, high, low], axis=0))


def elu_pair(x):
    slope = jnp.exp(jnp.minimum(x, 0.0))
    return jnp.where(x > 0, x, slope - 1.0), slope


def moved(x, by):
    return pltpu.roll(x, by % x.shape[1], 1)


def decode(sizes, weights, latent, keep, mask):
    half = sizes[1]
    activated, slope = elu_pair(latent)
    keep("slope_a", slope)
    both = jnp.concatenate([activated, moved(activated, 1)], 0)
    pair = split(both)
    keep("a", pair)
    upper = apply(weights["up"], pair) * mask
    rect, slope = elu_pair(upper)
    keep("slope_u", slope)
    pair = split(
        jnp.concatenate([moved(rect[half:], 1), rect, moved(rect[:half], -1)], 0)
    )
    keep("e", pair)
    hid, slope = elu_pair(apply(weights["inner"], pair))
    keep("slope_c", slope)
    pair = split(hid)
    keep("h", pair)
    mixed = (upper + apply(weights["outer"], pair)) * mask
    rect, slope = elu_pair(mixed)
    keep("slope_m", slope)
    pair = split(rect)
    keep("g", pair)
    taps = apply(weights["out"], pair)
    plus1, plus2, minus1, minus2 = (moved(taps, by) for by in (1, 2, -1, -2))
    return (
        (plus2[0:1] + plus1[2:3] + taps[4:5] + minus1[6:7]) * mask,
        (plus1[1:2] + taps[3:4] + minus1[5:6] + minus2[7:8]) * mask,
    )


KEPT = ("slope_a", "a_h", "a_l", "slope_u", "e_h", "e_l", "slope_c", "h_h", "h_l", "slope_m", "g_h", "g_l")


def kept_shapes(channels, half, hidden, window):
    rows = (channels, 2 * channels, 2 * half, 4 * half, 2 * hidden, 2 * hidden, 2 * half, 2 * half)
    shapes = []
    for i in range(4):
        shapes.append(((rows[2 * i], window), F32))
        shapes += [((rows[2 * i + 1], window), BF16)] * 2
    return shapes


def forward_weights(sizes, up, inner, outer, out, square):
    channels, half, hidden, _ = sizes
    weights = {}
    weights["up"] = three_wide(
        jnp.concatenate(
            [jnp.concatenate([up[r], up[r + 2]], axis=1) for r in range(2)], axis=0
        )
    )
    square[...] = jnp.zeros_like(square)
    for j in range(3):
        square[0:hidden, j * half : (j + 1) * half] = inner[j]
        square[hidden : 2 * hidden, (j + 1) * half : (j + 2) * half] = inner[j]
    weights["inner"] = three_wide(square[0 : 2 * hidden, :])
    square[...] = jnp.zeros_like(square)
    square[0:hidden, 0:half] = outer[...]
    square[hidden : 2 * hidden, half : 2 * half] = outer[...]
    weights["outer"] = three_wide(jnp.transpose(square[...])[0 : 2 * half, 0 : 2 * hidden])
    square[...] = jnp.zeros_like(square)
    square[1:8, 0:half] = out[...]
    square[0:7, half : 2 * half] = out[...]
    weights["out"] = three_wide(square[0:8, 0 : 2 * half])
    return weights


FORWARD = ("up", "inner", "outer", "out")


def backward_kernel(sizes, *refs):
    up, inner, outer, out = refs[:4]
    up_ref, inner_ref, outer_ref, out_ref = refs[8:12]
    square, sems = refs[15:]
    copies = [pltpu.make_async_copy(refs[5 + i], refs[12 + i], sems.at[i]) for i in range(3)]
    for copy in copies:
        copy.start()
    channels, half, hidden, _ = sizes
    for r in range(4):
        square[r * half : (r + 1) * half, 0:channels] = up[r]
        square[r * half : (r + 1) * half, channels:] = up[r]
    up_ref[...] = three_wide(jnp.transpose(square[...])[0:channels, :])
    square[...] = jnp.zeros_like(square)
    for j in range(3):
        square[(2 - j) * hidden : (3 - j) * hidden, 0:half] = inner[j]
        square[(3 - j) * hidden : (4 - j) * hidden, half : 2 * half] = inner[j]
    inner_ref[...] = three_wide(jnp.transpose(square[...])[0 : 2 * half, 0 : 4 * hidden])
    square[...] = jnp.zeros_like(square)
    square[0:hidden, 0:half] = outer[...]
    square[hidden : 2 * hidden, half : 2 * half] = outer[...]
    outer_ref[...] = three_wide(square[0 : 2 * hidden, 0 : 2 * half])
    square[...] = jnp.zeros_like(square)
    square[1:8, 0:half] = out[...]
    square[0:7, half : 2 * half] = out[...]
    out_ref[...] = three_wide(jnp.transpose(square[...])[0 : 2 * half, 0:8])
    for copy in copies:
        copy.wait()


def own_kernel(sizes, *refs):
    sources = refs[:9]
    packet_ref, latent_ref = refs[9:11]
    weight_refs = refs[11:15]
    kept = dict(zip(KEPT, refs[15:27]))
    table_refs = refs[27:29]
    up_ref, inner_ref, outer_ref, out_ref, target_ref, deal_ref, square, rows_ref, sems = refs[29:]
    channels, half, hidden, frames = sizes
    spaces = (latent_ref, target_ref, up_ref, inner_ref, outer_ref, out_ref, deal_ref, *table_refs)
    copies = []
    for i, (source, space) in enumerate(zip(sources, spaces)):
        if i == 0:
            source = source.at[0]
        copies.append(pltpu.make_async_copy(source, space, sems.at[i]))
    for copy in copies:
        copy.start()
    for copy in copies[:7]:
        copy.wait()
    weights = forward_weights(sizes, up_ref, inner_ref, outer_ref, out_ref, square)
    for name, ref in zip(FORWARD, weight_refs):
        ref[...] = weights[name]

    def keep(name, value):
        if isinstance(value, tuple):
            kept[name + "_h"][...], kept[name + "_l"][...] = value
        else:
            kept[name][...] = value

    latent = latent_ref[...]
    spread = moved(jnp.concatenate([latent, jnp.zeros((channels, LANES), F32)], 1), MARGIN)
    wave = jnp.concatenate(decode(sizes, weights, spread, keep, 1.0), 0)
    wave = moved(wave, -MARGIN)
    blocks = frames // LANES
    rows_ref[...] = jnp.zeros_like(rows_ref)
    for b in range(blocks):
        rows_ref[b : b + 1, :] = target_ref[:, b * BLOCK : (b + 1) * BLOCK]
    whole = rows_ref[...]
    high = whole.astype(BF16)
    rest = whole - high.astype(F32)
    middle = rest.astype(BF16)
    last = (rest - middle.astype(F32)).astype(BF16)
    deal = deal_ref[...]
    dealt = dot(high, deal) + dot(middle, deal) + dot(last, deal)
    packet_ref[0:8, 0:channels] = jnp.transpose(latent[:, 0:LANES])[0:8]
    packet_ref[0:8, channels:] = jnp.transpose(latent[:, frames - LANES :])[LANES - 8 :]
    for r in range(2):
        for b in range(blocks):
            packet_ref[8 + r * blocks + b : 9 + r * blocks + b, :] = wave[
                r : r + 1, b * LANES : (b + 1) * LANES
            ]
        at = 8 + (2 + r) * blocks
        packet_ref[at : at + blocks, :] = dealt[0:blocks, r * LANES : (r + 1) * LANES]
    for copy in copies[7:]:
        copy.wait()


def main_kernel(sizes, *refs):
    own_ref, first_ref, second_ref, latent_ref = refs[:4]
    weights = {name: ref[...] for name, ref in zip(FORWARD, refs[4:8])}
    kept = dict(zip(KEPT, refs[8:20]))
    up_back, back_inner, outer_back, out_back = (ref[...] for ref in refs[20:24])
    even_ref, odd_ref, hann_ref, fine_ref, bank_ref = refs[24:29]
    payload_ref, grads_ref = refs[29:31]
    (square, wblock, shifted, wave_b, targ_b, lanes_b) = refs[31:37]
    channels, half, hidden, frames = sizes
    window = frames + LANES
    own_blocks = frames // LANES
    index = lax.axis_index("tm")
    count = lax.axis_size("tm")
    odd_place = lax.rem(index, 2) == 1

    first, second = first_ref[...], second_ref[...]
    left = jnp.where(odd_place, first, second)
    right = jnp.where(odd_place, second, first)
    square[...] = jnp.zeros_like(square)
    square[MARGIN - 8 : MARGIN, 0:channels] = left[0:8, channels:]
    square[MARGIN : MARGIN + 8, channels:] = right[0:8, 0:channels]
    turned = jnp.transpose(square[...])
    lane = lax.broadcasted_iota(jnp.int32, (1, LANES), 1)
    ends = jnp.concatenate(
        [
            jnp.where(lane < MARGIN, turned[0:channels], moved(latent_ref[:, 0:LANES], MARGIN)),
            jnp.where(
                lane < MARGIN, moved(latent_ref[:, frames - LANES :], MARGIN), turned[channels:]
            ),
        ],
        axis=1,
    )
    place = lax.broadcasted_iota(jnp.int32, (1, window), 1) + index * frames - MARGIN
    mask = ((place >= 0) & (place < count * frames)).astype(F32)
    ends_mask = jnp.concatenate([mask[:, :LANES], mask[:, window - LANES :]], axis=1)
    saved = {}

    def joined(name, value):
        inside = kept[name]
        quarter = LANES // 4
        lane = lax.broadcasted_iota(jnp.int32, (value.shape[0], LANES), 1)
        head = jnp.where(lane < 3 * quarter, value[:, :LANES], inside[:, :LANES])
        tail = jnp.where(lane >= quarter, value[:, LANES:], inside[:, window - LANES :])
        saved[name] = jnp.concatenate([head, inside[:, LANES : window - LANES], tail], axis=1)

    def keep(name, value):
        if isinstance(value, tuple):
            joined(name + "_h", value[0])
            joined(name + "_l", value[1])
        else:
            joined(name, value)

    ends_wave = decode(sizes, weights, ends, keep, ends_mask)
    slope_a, slope_u, slope_c, slope_m = (saved["slope_" + x] for x in "aucm")

    for side, packet in enumerate((left, own_ref[...], right)):
        rows = slice(side * own_blocks, (side + 1) * own_blocks)
        for r in range(2):
            columns = slice(r * LANES, (r + 1) * LANES)
            at = 8 + r * own_blocks
            wave_b[rows, columns] = packet[at : at + own_blocks]
            at = 8 + (2 + r) * own_blocks
            targ_b[rows, columns] = packet[at : at + own_blocks]
    for r in range(2):
        columns = slice(r * LANES, (r + 1) * LANES)
        for side in range(2):
            piece = moved(ends_wave[r][:, side * LANES : (side + 1) * LANES], MARGIN)
            row = own_blocks * (1 + side)
            wave_b[row - 1 : row, columns] = jnp.where(
                lane >= LANES - 4, piece, wave_b[row - 1 : row, columns]
            )
            wave_b[row : row + 1, columns] = jnp.where(lane < 4, piece, wave_b[row : row + 1, columns])
    size = 2 * BLOCK
    even_h, even_l = even_ref.at[pl.ds(0, size)], even_ref.at[pl.ds(size, size)]
    odd_h, odd_l = odd_ref[0:BLOCK], odd_ref[BLOCK:]
    fine_h, fine_l = fine_ref.at[pl.ds(0, BLOCK)], fine_ref.at[pl.ds(BLOCK, BLOCK)]
    coarse_bank, fine_bank = bank_ref[0:size], bank_ref[size:]

    row_count = own_blocks + 4
    start = own_blocks - 3
    parts = []
    for j in range(4):
        rows = jnp.concatenate(
            [wave_b[pl.ds(start + j, row_count), :], targ_b[pl.ds(start + j, row_count), :]], 0
        )
        parts.append(rows * hann_ref[j : j + 1, :])
    even_sum, odd_sum = parts[0] + parts[2], parts[1] + parts[3]
    turned = jnp.concatenate([parts[0] - parts[2], parts[1] - parts[3]], axis=0)
    spec0 = dot3(even_sum + odd_sum, even_h[0:BLOCK], even_l[0:BLOCK])
    spec2 = dot3(even_sum - odd_sum, even_h[BLOCK:], even_l[BLOCK:])
    spec1 = dot3(turned, odd_h, odd_l)
    rows = 2 * row_count
    quarter = [(spec1[:rows, at : at + LANES], spec1[rows:, at : at + LANES]) for at in range(0, size, LANES)]
    real = jnp.concatenate(
        [
            spec0[:, :LANES],
            spec2[:, :LANES],
            quarter[0][0] + quarter[1][1],
            quarter[2][0] - quarter[3][1],
        ],
        1,
    )
    imag = jnp.concatenate(
        [
            spec0[:, LANES:],
            spec2[:, LANES:],
            quarter[1][0] - quarter[0][1],
            quarter[3][0] + quarter[2][1],
        ],
        1,
    )
    mel = to_mel(real * real + imag * imag, coarse_bank)
    level = jnp.sqrt(mel + 1.0)
    level_wave = level[:row_count]
    frame = lax.broadcasted_iota(jnp.int32, (row_count, MELS), 0) + index * own_blocks - 3
    slope = jnp.where(frame >= 0, (level_wave - level[row_count:]) / level_wave, 0.0)
    push = 2.0 * from_mel(slope, coarse_bank)
    real, imag = real[:row_count] * push, imag[:row_count] * push
    back0 = dot3(
        jnp.concatenate([real[:, :LANES], imag[:, :LANES]], 1), even_h[0:BLOCK], even_l[0:BLOCK], True
    )
    back2 = dot3(
        jnp.concatenate([real[:, LANES:BLOCK], imag[:, LANES:BLOCK]], 1),
        even_h[BLOCK:],
        even_l[BLOCK:],
        True,
    )
    real1, real3 = real[:, BLOCK : BLOCK + LANES], real[:, BLOCK + LANES :]
    imag1, imag3 = imag[:, BLOCK : BLOCK + LANES], imag[:, BLOCK + LANES :]
    back1 = dot3(
        jnp.concatenate(
            [
                jnp.concatenate([real1, imag1, real3, imag3], 1),
                jnp.concatenate([-imag1, real1, imag3, -real3], 1),
            ],
            0,
        ),
        odd_h,
        odd_l,
        True,
    )
    back1 = [back1[:row_count], back1[row_count:]]
    plus, minus = back0 + back2, back0 - back2
    backs = [
        plus + back1[0],
        minus + back1[1],
        plus - back1[0],
        minus - back1[1],
    ]
    coarse = jnp.zeros((own_blocks, BLOCK), F32)
    for j in range(4):
        coarse = coarse + (backs[j] * hann_ref[j : j + 1, :])[3 - j : 3 - j + own_blocks]

    hop = LANES // 4
    lane = lax.broadcasted_iota(jnp.int32, (1, LANES), 1)
    start = own_blocks - 1
    for which, source in enumerate((wave_b, targ_b)):
        for s in range(4):
            base = (which * 4 + s) * row_count
            for r in range(2):
                here = source[pl.ds(start, row_count), r * LANES : (r + 1) * LANES]
                if s:
                    there = source[pl.ds(start + 1, row_count), r * LANES : (r + 1) * LANES]
                    here = jnp.where(
                        lane < LANES - s * hop,
                        pltpu.roll(here, LANES - s * hop, 1),
                        pltpu.roll(there, LANES - s * hop, 1),
                    )
                shifted[base : base + row_count, r * LANES : (r + 1) * LANES] = here
    spec = dot3(shifted[...], fine_h[...], fine_l[...])
    real, imag = spec[:, :LANES], spec[:, LANES:]
    mel = to_mel(real * real + imag * imag, fine_bank)
    level = jnp.sqrt(mel + 1.0)
    fine_rows = 4 * row_count
    level_wave = level[:fine_rows]
    row = lax.broadcasted_iota(jnp.int32, (fine_rows, MELS), 0)
    frame = (lax.rem(row, row_count) - 1 + index * own_blocks) * 4 + row // row_count
    slope = jnp.where(frame >= 0, (level_wave - level[fine_rows:]) / level_wave, 0.0)
    push = 2.0 * from_mel(slope, fine_bank)
    back = dot3(
        jnp.concatenate([real[:fine_rows] * push, imag[:fine_rows] * push], 1),
        fine_h[...],
        fine_l[...],
        True,
    )
    fine = []
    for r in range(2):
        total = jnp.zeros((own_blocks, LANES), F32)
        for s in range(4):
            piece = back[s * row_count : (s + 1) * row_count, r * LANES : (r + 1) * LANES]
            if s:
                piece = pltpu.roll(piece, s * hop, 1)
                total = total + jnp.where(
                    lane >= s * hop, piece[1 : 1 + own_blocks], piece[0:own_blocks]
                )
            else:
                total = total + piece[1 : 1 + own_blocks]
        fine.append(total)
    fine = jnp.concatenate(fine, axis=1)

    own_rows = pl.ds(own_blocks, own_blocks)
    timed = 2.0 * (wave_b[own_rows, :] - targ_b[own_rows, :])

    totals, views, uppers, inners, mixeds, edges = [], [], [], [], [], []
    for i, stream in enumerate((timed, coarse, fine)):
        totals.append(jnp.sum(stream * stream))
        lanes_b[i] = jnp.zeros((8, window), F32)
        for b in range(own_blocks):
            for r in range(2):
                lanes_b[i, r : r + 1, b * LANES : (b + 1) * LANES] = stream[
                    b : b + 1, r * LANES : (r + 1) * LANES
                ]
        evens, odds = lanes_b[i, 0:1, :], lanes_b[i, 1:2, :]
        for k in range(8):
            source = odds if k % 2 else evens
            lanes_b[i, k : k + 1, :] = moved(source, MARGIN - (4 - k) // 2)
        view = lanes_b[i]
        views.append(view)
        high = view.astype(BF16).astype(F32)
        three = jnp.concatenate([high, high, view - high], axis=0).astype(BF16)
        grad_mixed = dot(out_back, three) * slope_m * mask
        mixed = split(grad_mixed)
        mixeds.append(mixed)
        grad_inner = apply(outer_back, mixed) * slope_c
        inners.append(split(grad_inner))
        spread = jnp.concatenate(
            [moved(grad_inner[hidden:], 1), grad_inner, moved(grad_inner[:hidden], -1)], 0
        )
        grad_upper = (grad_mixed + apply(back_inner, split(spread)) * slope_u) * mask
        uppers.append(split(grad_upper))
        both = jnp.concatenate([grad_upper, moved(grad_upper, -1)], 0)
        grads = moved(apply(up_back, split(both)) * slope_a * mask, -MARGIN)
        grads_ref[i * channels : (i + 1) * channels, :] = grads[:, :frames]
        turned = jnp.transpose(grads[:, frames:])
        edges.append(jnp.concatenate([turned[LANES - 8 :], turned[:8]], axis=1))

    def summed(pairs, name):
        rows = pairs[0][0].shape[0]
        both = jnp.concatenate([x for pair in pairs for x in pair], axis=0)
        highs = jnp.concatenate([pair[0] for pair in pairs], axis=0)
        first = dot(both, saved[name + "_h"], True)
        second = dot(highs, saved[name + "_l"], True)
        return [
            first[2 * i * rows : (2 * i + 1) * rows]
            + first[(2 * i + 1) * rows : (2 * i + 2) * rows]
            + second[i * rows : (i + 1) * rows]
            for i in range(STREAMS)
        ]

    for i, value in enumerate(summed(uppers, "a")):
        payload_ref[i * 2 * half : (i + 1) * 2 * half, :] = value
    base = STREAMS * 2 * half
    for i, value in enumerate(summed(inners, "e")):
        at = base + i * hidden
        payload_ref[at : at + hidden, 0 : 3 * half] = value[:hidden, : 3 * half] + value[hidden:, half:]
    highs = jnp.concatenate([pair[0] for pair in mixeds], axis=0)
    lows = jnp.concatenate([pair[1] for pair in mixeds], axis=0)
    both = jnp.concatenate([saved["h_h"], saved["h_l"]], axis=0)
    first = dot(both, highs, True)
    value = first[: 2 * hidden] + first[2 * hidden :] + dot(saved["h_h"], lows, True)
    for i in range(STREAMS):
        at = base + i * hidden
        columns = i * 2 * half
        payload_ref[at : at + hidden, 3 * half : 4 * half] = (
            value[:hidden, columns : columns + half] + value[hidden:, columns + half : columns + 2 * half]
        )
    taps = dot3(jnp.concatenate(views, axis=0), saved["g_h"], saved["g_l"], True)
    for i in range(STREAMS):
        wblock[0:7, i * half : (i + 1) * half] = (
            taps[8 * i + 1 : 8 * i + 8, :half] + taps[8 * i : 8 * i + 7, half:]
        )
    base = STREAMS * (2 * half + hidden)
    lane = lax.broadcasted_iota(jnp.int32, (1, half), 1)
    sums = jnp.where(lane == 0, totals[0], jnp.where(lane == 1, totals[1], totals[2]))
    wblock[7:8, :] = jnp.zeros((1, 4 * half), F32)
    wblock[0:7, STREAMS * half :] = jnp.zeros((7, half), F32)
    wblock[7:8, STREAMS * half :] = sums
    payload_ref[base : base + 8, :] = wblock[...]
    payload_ref[base + 8 :, :] = jnp.concatenate(edges, axis=0)


def combine_kernel(sizes, mine_ref, theirs_ref, weights_ref, aux_ref):
    half, hidden, samples = sizes
    rows = STREAMS * (2 * half + hidden)
    total = mine_ref[0 : rows + 8, :] + theirs_ref[0 : rows + 8, :]
    line = total[rows + 7 : rows + 8, :]
    lane = lax.broadcasted_iota(jnp.int32, line.shape, 1) - STREAMS * half
    wanted = jnp.where(lane == 0, LOSS_WEIGHTS[0], jnp.where(lane == 1, LOSS_WEIGHTS[1], LOSS_WEIGHTS[2]))
    line = wanted / jnp.sqrt(line / samples + 1e-06)
    scale = [
        jnp.sum(jnp.where(lane == i, line, 0.0), axis=1, keepdims=True) for i in range(STREAMS)
    ]
    up = sum(total[i * 2 * half : (i + 1) * 2 * half] * scale[i] for i in range(STREAMS))
    base = STREAMS * 2 * half
    inner = sum(total[base + i * hidden : base + (i + 1) * hidden] * scale[i] for i in range(STREAMS))
    last = total[rows : rows + 8]
    out = sum(
        (pltpu.roll(last, (4 - i) * half % (4 * half), 1) if i else last) * scale[i]
        for i in range(STREAMS)
    )
    place = lax.broadcasted_iota(jnp.int32, out.shape, 0)
    lane = lax.broadcasted_iota(jnp.int32, out.shape, 1)
    weights_ref[0 : 2 * half, :] = up
    weights_ref[2 * half : 2 * half + hidden, :] = inner
    weights_ref[2 * half + hidden :, :] = jnp.where((place < 7) & (lane < half), out, 0.0)
    index = lax.axis_index("tm")
    step = lax.axis_size("tm") // 2
    low = lax.rem(index, step)
    edge_lane = lax.broadcasted_iota(jnp.int32, (1, LANES), 1)
    swap = ((low == 0) & (edge_lane >= LANES // 2)) | ((low == step - 1) & (edge_lane < LANES // 2))
    edges = jnp.where(swap, theirs_ref[rows + 8 :, :], mine_ref[rows + 8 :, :])
    aux_ref[0:8, :] = sum(edges[8 * i : 8 * i + 8] * scale[i] for i in range(STREAMS))
    for i in range(STREAMS):
        aux_ref[8 + i : 9 + i, :] = jnp.broadcast_to(scale[i], (1, LANES))


def latent_kernel(channels, grads_ref, aux_ref, square, grad_ref):
    frames = grads_ref.shape[1]
    total = sum(
        grads_ref[i * channels : (i + 1) * channels, :] * aux_ref[8 + i : 9 + i, 0:1]
        for i in range(STREAMS)
    )
    grad_ref[0] = total
    square[...] = jnp.zeros_like(square)
    square[0:8, 0:channels] = aux_ref[0:8, channels:]
    square[LANES - 8 :, channels:] = aux_ref[0:8, 0:channels]
    turned = jnp.transpose(square[...])
    grad_ref[0, :, 0:LANES] = grad_ref[0, :, 0:LANES] + turned[0:channels]
    grad_ref[0, :, frames - LANES :] = grad_ref[0, :, frames - LANES :] + turned[channels:]


def final_kernel(sizes, mine_ref, theirs_ref, up_ref, inner_ref, outer_ref, out_ref):
    channels, half, hidden, params = sizes
    total = mine_ref[...] + theirs_ref[...]
    squares = jnp.sum(total * total)
    factor = jnp.minimum(1.0, 1.0 / jnp.sqrt(jnp.full((1, 1), squares / params + 1e-06, F32)))
    total = total * factor
    for r in range(2):
        up_ref[r] = total[r * half : (r + 1) * half, 0:channels]
        up_ref[r + 2] = total[r * half : (r + 1) * half, channels:]
    inner = total[2 * half : 2 * half + hidden]
    for j in range(3):
        inner_ref[j] = inner[:, j * half : (j + 1) * half]
    outer_ref[...] = inner[:, 3 * half :]
    out_ref[...] = total[2 * half + hidden : 2 * half + hidden + 7, 0:half]


def run(kernel, out_shape, operands, scratch, name, mebibytes, left=0):
    spec = pl.BlockSpec(memory_space=VMEM)
    kept = len(operands) - left
    hbm = [pltpu.with_memory_space_constraint(x, pltpu.MemorySpace.HBM) for x in operands[kept:]]
    operands = [*operands[:kept], *hbm]
    stay = pl.BlockSpec(memory_space=pltpu.MemorySpace.HBM)
    return pl.pallas_call(
        kernel,
        out_shape=tuple(
            jax.ShapeDtypeStruct(*(x if isinstance(x[1], type) else (x, F32))) for x in out_shape
        ),
        in_specs=[spec] * (len(operands) - left) + [stay] * left,
        out_specs=tuple([spec] * len(out_shape)),
        scratch_shapes=scratch,
        compiler_params=pltpu.CompilerParams(vmem_limit_bytes=mebibytes << 20),
        name=name,
    )(*operands)


def local(latent, target, up_kernel, inner_kernel, outer_kernel, out_kernel):
    assert latent.shape[0] == 1
    channels, frames = latent.shape[1:]
    half, hidden = outer_kernel.shape
    window = frames + LANES
    blocks = frames // LANES
    count = lax.axis_size("tm")
    samples = target.shape[1] * count
    params = sum(x.size for x in (up_kernel, inner_kernel, outer_kernel, out_kernel))

    constants = tables()
    sizes = (channels, half, hidden, frames)
    weights = [up_kernel, inner_kernel, outer_kernel.T, out_kernel]
    forward = [
        ((2 * half, 6 * channels), BF16),
        ((2 * hidden, 12 * half), BF16),
        ((2 * half, 6 * hidden), BF16),
        ((8, 6 * half), BF16),
    ]
    own, own_latent, *made, even, odd = run(
        lambda *refs: own_kernel(sizes, *refs),
        [
            (8 + 4 * blocks, LANES),
            (channels, frames),
            *forward,
            *kept_shapes(channels, half, hidden, window),
            *[(x.shape, BF16) for x in constants[1:3]],
        ],
        [latent, target, *weights, *constants[:3]],
        [
            *[pltpu.VMEM(x.shape, F32) for x in weights],
            pltpu.VMEM(target.shape, F32),
            pltpu.VMEM((BLOCK, BLOCK), BF16),
            pltpu.VMEM((LANES, LANES), F32),
            pltpu.VMEM((8, BLOCK), F32),
            pltpu.SemaphoreType.DMA((9,)),
        ],
        "own_decode",
        8,
        9,
    )
    backward = run(
        lambda *refs: backward_kernel(sizes, *refs),
        [
            ((channels, 12 * half), BF16),
            ((2 * half, 12 * hidden), BF16),
            ((2 * hidden, 6 * half), BF16),
            ((2 * half, 24), BF16),
            constants[3].shape,
            *[(x.shape, BF16) for x in constants[4:]],
        ],
        [*weights, own, *constants[3:]],
        [pltpu.VMEM((LANES, LANES), F32), pltpu.SemaphoreType.DMA((3,))],
        "backward_weights",
        4,
        3,
    )
    pairs = [(i, i ^ 1) for i in range(count) if i ^ 1 < count]
    first = lax.ppermute(own, "tm", pairs)
    pairs = [(i, i + 1 if i % 2 else i - 1) for i in range(count)]
    second = lax.ppermute(own, "tm", [(a, b) for a, b in pairs if 0 <= b < count])

    rows = STREAMS * (2 * half + hidden)

    payload, grads = run(
        lambda *refs: main_kernel(sizes, *refs),
        [(rows + 8 + 8 * STREAMS, LANES), (STREAMS * channels, frames)],
        [own, first, second, own_latent, *made, *backward[:4], even, odd, *backward[4:]],
        [
            pltpu.VMEM((LANES, LANES), F32),
            pltpu.VMEM((8, 4 * half), F32),
            pltpu.VMEM((8 * (blocks + 4), BLOCK), F32),
            pltpu.VMEM((3 * blocks, BLOCK), F32),
            pltpu.VMEM((3 * blocks, BLOCK), F32),
            pltpu.VMEM((STREAMS, 8, window), F32),
        ],
        "losses",
        16,
    )

    index = lax.axis_index("tm")
    line = lax.broadcasted_iota(jnp.int32, payload.shape, 0)
    lane = lax.broadcasted_iota(jnp.int32, payload.shape, 1)
    step = 1
    while True:
        theirs = lax.ppermute(payload, "tm", [(i, i ^ step) for i in range(count)])
        if 2 * step == count:
            break
        low = index % step
        swap = ((low == 0) & (lane >= LANES // 2)) | ((low == step - 1) & (lane < LANES // 2))
        payload = jnp.where(
            line < rows + 8, payload + theirs, jnp.where(swap, theirs, payload)
        )
        step *= 2

    weights, aux = run(
        lambda *refs: combine_kernel((half, hidden, samples), *refs),
        [(2 * half + hidden + 8, LANES), (16, LANES)],
        [payload, theirs],
        [],
        "combine",
        2,
    )
    (latent_grad,) = run(
        lambda grads_ref, aux_ref, out, square: latent_kernel(channels, grads_ref, aux_ref, square, out),
        [latent.shape],
        [grads, aux],
        [pltpu.VMEM((LANES, LANES), F32)],
        "latent",
        2,
    )

    count = lax.axis_size("dp")
    step = 1
    while True:
        theirs = lax.ppermute(weights, "dp", [(i, i ^ step) for i in range(count)])
        if 2 * step == count:
            break
        weights = weights + theirs
        step *= 2
    up, inner, outer, out = run(
        lambda *refs: final_kernel((channels, half, hidden, params), *refs),
        [up_kernel.shape, inner_kernel.shape, outer_kernel.shape[::-1], out_kernel.shape],
        [weights, theirs],
        [],
        "final",
        2,
    )
    return (latent_grad, up, inner, outer.T, out)


def solution(mesh):
    for axis in ("dp", "tm"):
        size = mesh.shape[axis]
        assert size > 1 and size & (size - 1) == 0
    placed = (P("dp", None, "tm"), P("dp", "tm"), P(), P(), P(), P())
    return jax.shard_map(
        local,
        mesh=mesh,
        in_specs=placed,
        out_specs=(P("dp", None, "tm"), P(), P(), P(), P()),
        check_vma=False,
    )
```

```python
import jax
import jax.numpy as jnp
import numpy as np
from jax import lax
from jax.experimental import pallas as pl
from jax.experimental.pallas import tpu as pltpu
from jax.sharding import PartitionSpec as P

MELS = 64
WIN_COARSE = 1024
WIN_FINE = 256
LOSS_WEIGHTS = (0.25, 0.5, 0.5)
LANES = 128
BLOCK = 2 * LANES
STREAMS = 3
MARGIN = LANES // 2
F32 = jnp.float32
BF16 = jnp.bfloat16
VMEM = pltpu.MemorySpace.VMEM


def hi_lo(table):
    high = table.astype(np.float32).astype(BF16)
    low = (table - high.astype(np.float64)).astype(np.float32).astype(BF16)
    return high, low


def mel_table(window):
    half = window // 2
    top = 2595.0 * np.log10(1.0 + 12000.0 / 700.0)
    points = (np.arange(MELS + 1) + 1.0) / (MELS + 2.0) * top
    centers = 700.0 * (10.0 ** (points / 2595.0) - 1.0) / 12000.0 * half
    spacing = np.maximum(centers[1:] - centers[:-1], 1.0)
    places = np.arange(half)[:, None]
    return np.maximum(0.0, 1.0 - np.abs(places - centers[None, :MELS]) / spacing[None, :])


def tables():
    order = np.concatenate([np.arange(0, BLOCK, 2), np.arange(1, BLOCK, 2)])
    angle = 2.0 * np.pi / BLOCK * ((order[:, None] * np.arange(LANES)[None, :]) % BLOCK)
    turns = np.concatenate([np.cos(angle), -np.sin(angle)], 1)
    coarse_mel = mel_table(WIN_COARSE)
    coarse_mel = np.concatenate([coarse_mel[rho::4] for rho in range(4)], 0)
    fine_mel = mel_table(WIN_FINE)
    hann = 0.5 - 0.5 * np.cos(2.0 * np.pi / WIN_COARSE * np.arange(WIN_COARSE))
    twist = 2.0 * np.pi / WIN_COARSE * np.arange(1, 4)[:, None] * order[None, :]
    taper = 0.5 - 0.5 * np.cos(2.0 * np.pi / WIN_FINE * order)[None, :]
    lines = [hann.reshape(4, BLOCK)[:, order], np.cos(twist), np.sin(twist), taper]
    lines = np.concatenate(lines + [np.zeros((5, BLOCK))], 0).astype(np.float32)
    deal = np.zeros((BLOCK, BLOCK), np.float32)
    deal[order, np.arange(BLOCK)] = 1.0
    banks = [np.concatenate(hi_lo(x), 1) for x in (coarse_mel, fine_mel)]
    return deal.astype(BF16), lines, np.concatenate(hi_lo(turns), 0), np.concatenate(banks, 0)


def split(x):
    high = x.astype(BF16)
    return high, (x - high.astype(F32)).astype(BF16)


def stacked(x):
    high = x.astype(BF16).astype(F32)
    return jnp.concatenate([high, x - high], axis=0).astype(BF16)


def dot(left, right, transposed=False):
    dims = (((1,), (1 if transposed else 0,)), ((), ()))
    return lax.dot_general(left, right, dims, preferred_element_type=F32)


def dot3(left, right_high, right_low, transposed=False):
    rows = left.shape[0]
    both = stacked(left)
    first = dot(both, right_high, transposed)
    second = dot(left.astype(BF16), right_low, transposed)
    return first[:rows] + first[rows:] + second


def to_mel(energy, bank):
    rows = energy.shape[0]
    both = dot(stacked(energy), bank)
    both = both[:rows] + both[rows:]
    return both[:, :MELS] + both[:, MELS:]


def from_mel(push, bank):
    rows = push.shape[0]
    both = dot(stacked(jnp.concatenate([push, push], axis=1)), bank, True)
    return both[:rows] + both[rows:]


def three_wide(weight):
    high = weight.astype(BF16).astype(F32)
    return jnp.concatenate([high, weight - high, high], axis=1).astype(BF16)


def apply(weight3, pair):
    high, low = pair
    return dot(weight3, jnp.concatenate([high, high, low], axis=0))


def elu_pair(x):
    slope = jnp.exp(jnp.minimum(x, 0.0))
    return jnp.where(x > 0, x, slope - 1.0), slope


def moved(x, by):
    return pltpu.roll(x, by % x.shape[1], 1)


def decode(sizes, weights, latent, keep, mask):
    half = sizes[1]
    activated, slope = elu_pair(latent)
    keep("slope_a", slope)
    both = jnp.concatenate([activated, moved(activated, 1)], 0)
    pair = split(both)
    keep("a", pair)
    upper = apply(weights["up"], pair) * mask
    rect, slope = elu_pair(upper)
    keep("slope_u", slope)
    pair = split(
        jnp.concatenate([moved(rect[half:], 1), rect, moved(rect[:half], -1)], 0)
    )
    keep("e", pair)
    hid, slope = elu_pair(apply(weights["inner"], pair))
    keep("slope_c", slope)
    pair = split(hid)
    keep("h", pair)
    mixed = (upper + apply(weights["outer"], pair)) * mask
    rect, slope = elu_pair(mixed)
    keep("slope_m", slope)
    pair = split(rect)
    keep("g", pair)
    taps = apply(weights["out"], pair)
    plus1, plus2, minus1, minus2 = (moved(taps, by) for by in (1, 2, -1, -2))
    return (
        (plus2[0:1] + plus1[2:3] + taps[4:5] + minus1[6:7]) * mask,
        (plus1[1:2] + taps[3:4] + minus1[5:6] + minus2[7:8]) * mask,
    )


KEPT = ("slope_a", "a_h", "a_l", "slope_u", "e_h", "e_l", "slope_c", "h_h", "h_l", "slope_m", "g_h", "g_l")


def kept_shapes(channels, half, hidden, window):
    rows = (channels, 2 * channels, 2 * half, 4 * half, 2 * hidden, 2 * hidden, 2 * half, 2 * half)
    shapes = []
    for i in range(4):
        shapes.append(((rows[2 * i], window), F32))
        shapes += [((rows[2 * i + 1], window), BF16)] * 2
    return shapes


def forward_weights(sizes, up, inner, outer, out, square):
    channels, half, hidden, _ = sizes
    weights = {}
    weights["up"] = three_wide(
        jnp.concatenate(
            [jnp.concatenate([up[r], up[r + 2]], axis=1) for r in range(2)], axis=0
        )
    )
    square[...] = jnp.zeros_like(square)
    for j in range(3):
        square[0:hidden, j * half : (j + 1) * half] = inner[j]
        square[hidden : 2 * hidden, (j + 1) * half : (j + 2) * half] = inner[j]
    weights["inner"] = three_wide(square[0 : 2 * hidden, :])
    square[...] = jnp.zeros_like(square)
    square[0:hidden, 0:half] = outer[...]
    square[hidden : 2 * hidden, half : 2 * half] = outer[...]
    weights["outer"] = three_wide(jnp.transpose(square[...])[0 : 2 * half, 0 : 2 * hidden])
    square[...] = jnp.zeros_like(square)
    square[1:8, 0:half] = out[...]
    square[0:7, half : 2 * half] = out[...]
    weights["out"] = three_wide(square[0:8, 0 : 2 * half])
    return weights


FORWARD = ("up", "inner", "outer", "out")


def backward_kernel(sizes, *refs):
    up, inner, outer, out = refs[:4]
    up_ref, inner_ref, outer_ref, out_ref = refs[8:12]
    square, sems = refs[15:]
    copies = [pltpu.make_async_copy(refs[5 + i], refs[12 + i], sems.at[i]) for i in range(3)]
    for copy in copies:
        copy.start()
    channels, half, hidden, _ = sizes
    for r in range(4):
        square[r * half : (r + 1) * half, 0:channels] = up[r]
        square[r * half : (r + 1) * half, channels:] = up[r]
    up_ref[...] = three_wide(jnp.transpose(square[...])[0:channels, :])
    square[...] = jnp.zeros_like(square)
    for j in range(3):
        square[(2 - j) * hidden : (3 - j) * hidden, 0:half] = inner[j]
        square[(3 - j) * hidden : (4 - j) * hidden, half : 2 * half] = inner[j]
    inner_ref[...] = three_wide(jnp.transpose(square[...])[0 : 2 * half, 0 : 4 * hidden])
    square[...] = jnp.zeros_like(square)
    square[0:hidden, 0:half] = outer[...]
    square[hidden : 2 * hidden, half : 2 * half] = outer[...]
    outer_ref[...] = three_wide(square[0 : 2 * hidden, 0 : 2 * half])
    square[...] = jnp.zeros_like(square)
    square[1:8, 0:half] = out[...]
    square[0:7, half : 2 * half] = out[...]
    out_ref[...] = three_wide(jnp.transpose(square[...])[0 : 2 * half, 0:8])
    for copy in copies:
        copy.wait()


def own_kernel(sizes, *refs):
    sources = refs[:7]
    packet_ref, latent_ref = refs[7:9]
    weight_refs = refs[9:13]
    kept = dict(zip(KEPT, refs[13:25]))
    up_ref, inner_ref, outer_ref, out_ref, target_ref, deal_ref, square, rows_ref, sems = refs[25:]
    channels, half, hidden, frames = sizes
    spaces = (latent_ref, target_ref, up_ref, inner_ref, outer_ref, out_ref, deal_ref)
    copies = []
    for i, (source, space) in enumerate(zip(sources, spaces)):
        if i == 0:
            source = source.at[0]
        copies.append(pltpu.make_async_copy(source, space, sems.at[i]))
    for copy in copies:
        copy.start()
    for copy in copies:
        copy.wait()
    weights = forward_weights(sizes, up_ref, inner_ref, outer_ref, out_ref, square)
    for name, ref in zip(FORWARD, weight_refs):
        ref[...] = weights[name]

    def keep(name, value):
        if isinstance(value, tuple):
            kept[name + "_h"][...], kept[name + "_l"][...] = value
        else:
            kept[name][...] = value

    latent = latent_ref[...]
    spread = moved(jnp.concatenate([latent, jnp.zeros((channels, LANES), F32)], 1), MARGIN)
    wave = jnp.concatenate(decode(sizes, weights, spread, keep, 1.0), 0)
    wave = moved(wave, -MARGIN)
    blocks = frames // LANES
    rows_ref[...] = jnp.zeros_like(rows_ref)
    for b in range(blocks):
        rows_ref[b : b + 1, :] = target_ref[:, b * BLOCK : (b + 1) * BLOCK]
    whole = rows_ref[...]
    high = whole.astype(BF16)
    rest = whole - high.astype(F32)
    middle = rest.astype(BF16)
    last = (rest - middle.astype(F32)).astype(BF16)
    deal = deal_ref[...]
    dealt = dot(high, deal) + dot(middle, deal) + dot(last, deal)
    packet_ref[0:8, 0:channels] = jnp.transpose(latent[:, 0:LANES])[0:8]
    packet_ref[0:8, channels:] = jnp.transpose(latent[:, frames - LANES :])[LANES - 8 :]
    for r in range(2):
        for b in range(blocks):
            packet_ref[8 + r * blocks + b : 9 + r * blocks + b, :] = wave[
                r : r + 1, b * LANES : (b + 1) * LANES
            ]
        at = 8 + (2 + r) * blocks
        packet_ref[at : at + blocks, :] = dealt[0:blocks, r * LANES : (r + 1) * LANES]


def main_kernel(sizes, *refs):
    own_ref, first_ref, second_ref, latent_ref = refs[:4]
    weights = {name: ref[...] for name, ref in zip(FORWARD, refs[4:8])}
    kept = dict(zip(KEPT, refs[8:20]))
    up_back, back_inner, outer_back, out_back = (ref[...] for ref in refs[20:24])
    lines_ref, turns_ref, bank_ref = refs[24:27]
    keep_ref, send_ref, grads_ref = refs[27:30]
    (square, wblock, shifted, wave_b, targ_b, lanes_b) = refs[30:36]
    channels, half, hidden, frames = sizes
    window = frames + LANES
    own_blocks = frames // LANES
    index = lax.axis_index("tm")
    count = lax.axis_size("tm")
    odd_place = lax.rem(index, 2) == 1

    first, second = first_ref[...], second_ref[...]
    left = jnp.where(odd_place, first, second)
    right = jnp.where(odd_place, second, first)
    square[...] = jnp.zeros_like(square)
    square[MARGIN - 8 : MARGIN, 0:channels] = left[0:8, channels:]
    square[MARGIN : MARGIN + 8, channels:] = right[0:8, 0:channels]
    turned = jnp.transpose(square[...])
    lane = lax.broadcasted_iota(jnp.int32, (1, LANES), 1)
    ends = jnp.concatenate(
        [
            jnp.where(lane < MARGIN, turned[0:channels], moved(latent_ref[:, 0:LANES], MARGIN)),
            jnp.where(
                lane < MARGIN, moved(latent_ref[:, frames - LANES :], MARGIN), turned[channels:]
            ),
        ],
        axis=1,
    )
    place = lax.broadcasted_iota(jnp.int32, (1, window), 1) + index * frames - MARGIN
    mask = ((place >= 0) & (place < count * frames)).astype(F32)
    ends_mask = jnp.concatenate([mask[:, :LANES], mask[:, window - LANES :]], axis=1)
    saved = {}

    def joined(name, value):
        inside = kept[name]
        quarter = LANES // 4
        lane = lax.broadcasted_iota(jnp.int32, (value.shape[0], LANES), 1)
        head = jnp.where(lane < 3 * quarter, value[:, :LANES], inside[:, :LANES])
        tail = jnp.where(lane >= quarter, value[:, LANES:], inside[:, window - LANES :])
        saved[name] = jnp.concatenate([head, inside[:, LANES : window - LANES], tail], axis=1)

    def keep(name, value):
        if isinstance(value, tuple):
            joined(name + "_h", value[0])
            joined(name + "_l", value[1])
        else:
            joined(name, value)

    ends_wave = decode(sizes, weights, ends, keep, ends_mask)
    slope_a, slope_u, slope_c, slope_m = (saved["slope_" + x] for x in "aucm")

    for side, packet in enumerate((left, own_ref[...], right)):
        rows = slice(side * own_blocks, (side + 1) * own_blocks)
        for r in range(2):
            columns = slice(r * LANES, (r + 1) * LANES)
            at = 8 + r * own_blocks
            wave_b[rows, columns] = packet[at : at + own_blocks]
            at = 8 + (2 + r) * own_blocks
            targ_b[rows, columns] = packet[at : at + own_blocks]
    for r in range(2):
        columns = slice(r * LANES, (r + 1) * LANES)
        for side in range(2):
            piece = moved(ends_wave[r][:, side * LANES : (side + 1) * LANES], MARGIN)
            row = own_blocks * (1 + side)
            wave_b[row - 1 : row, columns] = jnp.where(
                lane >= LANES - 4, piece, wave_b[row - 1 : row, columns]
            )
            wave_b[row : row + 1, columns] = jnp.where(lane < 4, piece, wave_b[row : row + 1, columns])
    turns_h, turns_l = turns_ref[0:BLOCK], turns_ref[BLOCK:]
    coarse_bank, fine_bank = bank_ref[0 : 2 * BLOCK], bank_ref[2 * BLOCK :]
    line = [lines_ref[i : i + 1, :] for i in range(11)]
    hann, cos, sin, taper = line[0:4], line[4:7], line[7:10], line[10]

    row_count = own_blocks + 4
    start = own_blocks - 3
    parts = []
    for j in range(4):
        rows = jnp.concatenate(
            [wave_b[pl.ds(start + j, row_count), :], targ_b[pl.ds(start + j, row_count), :]], 0
        )
        parts.append(rows * hann[j])
    even_sum, odd_sum = parts[0] + parts[2], parts[1] + parts[3]
    pair0, pair1 = even_sum + odd_sum, even_sum - odd_sum
    part0, part1 = parts[0] - parts[2], parts[1] - parts[3]
    blocks_in = [
        pair0,
        part0 * cos[0] - part1 * sin[0],
        -part1 * cos[0] - part0 * sin[0],
        pair1 * cos[1],
        -pair1 * sin[1],
        part0 * cos[2] + part1 * sin[2],
        part1 * cos[2] - part0 * sin[2],
    ]

    hop = LANES // 4
    lane = lax.broadcasted_iota(jnp.int32, (1, LANES), 1)
    start_fine = own_blocks - 1
    for which, source in enumerate((wave_b, targ_b)):
        for s in range(4):
            base = (which * 4 + s) * row_count
            for r in range(2):
                here = source[pl.ds(start_fine, row_count), r * LANES : (r + 1) * LANES]
                if s:
                    there = source[pl.ds(start_fine + 1, row_count), r * LANES : (r + 1) * LANES]
                    here = jnp.where(
                        lane < LANES - s * hop,
                        pltpu.roll(here, LANES - s * hop, 1),
                        pltpu.roll(there, LANES - s * hop, 1),
                    )
                shifted[base : base + row_count, r * LANES : (r + 1) * LANES] = here
    spec = dot3(jnp.concatenate([*blocks_in, shifted[...] * taper], axis=0), turns_h, turns_l)
    rows = 2 * row_count
    bins = [spec[i * rows : (i + 1) * rows] for i in range(7)]
    real, imag = [bins[0][:, :LANES]], [bins[0][:, LANES:]]
    for first_bin, second_bin in (bins[1:3], bins[3:5], bins[5:7]):
        real.append(first_bin[:, :LANES] - second_bin[:, LANES:])
        imag.append(first_bin[:, LANES:] + second_bin[:, :LANES])
    real, imag = jnp.concatenate(real, axis=1), jnp.concatenate(imag, axis=1)
    spec_fine = spec[7 * rows :]
    real_fine, imag_fine = spec_fine[:, :LANES], spec_fine[:, LANES:]
    mel_fine = to_mel(real_fine * real_fine + imag_fine * imag_fine, fine_bank)
    level_fine = jnp.sqrt(mel_fine + 1.0)
    fine_rows = 4 * row_count
    level_wave_fine = level_fine[:fine_rows]
    row_fine = lax.broadcasted_iota(jnp.int32, (fine_rows, MELS), 0)
    frame_fine = (lax.rem(row_fine, row_count) - 1 + index * own_blocks) * 4 + row_fine // row_count
    slope_fine = jnp.where(frame_fine >= 0, (level_wave_fine - level_fine[fine_rows:]) / level_wave_fine, 0.0)
    mel = to_mel(real * real + imag * imag, coarse_bank)
    level = jnp.sqrt(mel + 1.0)
    level_wave = level[:row_count]
    frame = lax.broadcasted_iota(jnp.int32, (row_count, MELS), 0) + index * own_blocks - 3
    slope = jnp.where(frame >= 0, (level_wave - level[row_count:]) / level_wave, 0.0)
    push_fine = 2.0 * from_mel(slope_fine, fine_bank)
    push = 2.0 * from_mel(slope, coarse_bank)
    real, imag = real[:row_count] * push, imag[:row_count] * push
    wide = []
    for rho in range(4):
        columns = slice(rho * LANES, (rho + 1) * LANES)
        first_bin, second_bin = real[:, columns], imag[:, columns]
        wide.append(jnp.concatenate([first_bin, second_bin], axis=1))
        if rho:
            wide.append(jnp.concatenate([second_bin, -first_bin], axis=1))
    wide.append(
        jnp.concatenate([real_fine[:fine_rows] * push_fine, imag_fine[:fine_rows] * push_fine], 1)
    )
    back = dot3(jnp.concatenate(wide, axis=0), turns_h, turns_l, True)
    back_fine = back[7 * row_count :] * taper
    back = [back[i * row_count : (i + 1) * row_count] for i in range(7)]
    back0, back2 = back[0], back[3] * cos[1] - back[4] * sin[1]
    back1 = [
        back[1] * cos[0] - back[2] * sin[0] + back[5] * cos[2] - back[6] * sin[2],
        back[5] * sin[2] + back[6] * cos[2] - back[1] * sin[0] - back[2] * cos[0],
    ]
    fine = []
    for r in range(2):
        total = jnp.zeros((own_blocks, LANES), F32)
        for s in range(4):
            piece = back_fine[s * row_count : (s + 1) * row_count, r * LANES : (r + 1) * LANES]
            if s:
                piece = pltpu.roll(piece, s * hop, 1)
                total = total + jnp.where(
                    lane >= s * hop, piece[1 : 1 + own_blocks], piece[0:own_blocks]
                )
            else:
                total = total + piece[1 : 1 + own_blocks]
        fine.append(total)
    fine = jnp.concatenate(fine, axis=1)

    plus, minus = back0 + back2, back0 - back2
    backs = [
        plus + back1[0],
        minus + back1[1],
        plus - back1[0],
        minus - back1[1],
    ]
    coarse = jnp.zeros((own_blocks, BLOCK), F32)
    for j in range(4):
        coarse = coarse + (backs[j] * hann[j])[3 - j : 3 - j + own_blocks]

    own_rows = pl.ds(own_blocks, own_blocks)
    timed = 2.0 * (wave_b[own_rows, :] - targ_b[own_rows, :])

    streams = (timed, coarse, fine)
    totals = [jnp.sum(stream * stream) for stream in streams]
    lanes_b[...] = jnp.zeros_like(lanes_b)
    for i, stream in enumerate(streams):
        for b in range(own_blocks):
            for r in range(2):
                lanes_b[r, i : i + 1, b * LANES : (b + 1) * LANES] = stream[
                    b : b + 1, r * LANES : (r + 1) * LANES
                ]
    evens, odds = lanes_b[0], lanes_b[1]
    shifted_rows = [moved(odds if k % 2 else evens, MARGIN - (4 - k) // 2) for k in range(8)]
    views = [
        jnp.concatenate([shifted_rows[k][i : i + 1] for k in range(8)], axis=0) for i in range(STREAMS)
    ]
    threes = []
    for view in views:
        high = view.astype(BF16).astype(F32)
        threes.append(jnp.concatenate([high, high, view - high], axis=0).astype(BF16))
    slope_m, slope_u = slope_m * mask, slope_u * mask
    slope_a = slope_a * mask
    grad_mixed = [dot(out_back, three) * slope_m for three in threes]
    mixeds = [split(x) for x in grad_mixed]
    grad_inner = [apply(outer_back, pair) * slope_c for pair in mixeds]
    inners = [split(x) for x in grad_inner]
    spreads = [
        split(jnp.concatenate([moved(x[hidden:], 1), x, moved(x[:hidden], -1)], 0)) for x in grad_inner
    ]
    grad_upper = [
        x + apply(back_inner, pair) * slope_u for x, pair in zip(grad_mixed, spreads)
    ]
    uppers = [split(x) for x in grad_upper]
    nexts = [split(moved(x, -1)) for x in grad_upper]
    edges = []
    for i in range(STREAMS):
        both = tuple(jnp.concatenate([x, y], 0) for x, y in zip(uppers[i], nexts[i]))
        grads = moved(apply(up_back, both) * slope_a, -MARGIN)
        grads_ref[i * channels : (i + 1) * channels, :] = grads[:, :frames]
        turned = jnp.transpose(grads[:, frames:])
        edges.append(jnp.concatenate([turned[LANES - 8 :], turned[:8]], axis=1))

    def summed(pairs, name):
        rows = pairs[0][0].shape[0]
        both = jnp.concatenate([x for pair in pairs for x in pair], axis=0)
        highs = jnp.concatenate([pair[0] for pair in pairs], axis=0)
        first = dot(both, saved[name + "_h"], True)
        second = dot(highs, saved[name + "_l"], True)
        return [
            first[2 * i * rows : (2 * i + 1) * rows]
            + first[(2 * i + 1) * rows : (2 * i + 2) * rows]
            + second[i * rows : (i + 1) * rows]
            for i in range(STREAMS)
        ]

    def put(value, at, columns):
        rows = value.shape[0] // 2
        low, high = value[:rows], value[rows:]
        keep_ref[at : at + rows, columns] = jnp.where(odd_place, high, low)
        send_ref[at : at + rows, columns] = jnp.where(odd_place, low, high)

    step = half + hidden // 2
    for i, value in enumerate(summed(uppers, "a")):
        put(value, i * step, slice(0, 2 * channels))
    for i, value in enumerate(summed(inners, "e")):
        put(value[:hidden, : 3 * half] + value[hidden:, half:], i * step + half, slice(0, 3 * half))
    highs = jnp.concatenate([pair[0] for pair in mixeds], axis=0)
    lows = jnp.concatenate([pair[1] for pair in mixeds], axis=0)
    both = jnp.concatenate([saved["h_h"], saved["h_l"]], axis=0)
    first = dot(both, highs, True)
    value = first[: 2 * hidden] + first[2 * hidden :] + dot(saved["h_h"], lows, True)
    for i in range(STREAMS):
        columns = i * 2 * half
        put(
            value[:hidden, columns : columns + half]
            + value[hidden:, columns + half : columns + 2 * half],
            i * step + half,
            slice(3 * half, 4 * half),
        )
    taps = dot3(jnp.concatenate(views, axis=0), saved["g_h"], saved["g_l"], True)
    for i in range(STREAMS):
        wblock[0:7, i * half : (i + 1) * half] = (
            taps[8 * i + 1 : 8 * i + 8, :half] + taps[8 * i : 8 * i + 7, half:]
        )
    lane = lax.broadcasted_iota(jnp.int32, (1, half), 1)
    sums = jnp.where(lane == 0, totals[0], jnp.where(lane == 1, totals[1], totals[2]))
    wblock[7:8, :] = jnp.zeros((1, 4 * half), F32)
    wblock[0:7, STREAMS * half :] = jnp.zeros((7, half), F32)
    wblock[7:8, STREAMS * half :] = sums
    edges = jnp.concatenate(edges, axis=0)
    for ref in (keep_ref, send_ref):
        ref[STREAMS * step : STREAMS * step + 8, :] = wblock[...]
        ref[STREAMS * step + 8 :, :] = edges


def combine_kernel(sizes, mine_ref, theirs_ref, weights_ref, aux_ref):
    half, hidden, samples = sizes
    step = half + hidden // 2
    rows = STREAMS * step
    total = mine_ref[0 : rows + 8, :] + theirs_ref[0 : rows + 8, :]
    line = total[rows + 7 : rows + 8, :]
    lane = lax.broadcasted_iota(jnp.int32, line.shape, 1) - STREAMS * half
    wanted = jnp.where(lane == 0, LOSS_WEIGHTS[0], jnp.where(lane == 1, LOSS_WEIGHTS[1], LOSS_WEIGHTS[2]))
    line = wanted / jnp.sqrt(line / samples + 1e-06)
    scale = [
        jnp.sum(jnp.where(lane == i, line, 0.0), axis=1, keepdims=True) for i in range(STREAMS)
    ]
    weights_ref[0:step, :] = sum(total[i * step : (i + 1) * step] * scale[i] for i in range(STREAMS))
    last = total[rows : rows + 8]
    out = sum(
        (pltpu.roll(last, (4 - i) * half % (4 * half), 1) if i else last) * scale[i]
        for i in range(STREAMS)
    )
    place = lax.broadcasted_iota(jnp.int32, out.shape, 0)
    lane = lax.broadcasted_iota(jnp.int32, out.shape, 1)
    weights_ref[step:, :] = jnp.where((place < 7) & (lane < half), out, 0.0)
    index = lax.axis_index("tm")
    step = lax.axis_size("tm") // 2
    low = lax.rem(index, step)
    edge_lane = lax.broadcasted_iota(jnp.int32, (1, LANES), 1)
    swap = ((low == 0) & (edge_lane >= LANES // 2)) | ((low == step - 1) & (edge_lane < LANES // 2))
    edges = jnp.where(swap, theirs_ref[rows + 8 :, :], mine_ref[rows + 8 :, :])
    aux_ref[0:8, :] = sum(edges[8 * i : 8 * i + 8] * scale[i] for i in range(STREAMS))
    for i in range(STREAMS):
        aux_ref[8 + i : 9 + i, :] = jnp.broadcast_to(scale[i], (1, LANES))


def latent_kernel(channels, grads_ref, aux_ref, square, grad_ref):
    frames = grads_ref.shape[1]
    total = sum(
        grads_ref[i * channels : (i + 1) * channels, :] * aux_ref[8 + i : 9 + i, 0:1]
        for i in range(STREAMS)
    )
    grad_ref[0] = total
    square[...] = jnp.zeros_like(square)
    square[0:8, 0:channels] = aux_ref[0:8, channels:]
    square[LANES - 8 :, channels:] = aux_ref[0:8, 0:channels]
    turned = jnp.transpose(square[...])
    grad_ref[0, :, 0:LANES] = grad_ref[0, :, 0:LANES] + turned[0:channels]
    grad_ref[0, :, frames - LANES :] = grad_ref[0, :, frames - LANES :] + turned[channels:]


def final_kernel(sizes, mine_ref, theirs_ref, up_ref, inner_ref, outer_ref, out_ref):
    channels, half, hidden, params = sizes
    step = half + hidden // 2
    mine, theirs = mine_ref[...], theirs_ref[...]
    odd_place = lax.rem(lax.axis_index("tm"), 2) == 1
    low = jnp.where(odd_place, theirs[:step], mine[:step])
    high = jnp.where(odd_place, mine[:step], theirs[:step])
    out = mine[step:]
    squares = jnp.sum(low * low) + jnp.sum(high * high) + jnp.sum(out * out)
    factor = jnp.minimum(1.0, 1.0 / jnp.sqrt(jnp.full((1, 1), squares / params + 1e-06, F32)))
    low, high = low * factor, high * factor
    for r, part in enumerate((low, high)):
        up_ref[r] = part[0:half, 0:channels]
        up_ref[r + 2] = part[0:half, channels:]
    inner = jnp.concatenate([low[half:], high[half:]], axis=0)
    for j in range(3):
        inner_ref[j] = inner[:, j * half : (j + 1) * half]
    outer_ref[...] = inner[:, 3 * half :]
    out_ref[...] = (out * factor)[0:7, 0:half]


def run(kernel, out_shape, operands, scratch, name, mebibytes, left=0):
    spec = pl.BlockSpec(memory_space=VMEM)
    kept = len(operands) - left
    hbm = [pltpu.with_memory_space_constraint(x, pltpu.MemorySpace.HBM) for x in operands[kept:]]
    operands = [*operands[:kept], *hbm]
    stay = pl.BlockSpec(memory_space=pltpu.MemorySpace.HBM)
    return pl.pallas_call(
        kernel,
        out_shape=tuple(
            jax.ShapeDtypeStruct(*(x if isinstance(x[1], type) else (x, F32))) for x in out_shape
        ),
        in_specs=[spec] * (len(operands) - left) + [stay] * left,
        out_specs=tuple([spec] * len(out_shape)),
        scratch_shapes=scratch,
        compiler_params=pltpu.CompilerParams(vmem_limit_bytes=mebibytes << 20),
        name=name,
    )(*operands)


def local(latent, target, up_kernel, inner_kernel, outer_kernel, out_kernel):
    assert latent.shape[0] == 1
    channels, frames = latent.shape[1:]
    half, hidden = outer_kernel.shape
    window = frames + LANES
    blocks = frames // LANES
    count = lax.axis_size("tm")
    samples = target.shape[1] * count
    params = sum(x.size for x in (up_kernel, inner_kernel, outer_kernel, out_kernel))

    constants = tables()
    sizes = (channels, half, hidden, frames)
    weights = [up_kernel, inner_kernel, outer_kernel.T, out_kernel]
    forward = [
        ((2 * half, 6 * channels), BF16),
        ((2 * hidden, 12 * half), BF16),
        ((2 * half, 6 * hidden), BF16),
        ((8, 6 * half), BF16),
    ]
    own, own_latent, *made = run(
        lambda *refs: own_kernel(sizes, *refs),
        [
            (8 + 4 * blocks, LANES),
            (channels, frames),
            *forward,
            *kept_shapes(channels, half, hidden, window),
        ],
        [latent, target, *weights, constants[0]],
        [
            *[pltpu.VMEM(x.shape, F32) for x in weights],
            pltpu.VMEM(target.shape, F32),
            pltpu.VMEM((BLOCK, BLOCK), BF16),
            pltpu.VMEM((LANES, LANES), F32),
            pltpu.VMEM((8, BLOCK), F32),
            pltpu.SemaphoreType.DMA((7,)),
        ],
        "own_decode",
        8,
        7,
    )
    backward = run(
        lambda *refs: backward_kernel(sizes, *refs),
        [
            ((channels, 12 * half), BF16),
            ((2 * half, 12 * hidden), BF16),
            ((2 * hidden, 6 * half), BF16),
            ((2 * half, 24), BF16),
            constants[1].shape,
            *[(x.shape, BF16) for x in constants[2:]],
        ],
        [*weights, own, *constants[1:]],
        [pltpu.VMEM((LANES, LANES), F32), pltpu.SemaphoreType.DMA((3,))],
        "backward_weights",
        4,
        3,
    )
    pairs = [(i, i ^ 1) for i in range(count) if i ^ 1 < count]
    first = lax.ppermute(own, "tm", pairs)
    pairs = [(i, i + 1 if i % 2 else i - 1) for i in range(count)]
    second = lax.ppermute(own, "tm", [(a, b) for a, b in pairs if 0 <= b < count])

    part = half + hidden // 2
    rows = STREAMS * part

    payload, sent, grads = run(
        lambda *refs: main_kernel(sizes, *refs),
        [*[(rows + 8 + 8 * STREAMS, LANES)] * 2, (STREAMS * channels, frames)],
        [own, first, second, own_latent, *made, *backward],
        [
            pltpu.VMEM((LANES, LANES), F32),
            pltpu.VMEM((8, 4 * half), F32),
            pltpu.VMEM((8 * (blocks + 4), BLOCK), F32),
            pltpu.VMEM((3 * blocks, BLOCK), F32),
            pltpu.VMEM((3 * blocks, BLOCK), F32),
            pltpu.VMEM((2, 8, window), F32),
        ],
        "losses",
        16,
    )

    index = lax.axis_index("tm")
    line = lax.broadcasted_iota(jnp.int32, payload.shape, 0)
    lane = lax.broadcasted_iota(jnp.int32, payload.shape, 1)
    step = 1
    while True:
        theirs = lax.ppermute(sent, "tm", [(i, i ^ step) for i in range(count)])
        if 2 * step == count:
            break
        low = index % step
        swap = ((low == 0) & (lane >= LANES // 2)) | ((low == step - 1) & (lane < LANES // 2))
        payload = jnp.where(
            line < rows + 8, payload + theirs, jnp.where(swap, theirs, payload)
        )
        sent = payload
        step *= 2

    weights, aux = run(
        lambda *refs: combine_kernel((half, hidden, samples), *refs),
        [(part + 8, LANES), (16, LANES)],
        [payload, theirs],
        [],
        "combine",
        2,
    )
    (latent_grad,) = run(
        lambda grads_ref, aux_ref, out, square: latent_kernel(channels, grads_ref, aux_ref, square, out),
        [latent.shape],
        [grads, aux],
        [pltpu.VMEM((LANES, LANES), F32)],
        "latent",
        2,
    )

    count = lax.axis_size("dp")
    step = 1
    while True:
        theirs = lax.ppermute(weights, "dp", [(i, i ^ step) for i in range(count)])
        weights = weights + theirs
        step *= 2
        if step == count:
            break
    count = lax.axis_size("tm")
    theirs = lax.ppermute(weights, "tm", [(i, i ^ 1) for i in range(count)])
    up, inner, outer, out = run(
        lambda *refs: final_kernel((channels, half, hidden, params), *refs),
        [up_kernel.shape, inner_kernel.shape, outer_kernel.shape[::-1], out_kernel.shape],
        [weights, theirs],
        [],
        "final",
        2,
    )
    return (latent_grad, up, inner, outer.T, out)


def solution(mesh):
    for axis in ("dp", "tm"):
        size = mesh.shape[axis]
        assert size > 1 and size & (size - 1) == 0
    placed = (P("dp", None, "tm"), P("dp", "tm"), P(), P(), P(), P())
    return jax.shard_map(
        local,
        mesh=mesh,
        in_specs=placed,
        out_specs=(P("dp", None, "tm"), P(), P(), P(), P()),
        check_vma=False,
    )
```

```python
import jax
import jax.numpy as jnp
import numpy as np
from jax import lax
from jax.experimental import pallas as pl
from jax.experimental.pallas import tpu as pltpu
from jax.sharding import PartitionSpec as P

MELS = 64
WIN_COARSE = 1024
WIN_FINE = 256
LOSS_WEIGHTS = (0.25, 0.5, 0.5)
LANES = 128
BLOCK = 2 * LANES
STREAMS = 3
REACH = 3
MARGIN = LANES // 2
F32 = jnp.float32
BF16 = jnp.bfloat16
VMEM = pltpu.MemorySpace.VMEM


def hi_lo(table):
    high = table.astype(np.float32).astype(BF16)
    low = (table - high.astype(np.float64)).astype(np.float32).astype(BF16)
    return high, low


def mel_table(window):
    half = window // 2
    top = 2595.0 * np.log10(1.0 + 12000.0 / 700.0)
    points = (np.arange(MELS + 1) + 1.0) / (MELS + 2.0) * top
    centers = 700.0 * (10.0 ** (points / 2595.0) - 1.0) / 12000.0 * half
    spacing = np.maximum(centers[1:] - centers[:-1], 1.0)
    places = np.arange(half)[:, None]
    return np.maximum(0.0, 1.0 - np.abs(places - centers[None, :MELS]) / spacing[None, :])


def tables():
    order = np.concatenate([np.arange(0, BLOCK, 2), np.arange(1, BLOCK, 2)])
    angle = 2.0 * np.pi / BLOCK * ((order[:, None] * np.arange(LANES)[None, :]) % BLOCK)
    turns = np.concatenate([np.cos(angle), -np.sin(angle)], 1)
    coarse_mel = mel_table(WIN_COARSE)
    coarse_mel = np.concatenate([coarse_mel[rho::4] for rho in range(4)], 0)
    fine_mel = mel_table(WIN_FINE)
    hann = 0.5 - 0.5 * np.cos(2.0 * np.pi / WIN_COARSE * np.arange(WIN_COARSE))
    twist = 2.0 * np.pi / WIN_COARSE * np.arange(1, 4)[:, None] * order[None, :]
    taper = 0.5 - 0.5 * np.cos(2.0 * np.pi / WIN_FINE * order)[None, :]
    lines = [hann.reshape(4, BLOCK)[:, order], np.cos(twist), np.sin(twist), taper]
    lines = np.concatenate(lines + [np.zeros((5, BLOCK))], 0).astype(np.float32)
    deal = np.zeros((BLOCK, BLOCK), np.float32)
    deal[order, np.arange(BLOCK)] = 1.0
    banks = [np.concatenate(hi_lo(x), 1) for x in (coarse_mel, fine_mel)]
    return lines, np.concatenate(hi_lo(turns), 0), np.concatenate(banks, 0), deal.astype(BF16)


def split(x):
    high = x.astype(BF16)
    return high, (x - high.astype(F32)).astype(BF16)


def stacked(x):
    high = x.astype(BF16).astype(F32)
    return jnp.concatenate([high, x - high], axis=0).astype(BF16)


def dot(left, right, transposed=False):
    dims = (((1,), (1 if transposed else 0,)), ((), ()))
    return lax.dot_general(left, right, dims, preferred_element_type=F32)


def dot3(left, right_high, right_low, transposed=False):
    rows = left.shape[0]
    both = stacked(left)
    first = dot(both, right_high, transposed)
    second = dot(left.astype(BF16), right_low, transposed)
    return first[:rows] + first[rows:] + second


def to_mel(energy, bank):
    rows = energy.shape[0]
    both = dot(stacked(energy), bank)
    both = both[:rows] + both[rows:]
    return both[:, :MELS] + both[:, MELS:]


def from_mel(push, bank):
    rows = push.shape[0]
    both = dot(stacked(jnp.concatenate([push, push], axis=1)), bank, True)
    return both[:rows] + both[rows:]


def three_wide(weight):
    high = weight.astype(BF16).astype(F32)
    return jnp.concatenate([high, weight - high, high], axis=1).astype(BF16)


def apply(weight3, pair):
    high, low = pair
    return dot(weight3, jnp.concatenate([high, high, low], axis=0))


def elu_pair(x):
    slope = jnp.exp(jnp.minimum(x, 0.0))
    return jnp.where(x > 0, x, slope - 1.0), slope


def moved(x, by):
    return pltpu.roll(x, by % x.shape[1], 1)


def decode(sizes, weights, latent, keep, mask):
    half = sizes[1]
    activated, slope = elu_pair(latent)
    keep("slope_a", slope)
    both = jnp.concatenate([activated, moved(activated, 1)], 0)
    pair = split(both)
    keep("a", pair)
    upper = apply(weights["up"], pair) * mask
    rect, slope = elu_pair(upper)
    keep("slope_u", slope)
    pair = split(
        jnp.concatenate([moved(rect[half:], 1), rect, moved(rect[:half], -1)], 0)
    )
    keep("e", pair)
    hid, slope = elu_pair(apply(weights["inner"], pair))
    keep("slope_c", slope)
    pair = split(hid)
    keep("h", pair)
    mixed = (upper + apply(weights["outer"], pair)) * mask
    rect, slope = elu_pair(mixed)
    keep("slope_m", slope)
    pair = split(rect)
    keep("g", pair)
    taps = apply(weights["out"], pair)
    plus1, plus2, minus1, minus2 = (moved(taps, by) for by in (1, 2, -1, -2))
    return (
        (plus2[0:1] + plus1[2:3] + taps[4:5] + minus1[6:7]) * mask,
        (plus1[1:2] + taps[3:4] + minus1[5:6] + minus2[7:8]) * mask,
    )


KEPT = ("slope_a", "a_h", "a_l", "slope_u", "e_h", "e_l", "slope_c", "h_h", "h_l", "slope_m", "g_h", "g_l")


def kept_shapes(channels, half, hidden, window):
    rows = (channels, 2 * channels, 2 * half, 4 * half, 2 * hidden, 2 * hidden, 2 * half, 2 * half)
    shapes = []
    for i in range(4):
        shapes.append(((rows[2 * i], window), F32))
        shapes += [((rows[2 * i + 1], window), BF16)] * 2
    return shapes


def forward_weights(sizes, up, inner, outer, out, square):
    channels, half, hidden, _ = sizes
    weights = {}
    weights["up"] = three_wide(
        jnp.concatenate(
            [jnp.concatenate([up[r], up[r + 2]], axis=1) for r in range(2)], axis=0
        )
    )
    square[...] = jnp.zeros_like(square)
    for j in range(3):
        square[0:hidden, j * half : (j + 1) * half] = inner[j]
        square[hidden : 2 * hidden, (j + 1) * half : (j + 2) * half] = inner[j]
    weights["inner"] = three_wide(square[0 : 2 * hidden, :])
    square[...] = jnp.zeros_like(square)
    square[0:hidden, 0:half] = outer[...]
    square[hidden : 2 * hidden, half : 2 * half] = outer[...]
    weights["outer"] = three_wide(jnp.transpose(square[...])[0 : 2 * half, 0 : 2 * hidden])
    square[...] = jnp.zeros_like(square)
    square[1:8, 0:half] = out[...]
    square[0:7, half : 2 * half] = out[...]
    weights["out"] = three_wide(square[0:8, 0 : 2 * half])
    return weights


FORWARD = ("up", "inner", "outer", "out")


def backward_kernel(sizes, *refs):
    up, inner, outer, out = refs[:4]
    up_ref, inner_ref, outer_ref, out_ref = refs[9:13]
    square, sems = refs[17:]
    copies = [pltpu.make_async_copy(refs[5 + i], refs[13 + i], sems.at[i]) for i in range(4)]
    for copy in copies:
        copy.start()
    channels, half, hidden, _ = sizes
    for r in range(4):
        square[r * half : (r + 1) * half, 0:channels] = up[r]
        square[r * half : (r + 1) * half, channels:] = up[r]
    up_ref[...] = three_wide(jnp.transpose(square[...])[0:channels, :])
    square[...] = jnp.zeros_like(square)
    for j in range(3):
        square[(2 - j) * hidden : (3 - j) * hidden, 0:half] = inner[j]
        square[(3 - j) * hidden : (4 - j) * hidden, half : 2 * half] = inner[j]
    inner_ref[...] = three_wide(jnp.transpose(square[...])[0 : 2 * half, 0 : 4 * hidden])
    square[...] = jnp.zeros_like(square)
    square[0:hidden, 0:half] = outer[...]
    square[hidden : 2 * hidden, half : 2 * half] = outer[...]
    outer_ref[...] = three_wide(square[0 : 2 * hidden, 0 : 2 * half])
    square[...] = jnp.zeros_like(square)
    square[1:8, 0:half] = out[...]
    square[0:7, half : 2 * half] = out[...]
    out_ref[...] = three_wide(jnp.transpose(square[...])[0 : 2 * half, 0:8])
    for copy in copies:
        copy.wait()


def own_kernel(sizes, *refs):
    sources = refs[:6]
    packet_ref, latent_ref = refs[6:8]
    weight_refs = refs[8:12]
    kept = dict(zip(KEPT, refs[12:24]))
    up_ref, inner_ref, outer_ref, out_ref, target_ref, square, sems = refs[24:]
    channels, half, hidden, frames = sizes
    spaces = (latent_ref, target_ref, up_ref, inner_ref, outer_ref, out_ref)
    copies = []
    for i, (source, space) in enumerate(zip(sources, spaces)):
        if i == 0:
            source = source.at[0]
        copies.append(pltpu.make_async_copy(source, space, sems.at[i]))
    for copy in copies:
        copy.start()
    for copy in copies:
        copy.wait()
    weights = forward_weights(sizes, up_ref, inner_ref, outer_ref, out_ref, square)
    for name, ref in zip(FORWARD, weight_refs):
        ref[...] = weights[name]

    def keep(name, value):
        if isinstance(value, tuple):
            kept[name + "_h"][...], kept[name + "_l"][...] = value
        else:
            kept[name][...] = value

    latent = latent_ref[...]
    spread = moved(jnp.concatenate([latent, jnp.zeros((channels, LANES), F32)], 1), MARGIN)
    wave = jnp.concatenate(decode(sizes, weights, spread, keep, 1.0), 0)
    wave = moved(wave, -MARGIN)
    blocks = frames // LANES
    packet_ref[0:8, 0:channels] = jnp.transpose(latent[:, 0:LANES])[0:8]
    packet_ref[0:8, channels:] = jnp.transpose(latent[:, frames - LANES :])[LANES - 8 :]
    for r in range(2):
        for b in range(blocks):
            packet_ref[8 + r * blocks + b : 9 + r * blocks + b, :] = wave[
                r : r + 1, b * LANES : (b + 1) * LANES
            ]
    for row in range(2 * blocks):
        at = 8 + 2 * blocks + row
        packet_ref[at : at + 1, :] = target_ref[:, row * LANES : (row + 1) * LANES]


def main_kernel(sizes, *refs):
    own_ref, first_ref, second_ref, latent_ref = refs[:4]
    weights = {name: ref[...] for name, ref in zip(FORWARD, refs[4:8])}
    kept = dict(zip(KEPT, refs[8:20]))
    up_back, back_inner, outer_back, out_back = (ref[...] for ref in refs[20:24])
    lines_ref, turns_ref, bank_ref, deal_ref = refs[24:28]
    keep_ref, send_ref, upper_ref, slope_ref = refs[28:32]
    (square, wblock, shifted, wave_b, targ_b, lanes_b) = refs[32:38]
    channels, half, hidden, frames = sizes
    window = frames + LANES
    own_blocks = frames // LANES
    index = lax.axis_index("tm")
    count = lax.axis_size("tm")
    odd_place = lax.rem(index, 2) == 1

    first, second = first_ref[...], second_ref[...]
    left = jnp.where(odd_place, first, second)
    right = jnp.where(odd_place, second, first)
    for side, packet in enumerate((left, own_ref[...], right)):
        rows = slice(side * own_blocks, (side + 1) * own_blocks)
        for r in range(2):
            columns = slice(r * LANES, (r + 1) * LANES)
            at = 8 + r * own_blocks
            wave_b[rows, columns] = packet[at : at + own_blocks]
            for b in range(own_blocks):
                at = 8 + 2 * own_blocks + 2 * b + r
                row = side * own_blocks + b
                targ_b[row : row + 1, columns] = packet[at : at + 1]
    whole = targ_b[...]
    high = whole.astype(BF16).astype(F32)
    middle = (whole - high).astype(BF16).astype(F32)
    dealt = dot(
        jnp.concatenate([high, middle, whole - high - middle], axis=0).astype(BF16), deal_ref[...]
    )
    size = targ_b.shape[0]
    targ_b[...] = dealt[:size] + dealt[size : 2 * size] + dealt[2 * size :]
    square[...] = jnp.zeros_like(square)
    square[MARGIN - 8 : MARGIN, 0:channels] = left[0:8, channels:]
    square[MARGIN : MARGIN + 8, channels:] = right[0:8, 0:channels]
    turned = jnp.transpose(square[...])
    lane = lax.broadcasted_iota(jnp.int32, (1, LANES), 1)
    ends = jnp.concatenate(
        [
            jnp.where(lane < MARGIN, turned[0:channels], moved(latent_ref[:, 0:LANES], MARGIN)),
            jnp.where(
                lane < MARGIN, moved(latent_ref[:, frames - LANES :], MARGIN), turned[channels:]
            ),
        ],
        axis=1,
    )
    place = lax.broadcasted_iota(jnp.int32, (1, window), 1) + index * frames - MARGIN
    mask = ((place >= 0) & (place < count * frames)).astype(F32)
    ends_mask = jnp.concatenate([mask[:, :LANES], mask[:, window - LANES :]], axis=1)
    saved = {}

    def joined(name, value):
        inside = kept[name]
        quarter = LANES // 4
        lane = lax.broadcasted_iota(jnp.int32, (value.shape[0], LANES), 1)
        head = jnp.where(lane < 3 * quarter, value[:, :LANES], inside[:, :LANES])
        tail = jnp.where(lane >= quarter, value[:, LANES:], inside[:, window - LANES :])
        saved[name] = jnp.concatenate([head, inside[:, LANES : window - LANES], tail], axis=1)

    def keep(name, value):
        if isinstance(value, tuple):
            joined(name + "_h", value[0])
            joined(name + "_l", value[1])
        else:
            joined(name, value)

    ends_wave = decode(sizes, weights, ends, keep, ends_mask)
    slope_a, slope_u, slope_c, slope_m = (saved["slope_" + x] for x in "aucm")

    for r in range(2):
        columns = slice(r * LANES, (r + 1) * LANES)
        for side in range(2):
            piece = moved(ends_wave[r][:, side * LANES : (side + 1) * LANES], MARGIN)
            row = own_blocks * (1 + side)
            wave_b[row - 1 : row, columns] = jnp.where(
                lane >= LANES - 4, piece, wave_b[row - 1 : row, columns]
            )
            wave_b[row : row + 1, columns] = jnp.where(lane < 4, piece, wave_b[row : row + 1, columns])
    turns_h, turns_l = turns_ref[0:BLOCK], turns_ref[BLOCK:]
    coarse_bank, fine_bank = bank_ref[0 : 2 * BLOCK], bank_ref[2 * BLOCK :]
    line = [lines_ref[i : i + 1, :] for i in range(11)]
    hann, cos, sin, taper = line[0:4], line[4:7], line[7:10], line[10]

    row_count = own_blocks + 4
    start = own_blocks - 3
    parts = []
    for j in range(4):
        rows = jnp.concatenate(
            [wave_b[pl.ds(start + j, row_count), :], targ_b[pl.ds(start + j, row_count), :]], 0
        )
        parts.append(rows * hann[j])
    even_sum, odd_sum = parts[0] + parts[2], parts[1] + parts[3]
    pair0, pair1 = even_sum + odd_sum, even_sum - odd_sum
    part0, part1 = parts[0] - parts[2], parts[1] - parts[3]
    blocks_in = [
        pair0,
        part0 * cos[0] - part1 * sin[0],
        -part1 * cos[0] - part0 * sin[0],
        pair1 * cos[1],
        -pair1 * sin[1],
        part0 * cos[2] + part1 * sin[2],
        part1 * cos[2] - part0 * sin[2],
    ]

    hop = LANES // 4
    lane = lax.broadcasted_iota(jnp.int32, (1, LANES), 1)
    start_fine = own_blocks - 1
    for which, source in enumerate((wave_b, targ_b)):
        for s in range(4):
            base = (which * 4 + s) * row_count
            for r in range(2):
                here = source[pl.ds(start_fine, row_count), r * LANES : (r + 1) * LANES]
                if s:
                    there = source[pl.ds(start_fine + 1, row_count), r * LANES : (r + 1) * LANES]
                    here = jnp.where(
                        lane < LANES - s * hop,
                        pltpu.roll(here, LANES - s * hop, 1),
                        pltpu.roll(there, LANES - s * hop, 1),
                    )
                shifted[base : base + row_count, r * LANES : (r + 1) * LANES] = here
    spec = dot3(jnp.concatenate([*blocks_in, shifted[...] * taper], axis=0), turns_h, turns_l)
    rows = 2 * row_count
    bins = [spec[i * rows : (i + 1) * rows] for i in range(7)]
    real, imag = [bins[0][:, :LANES]], [bins[0][:, LANES:]]
    for first_bin, second_bin in (bins[1:3], bins[3:5], bins[5:7]):
        real.append(first_bin[:, :LANES] - second_bin[:, LANES:])
        imag.append(first_bin[:, LANES:] + second_bin[:, :LANES])
    real, imag = jnp.concatenate(real, axis=1), jnp.concatenate(imag, axis=1)
    spec_fine = spec[7 * rows :]
    real_fine, imag_fine = spec_fine[:, :LANES], spec_fine[:, LANES:]
    mel_fine = to_mel(real_fine * real_fine + imag_fine * imag_fine, fine_bank)
    level_fine = jnp.sqrt(mel_fine + 1.0)
    fine_rows = 4 * row_count
    level_wave_fine = level_fine[:fine_rows]
    row_fine = lax.broadcasted_iota(jnp.int32, (fine_rows, MELS), 0)
    frame_fine = (lax.rem(row_fine, row_count) - 1 + index * own_blocks) * 4 + row_fine // row_count
    slope_fine = jnp.where(frame_fine >= 0, (level_wave_fine - level_fine[fine_rows:]) / level_wave_fine, 0.0)
    mel = to_mel(real * real + imag * imag, coarse_bank)
    level = jnp.sqrt(mel + 1.0)
    level_wave = level[:row_count]
    frame = lax.broadcasted_iota(jnp.int32, (row_count, MELS), 0) + index * own_blocks - 3
    slope = jnp.where(frame >= 0, (level_wave - level[row_count:]) / level_wave, 0.0)
    push_fine = 2.0 * from_mel(slope_fine, fine_bank)
    push = 2.0 * from_mel(slope, coarse_bank)
    real, imag = real[:row_count] * push, imag[:row_count] * push
    wide = []
    for rho in range(4):
        columns = slice(rho * LANES, (rho + 1) * LANES)
        first_bin, second_bin = real[:, columns], imag[:, columns]
        wide.append(jnp.concatenate([first_bin, second_bin], axis=1))
        if rho:
            wide.append(jnp.concatenate([second_bin, -first_bin], axis=1))
    wide.append(
        jnp.concatenate([real_fine[:fine_rows] * push_fine, imag_fine[:fine_rows] * push_fine], 1)
    )
    back = dot3(jnp.concatenate(wide, axis=0), turns_h, turns_l, True)
    back_fine = back[7 * row_count :] * taper
    back = [back[i * row_count : (i + 1) * row_count] for i in range(7)]
    back0, back2 = back[0], back[3] * cos[1] - back[4] * sin[1]
    back1 = [
        back[1] * cos[0] - back[2] * sin[0] + back[5] * cos[2] - back[6] * sin[2],
        back[5] * sin[2] + back[6] * cos[2] - back[1] * sin[0] - back[2] * cos[0],
    ]
    fine = []
    for r in range(2):
        total = jnp.zeros((own_blocks, LANES), F32)
        for s in range(4):
            piece = back_fine[s * row_count : (s + 1) * row_count, r * LANES : (r + 1) * LANES]
            if s:
                piece = pltpu.roll(piece, s * hop, 1)
                total = total + jnp.where(
                    lane >= s * hop, piece[1 : 1 + own_blocks], piece[0:own_blocks]
                )
            else:
                total = total + piece[1 : 1 + own_blocks]
        fine.append(total)
    fine = jnp.concatenate(fine, axis=1)

    plus, minus = back0 + back2, back0 - back2
    backs = [
        plus + back1[0],
        minus + back1[1],
        plus - back1[0],
        minus - back1[1],
    ]
    coarse = jnp.zeros((own_blocks, BLOCK), F32)
    for j in range(4):
        coarse = coarse + (backs[j] * hann[j])[3 - j : 3 - j + own_blocks]

    own_rows = pl.ds(own_blocks, own_blocks)
    timed = 2.0 * (wave_b[own_rows, :] - targ_b[own_rows, :])

    streams = (timed, coarse, fine)
    totals = [jnp.sum(stream * stream) for stream in streams]
    lanes_b[...] = jnp.zeros_like(lanes_b)
    for i, stream in enumerate(streams):
        for b in range(own_blocks):
            for r in range(2):
                lanes_b[r, i : i + 1, b * LANES : (b + 1) * LANES] = stream[
                    b : b + 1, r * LANES : (r + 1) * LANES
                ]
    evens, odds = lanes_b[0], lanes_b[1]
    shifted_rows = [moved(odds if k % 2 else evens, MARGIN - (4 - k) // 2) for k in range(8)]
    views = [
        jnp.concatenate([shifted_rows[k][i : i + 1] for k in range(8)], axis=0) for i in range(STREAMS)
    ]
    threes = []
    for view in views:
        high = view.astype(BF16).astype(F32)
        threes.append(jnp.concatenate([high, high, view - high], axis=0).astype(BF16))
    slope_m, slope_u = slope_m * mask, slope_u * mask
    slope_a = slope_a * mask
    grad_mixed = [dot(out_back, three) * slope_m for three in threes]
    mixeds = [split(x) for x in grad_mixed]
    grad_inner = [apply(outer_back, pair) * slope_c for pair in mixeds]
    inners = [split(x) for x in grad_inner]
    spreads = [
        split(jnp.concatenate([moved(x[hidden:], 1), x, moved(x[:hidden], -1)], 0)) for x in grad_inner
    ]
    grad_upper = [
        x + apply(back_inner, pair) * slope_u for x, pair in zip(grad_mixed, spreads)
    ]
    uppers = [split(x) for x in grad_upper]
    low = lane < MARGIN
    slope_edge = jnp.where(low, slope_a[:, :LANES], slope_a[:, frames:])
    edges = []
    for i, value in enumerate(grad_upper):
        upper_ref[i * 2 * half : (i + 1) * 2 * half, :] = value
        head, tail = value[:, :LANES], value[:, frames:]
        both = jnp.concatenate(
            [jnp.where(low, head, tail), jnp.where(low, moved(head, -1), moved(tail, -1))], 0
        )
        turned = jnp.transpose(apply(up_back, split(both)) * slope_edge)
        edges.append(
            jnp.concatenate([turned[MARGIN - REACH : MARGIN], turned[MARGIN : MARGIN + REACH]], axis=1)
        )
    slope_ref[...] = slope_a

    def against(highs, lows, name):
        high, low = saved[name + "_h"], saved[name + "_l"]
        count = high.shape[0]
        wide = dot(highs, jnp.concatenate([high, low], axis=0), True)
        return wide[:, :count] + wide[:, count:] + dot(lows, high, True)

    def summed(pairs, name):
        rows = pairs[0][0].shape[0]
        highs, lows = (jnp.concatenate([pair[i] for pair in pairs], axis=0) for i in range(2))
        value = against(highs, lows, name)
        return [value[i * rows : (i + 1) * rows] for i in range(STREAMS)]

    def put(value, at, columns):
        rows = value.shape[0] // 2
        low, high = value[:rows], value[rows:]
        keep_ref[at : at + rows, columns] = jnp.where(odd_place, high, low)
        send_ref[at : at + rows, columns] = jnp.where(odd_place, low, high)

    step = half + hidden // 2
    for i, value in enumerate(summed(uppers, "a")):
        put(value, i * step, slice(0, 2 * channels))
    for i, value in enumerate(summed(inners, "e")):
        put(value[:hidden, : 3 * half] + value[hidden:, half:], i * step + half, slice(0, 3 * half))
    highs = jnp.concatenate([pair[0] for pair in mixeds], axis=0)
    lows = jnp.concatenate([pair[1] for pair in mixeds], axis=0)
    both = jnp.concatenate([saved["h_h"], saved["h_l"]], axis=0)
    first = dot(both, highs, True)
    value = first[: 2 * hidden] + first[2 * hidden :] + dot(saved["h_h"], lows, True)
    for i in range(STREAMS):
        columns = i * 2 * half
        put(
            value[:hidden, columns : columns + half]
            + value[hidden:, columns + half : columns + 2 * half],
            i * step + half,
            slice(3 * half, 4 * half),
        )
    taps = against(*split(jnp.concatenate(views, axis=0)), "g")
    for i in range(STREAMS):
        wblock[0:7, i * half : (i + 1) * half] = (
            taps[8 * i + 1 : 8 * i + 8, :half] + taps[8 * i : 8 * i + 7, half:]
        )
    lane = lax.broadcasted_iota(jnp.int32, (1, half), 1)
    sums = jnp.where(lane == 0, totals[0], jnp.where(lane == 1, totals[1], totals[2]))
    wblock[7:8, :] = jnp.zeros((1, 4 * half), F32)
    wblock[0:7, STREAMS * half :] = jnp.zeros((7, half), F32)
    wblock[7:8, STREAMS * half :] = sums
    edges = jnp.concatenate(edges, axis=0)
    for ref in (keep_ref, send_ref):
        ref[STREAMS * step : STREAMS * step + 8, :] = wblock[...]
        ref[STREAMS * step + 8 :, :] = edges


def combine_kernel(sizes, mine_ref, theirs_ref, weights_ref, aux_ref):
    half, hidden, samples = sizes
    step = half + hidden // 2
    rows = STREAMS * step
    total = mine_ref[0 : rows + 8, :] + theirs_ref[0 : rows + 8, :]
    line = total[rows + 7 : rows + 8, :]
    lane = lax.broadcasted_iota(jnp.int32, line.shape, 1) - STREAMS * half
    wanted = jnp.where(lane == 0, LOSS_WEIGHTS[0], jnp.where(lane == 1, LOSS_WEIGHTS[1], LOSS_WEIGHTS[2]))
    line = wanted / jnp.sqrt(line / samples + 1e-06)
    scale = [
        jnp.sum(jnp.where(lane == i, line, 0.0), axis=1, keepdims=True) for i in range(STREAMS)
    ]
    weights_ref[0:step, :] = sum(total[i * step : (i + 1) * step] * scale[i] for i in range(STREAMS))
    last = total[rows : rows + 8]
    out = sum(
        (pltpu.roll(last, (4 - i) * half % (4 * half), 1) if i else last) * scale[i]
        for i in range(STREAMS)
    )
    place = lax.broadcasted_iota(jnp.int32, out.shape, 0)
    lane = lax.broadcasted_iota(jnp.int32, out.shape, 1)
    weights_ref[step:, :] = jnp.where((place < 7) & (lane < half), out, 0.0)
    index = lax.axis_index("tm")
    step = lax.axis_size("tm") // 2
    low = lax.rem(index, step)
    edge_lane = lax.broadcasted_iota(jnp.int32, (1, LANES), 1)
    swap = ((low == 0) & (edge_lane >= LANES // 2)) | ((low == step - 1) & (edge_lane < LANES // 2))
    edges = jnp.where(swap, theirs_ref[rows + 8 :, :], mine_ref[rows + 8 :, :])
    aux_ref[0:REACH, :] = sum(edges[REACH * i : REACH * (i + 1)] * scale[i] for i in range(STREAMS))
    for i in range(STREAMS):
        aux_ref[8 + i : 9 + i, :] = jnp.broadcast_to(scale[i], (1, LANES))


def latent_kernel(channels, upper_ref, slope_ref, weight_ref, aux_ref, grad_ref, square):
    frames = grad_ref.shape[2]
    rows = upper_ref.shape[0] // STREAMS
    upper = sum(
        upper_ref[i * rows : (i + 1) * rows, :] * aux_ref[8 + i : 9 + i, 0:1] for i in range(STREAMS)
    )
    both = split(jnp.concatenate([upper, moved(upper, -1)], 0))
    grads = moved(apply(weight_ref[...], both) * slope_ref[...], -MARGIN)[:, :frames]
    square[...] = jnp.zeros_like(square)
    square[0:REACH, 0:channels] = aux_ref[0:REACH, channels:]
    square[LANES - REACH :, channels:] = aux_ref[0:REACH, 0:channels]
    turned = jnp.transpose(square[...])
    grad_ref[0, :, 0:LANES] = grads[:, :LANES] + turned[0:channels]
    grad_ref[0, :, LANES : frames - LANES] = grads[:, LANES : frames - LANES]
    grad_ref[0, :, frames - LANES :] = grads[:, frames - LANES :] + turned[channels:]


def final_kernel(sizes, mine_ref, theirs_ref, up_ref, inner_ref, outer_ref, out_ref):
    channels, half, hidden, params = sizes
    step = half + hidden // 2
    mine, theirs = mine_ref[...], theirs_ref[...]
    odd_place = lax.rem(lax.axis_index("tm"), 2) == 1
    low = jnp.where(odd_place, theirs[:step], mine[:step])
    high = jnp.where(odd_place, mine[:step], theirs[:step])
    out = mine[step:]
    squares = jnp.sum(low * low) + jnp.sum(high * high) + jnp.sum(out * out)
    factor = jnp.minimum(1.0, 1.0 / jnp.sqrt(jnp.full((1, 1), squares / params + 1e-06, F32)))
    low, high = low * factor, high * factor
    for r, part in enumerate((low, high)):
        up_ref[r] = part[0:half, 0:channels]
        up_ref[r + 2] = part[0:half, channels:]
    inner = jnp.concatenate([low[half:], high[half:]], axis=0)
    for j in range(3):
        inner_ref[j] = inner[:, j * half : (j + 1) * half]
    outer_ref[...] = inner[:, 3 * half :]
    out_ref[...] = (out * factor)[0:7, 0:half]


def run(kernel, out_shape, operands, scratch, name, mebibytes, left=0):
    spec = pl.BlockSpec(memory_space=VMEM)
    kept = len(operands) - left
    hbm = [pltpu.with_memory_space_constraint(x, pltpu.MemorySpace.HBM) for x in operands[kept:]]
    operands = [*operands[:kept], *hbm]
    stay = pl.BlockSpec(memory_space=pltpu.MemorySpace.HBM)
    return pl.pallas_call(
        kernel,
        out_shape=tuple(
            jax.ShapeDtypeStruct(*(x if isinstance(x[1], type) else (x, F32))) for x in out_shape
        ),
        in_specs=[spec] * (len(operands) - left) + [stay] * left,
        out_specs=tuple([spec] * len(out_shape)),
        scratch_shapes=scratch,
        compiler_params=pltpu.CompilerParams(vmem_limit_bytes=mebibytes << 20),
        name=name,
    )(*operands)


def local(latent, target, up_kernel, inner_kernel, outer_kernel, out_kernel):
    assert latent.shape[0] == 1
    channels, frames = latent.shape[1:]
    half, hidden = outer_kernel.shape
    window = frames + LANES
    blocks = frames // LANES
    count = lax.axis_size("tm")
    samples = target.shape[1] * count
    params = sum(x.size for x in (up_kernel, inner_kernel, outer_kernel, out_kernel))

    constants = tables()
    sizes = (channels, half, hidden, frames)
    weights = [up_kernel, inner_kernel, outer_kernel.T, out_kernel]
    forward = [
        ((2 * half, 6 * channels), BF16),
        ((2 * hidden, 12 * half), BF16),
        ((2 * half, 6 * hidden), BF16),
        ((8, 6 * half), BF16),
    ]
    own, own_latent, *made = run(
        lambda *refs: own_kernel(sizes, *refs),
        [
            (8 + 4 * blocks, LANES),
            (channels, frames),
            *forward,
            *kept_shapes(channels, half, hidden, window),
        ],
        [latent, target, *weights],
        [
            *[pltpu.VMEM(x.shape, F32) for x in weights],
            pltpu.VMEM(target.shape, F32),
            pltpu.VMEM((LANES, LANES), F32),
            pltpu.SemaphoreType.DMA((6,)),
        ],
        "own_decode",
        8,
        6,
    )
    backward = run(
        lambda *refs: backward_kernel(sizes, *refs),
        [
            ((channels, 12 * half), BF16),
            ((2 * half, 12 * hidden), BF16),
            ((2 * hidden, 6 * half), BF16),
            ((2 * half, 24), BF16),
            constants[0].shape,
            *[(x.shape, BF16) for x in constants[1:]],
        ],
        [*weights, own, *constants],
        [pltpu.VMEM((LANES, LANES), F32), pltpu.SemaphoreType.DMA((4,))],
        "backward_weights",
        4,
        4,
    )
    pairs = [(i, i ^ 1) for i in range(count) if i ^ 1 < count]
    first = lax.ppermute(own, "tm", pairs)
    pairs = [(i, i + 1 if i % 2 else i - 1) for i in range(count)]
    second = lax.ppermute(own, "tm", [(a, b) for a, b in pairs if 0 <= b < count])

    part = half + hidden // 2
    rows = STREAMS * part

    payload, sent, upper, slope = run(
        lambda *refs: main_kernel(sizes, *refs),
        [
            *[(rows + 8 + REACH * STREAMS, LANES)] * 2,
            (STREAMS * 2 * half, window),
            (channels, window),
        ],
        [own, first, second, own_latent, *made, *backward],
        [
            pltpu.VMEM((LANES, LANES), F32),
            pltpu.VMEM((8, 4 * half), F32),
            pltpu.VMEM((8 * (blocks + 4), BLOCK), F32),
            pltpu.VMEM((3 * blocks, BLOCK), F32),
            pltpu.VMEM((3 * blocks, BLOCK), F32),
            pltpu.VMEM((2, 8, window), F32),
        ],
        "losses",
        16,
    )

    index = lax.axis_index("tm")
    line = lax.broadcasted_iota(jnp.int32, payload.shape, 0)
    lane = lax.broadcasted_iota(jnp.int32, payload.shape, 1)
    step = 1
    while True:
        theirs = lax.ppermute(sent, "tm", [(i, i ^ step) for i in range(count)])
        if 2 * step == count:
            break
        low = index % step
        swap = ((low == 0) & (lane >= LANES // 2)) | ((low == step - 1) & (lane < LANES // 2))
        payload = jnp.where(
            line < rows + 8, payload + theirs, jnp.where(swap, theirs, payload)
        )
        sent = payload
        step *= 2

    weights, aux = run(
        lambda *refs: combine_kernel((half, hidden, samples), *refs),
        [(part + 8, LANES), (16, LANES)],
        [payload, theirs],
        [],
        "combine",
        2,
    )
    (latent_grad,) = run(
        lambda *refs: latent_kernel(channels, *refs),
        [latent.shape],
        [upper, slope, backward[0], aux],
        [pltpu.VMEM((LANES, LANES), F32)],
        "latent",
        4,
    )

    count = lax.axis_size("dp")
    step = 1
    while True:
        theirs = lax.ppermute(weights, "dp", [(i, i ^ step) for i in range(count)])
        weights = weights + theirs
        step *= 2
        if step == count:
            break
    count = lax.axis_size("tm")
    theirs = lax.ppermute(weights, "tm", [(i, i ^ 1) for i in range(count)])
    up, inner, outer, out = run(
        lambda *refs: final_kernel((channels, half, hidden, params), *refs),
        [up_kernel.shape, inner_kernel.shape, outer_kernel.shape[::-1], out_kernel.shape],
        [weights, theirs],
        [],
        "final",
        2,
    )
    return (latent_grad, up, inner, outer.T, out)


def solution(mesh):
    for axis in ("dp", "tm"):
        size = mesh.shape[axis]
        assert size > 1 and size & (size - 1) == 0
    placed = (P("dp", None, "tm"), P("dp", "tm"), P(), P(), P(), P())
    return jax.shard_map(
        local,
        mesh=mesh,
        in_specs=placed,
        out_specs=(P("dp", None, "tm"), P(), P(), P(), P()),
        check_vma=False,
    )
```

```python
import jax
import jax.numpy as jnp
import numpy as np
from jax import lax
from jax.experimental import pallas as pl
from jax.experimental.pallas import tpu as pltpu
from jax.sharding import PartitionSpec as P

MELS = 64
WIN_COARSE = 1024
WIN_FINE = 256
LOSS_WEIGHTS = (0.25, 0.5, 0.5)
LANES = 128
BLOCK = 2 * LANES
STREAMS = 3
REACH = 3
MARGIN = LANES // 2
F32 = jnp.float32
BF16 = jnp.bfloat16
VMEM = pltpu.MemorySpace.VMEM


def hi_lo(table):
    high = table.astype(np.float32).astype(BF16)
    low = (table - high.astype(np.float64)).astype(np.float32).astype(BF16)
    return high, low


def mel_table(window):
    half = window // 2
    top = 2595.0 * np.log10(1.0 + 12000.0 / 700.0)
    points = (np.arange(MELS + 1) + 1.0) / (MELS + 2.0) * top
    centers = 700.0 * (10.0 ** (points / 2595.0) - 1.0) / 12000.0 * half
    spacing = np.maximum(centers[1:] - centers[:-1], 1.0)
    places = np.arange(half)[:, None]
    return np.maximum(0.0, 1.0 - np.abs(places - centers[None, :MELS]) / spacing[None, :])


def tables():
    order = np.concatenate([np.arange(0, BLOCK, 2), np.arange(1, BLOCK, 2)])
    angle = 2.0 * np.pi / BLOCK * ((order[:, None] * np.arange(LANES)[None, :]) % BLOCK)
    turns = np.concatenate([np.cos(angle), -np.sin(angle)], 1)
    coarse_mel = mel_table(WIN_COARSE)
    coarse_mel = np.concatenate([coarse_mel[rho::4] for rho in range(4)], 0)
    fine_mel = mel_table(WIN_FINE)
    hann = 0.5 - 0.5 * np.cos(2.0 * np.pi / WIN_COARSE * np.arange(WIN_COARSE))
    twist = 2.0 * np.pi / WIN_COARSE * np.arange(1, 4)[:, None] * order[None, :]
    taper = 0.5 - 0.5 * np.cos(2.0 * np.pi / WIN_FINE * order)[None, :]
    lines = [hann.reshape(4, BLOCK)[:, order], np.cos(twist), np.sin(twist), taper]
    lines = np.concatenate(lines + [np.zeros((5, BLOCK))], 0).astype(np.float32)
    deal = np.zeros((BLOCK, BLOCK), np.float32)
    deal[order, np.arange(BLOCK)] = 1.0
    banks = [np.concatenate(hi_lo(x), 1) for x in (coarse_mel, fine_mel)]
    return lines, np.concatenate(hi_lo(turns), 0), np.concatenate(banks, 0), deal.astype(BF16)


def split(x):
    high = x.astype(BF16)
    return high, (x - high.astype(F32)).astype(BF16)


def stacked(x):
    high = x.astype(BF16).astype(F32)
    return jnp.concatenate([high, x - high], axis=0).astype(BF16)


def dot(left, right, transposed=False):
    dims = (((1,), (1 if transposed else 0,)), ((), ()))
    return lax.dot_general(left, right, dims, preferred_element_type=F32)


def dot3(left, right_high, right_low, transposed=False):
    rows = left.shape[0]
    both = stacked(left)
    first = dot(both, right_high, transposed)
    second = dot(left.astype(BF16), right_low, transposed)
    return first[:rows] + first[rows:] + second


def to_mel(energy, bank):
    rows = energy.shape[0]
    both = dot(stacked(energy), bank)
    both = both[:rows] + both[rows:]
    return both[:, :MELS] + both[:, MELS:]


def from_mel(push, bank):
    rows = push.shape[0]
    both = dot(stacked(jnp.concatenate([push, push], axis=1)), bank, True)
    return both[:rows] + both[rows:]


def three_wide(weight):
    high = weight.astype(BF16).astype(F32)
    return jnp.concatenate([high, weight - high, high], axis=1).astype(BF16)


def apply(weight3, pair):
    high, low = pair
    return dot(weight3, jnp.concatenate([high, high, low], axis=0))


def elu_pair(x):
    slope = jnp.exp(jnp.minimum(x, 0.0))
    return jnp.where(x > 0, x, slope - 1.0), slope


def moved(x, by):
    return pltpu.roll(x, by % x.shape[1], 1)


def decode(sizes, weights, latent, keep, mask):
    half = sizes[1]
    activated, slope = elu_pair(latent)
    keep("slope_a", slope)
    both = jnp.concatenate([activated, moved(activated, 1)], 0)
    pair = split(both)
    keep("a", pair)
    upper = apply(weights["up"], pair) * mask
    rect, slope = elu_pair(upper)
    keep("slope_u", slope)
    pair = split(
        jnp.concatenate([moved(rect[half:], 1), rect, moved(rect[:half], -1)], 0)
    )
    keep("e", pair)
    hid, slope = elu_pair(apply(weights["inner"], pair))
    keep("slope_c", slope)
    pair = split(hid)
    keep("h", pair)
    mixed = (upper + apply(weights["outer"], pair)) * mask
    rect, slope = elu_pair(mixed)
    keep("slope_m", slope)
    pair = split(rect)
    keep("g", pair)
    taps = apply(weights["out"], pair)
    plus1, plus2, minus1, minus2 = (moved(taps, by) for by in (1, 2, -1, -2))
    return (
        (plus2[0:1] + plus1[2:3] + taps[4:5] + minus1[6:7]) * mask,
        (plus1[1:2] + taps[3:4] + minus1[5:6] + minus2[7:8]) * mask,
    )


KEPT = ("slope_a", "a_h", "a_l", "slope_u", "e_h", "e_l", "slope_c", "h_h", "h_l", "slope_m", "g_h", "g_l")


def kept_shapes(channels, half, hidden, window):
    rows = (channels, 2 * channels, 2 * half, 4 * half, 2 * hidden, 2 * hidden, 2 * half, 2 * half)
    shapes = []
    for i in range(4):
        shapes.append(((rows[2 * i], window), F32))
        shapes += [((rows[2 * i + 1], window), BF16)] * 2
    return shapes


def forward_weights(sizes, up, inner, outer, out, square):
    channels, half, hidden, _ = sizes
    weights = {}
    weights["up"] = three_wide(
        jnp.concatenate(
            [jnp.concatenate([up[r], up[r + 2]], axis=1) for r in range(2)], axis=0
        )
    )
    square[...] = jnp.zeros_like(square)
    for j in range(3):
        square[0:hidden, j * half : (j + 1) * half] = inner[j]
        square[hidden : 2 * hidden, (j + 1) * half : (j + 2) * half] = inner[j]
    weights["inner"] = three_wide(square[0 : 2 * hidden, :])
    square[...] = jnp.zeros_like(square)
    square[0:hidden, 0:half] = outer[...]
    square[hidden : 2 * hidden, half : 2 * half] = outer[...]
    weights["outer"] = three_wide(jnp.transpose(square[...])[0 : 2 * half, 0 : 2 * hidden])
    square[...] = jnp.zeros_like(square)
    square[1:8, 0:half] = out[...]
    square[0:7, half : 2 * half] = out[...]
    weights["out"] = three_wide(square[0:8, 0 : 2 * half])
    return weights


FORWARD = ("up", "inner", "outer", "out")


def backward_kernel(sizes, *refs):
    up, inner, outer, out = refs[:4]
    up_ref, inner_ref, outer_ref, out_ref = refs[9:13]
    square, sems = refs[17:]
    copies = [pltpu.make_async_copy(refs[5 + i], refs[13 + i], sems.at[i]) for i in range(4)]
    for copy in copies:
        copy.start()
    channels, half, hidden, _ = sizes
    for r in range(4):
        square[r * half : (r + 1) * half, 0:channels] = up[r]
        square[r * half : (r + 1) * half, channels:] = up[r]
    up_ref[...] = three_wide(jnp.transpose(square[...])[0:channels, :])
    square[...] = jnp.zeros_like(square)
    for j in range(3):
        square[(2 - j) * hidden : (3 - j) * hidden, 0:half] = inner[j]
        square[(3 - j) * hidden : (4 - j) * hidden, half : 2 * half] = inner[j]
    inner_ref[...] = three_wide(jnp.transpose(square[...])[0 : 2 * half, 0 : 4 * hidden])
    square[...] = jnp.zeros_like(square)
    square[0:hidden, 0:half] = outer[...]
    square[hidden : 2 * hidden, half : 2 * half] = outer[...]
    outer_ref[...] = three_wide(square[0 : 2 * hidden, 0 : 2 * half])
    square[...] = jnp.zeros_like(square)
    square[1:8, 0:half] = out[...]
    square[0:7, half : 2 * half] = out[...]
    out_ref[...] = three_wide(jnp.transpose(square[...])[0 : 2 * half, 0:8])
    for copy in copies:
        copy.wait()


def own_kernel(sizes, *refs):
    sources = refs[:6]
    packet_ref, latent_ref = refs[6:8]
    weight_refs = refs[8:12]
    kept = dict(zip(KEPT, refs[12:24]))
    up_ref, inner_ref, outer_ref, out_ref, target_ref, square, sems = refs[24:]
    channels, half, hidden, frames = sizes
    spaces = (latent_ref, target_ref, up_ref, inner_ref, outer_ref, out_ref)
    copies = []
    for i, (source, space) in enumerate(zip(sources, spaces)):
        if i == 0:
            source = source.at[0]
        copies.append(pltpu.make_async_copy(source, space, sems.at[i]))
    for copy in copies:
        copy.start()
    for copy in copies:
        copy.wait()
    weights = forward_weights(sizes, up_ref, inner_ref, outer_ref, out_ref, square)
    for name, ref in zip(FORWARD, weight_refs):
        ref[...] = weights[name]

    def keep(name, value):
        if isinstance(value, tuple):
            kept[name + "_h"][...], kept[name + "_l"][...] = value
        else:
            kept[name][...] = value

    latent = latent_ref[...]
    spread = moved(jnp.concatenate([latent, jnp.zeros((channels, LANES), F32)], 1), MARGIN)
    wave = jnp.concatenate(decode(sizes, weights, spread, keep, 1.0), 0)
    wave = moved(wave, -MARGIN)
    blocks = frames // LANES
    packet_ref[0:8, 0:channels] = jnp.transpose(latent[:, 0:LANES])[0:8]
    packet_ref[0:8, channels:] = jnp.transpose(latent[:, frames - LANES :])[LANES - 8 :]
    for r in range(2):
        for b in range(blocks):
            packet_ref[8 + r * blocks + b : 9 + r * blocks + b, :] = wave[
                r : r + 1, b * LANES : (b + 1) * LANES
            ]
    for row in range(2 * blocks):
        at = 8 + 2 * blocks + row
        packet_ref[at : at + 1, :] = target_ref[:, row * LANES : (row + 1) * LANES]


def main_kernel(sizes, *refs):
    own_ref, first_ref, second_ref, latent_ref = refs[:4]
    weights = {name: ref[...] for name, ref in zip(FORWARD, refs[4:8])}
    kept = dict(zip(KEPT, refs[8:20]))
    up_back, back_inner, outer_back, out_back = (ref[...] for ref in refs[20:24])
    lines_ref, turns_ref, bank_ref, deal_ref = refs[24:28]
    keep_ref, send_ref, upper_ref, slope_ref = refs[28:32]
    (square, wblock, shifted, wave_b, targ_b, lanes_b) = refs[32:38]
    channels, half, hidden, frames = sizes
    window = frames + LANES
    own_blocks = frames // LANES
    index = lax.axis_index("tm")
    count = lax.axis_size("tm")
    odd_place = lax.rem(index, 2) == 1

    first, second = first_ref[...], second_ref[...]
    left = jnp.where(odd_place, first, second)
    right = jnp.where(odd_place, second, first)
    for side, packet in enumerate((left, own_ref[...], right)):
        rows = slice(side * own_blocks, (side + 1) * own_blocks)
        for r in range(2):
            columns = slice(r * LANES, (r + 1) * LANES)
            at = 8 + r * own_blocks
            wave_b[rows, columns] = packet[at : at + own_blocks]
            for b in range(own_blocks):
                at = 8 + 2 * own_blocks + 2 * b + r
                row = side * own_blocks + b
                targ_b[row : row + 1, columns] = packet[at : at + 1]
    whole = targ_b[...]
    high = whole.astype(BF16).astype(F32)
    middle = (whole - high).astype(BF16).astype(F32)
    dealt = dot(
        jnp.concatenate([high, middle, whole - high - middle], axis=0).astype(BF16), deal_ref[...]
    )
    size = targ_b.shape[0]
    targ_b[...] = dealt[:size] + dealt[size : 2 * size] + dealt[2 * size :]
    square[...] = jnp.zeros_like(square)
    square[MARGIN - 8 : MARGIN, 0:channels] = left[0:8, channels:]
    square[MARGIN : MARGIN + 8, channels:] = right[0:8, 0:channels]
    turned = jnp.transpose(square[...])
    lane = lax.broadcasted_iota(jnp.int32, (1, LANES), 1)
    ends = jnp.concatenate(
        [
            jnp.where(lane < MARGIN, turned[0:channels], moved(latent_ref[:, 0:LANES], MARGIN)),
            jnp.where(
                lane < MARGIN, moved(latent_ref[:, frames - LANES :], MARGIN), turned[channels:]
            ),
        ],
        axis=1,
    )
    place = lax.broadcasted_iota(jnp.int32, (1, window), 1) + index * frames - MARGIN
    mask = ((place >= 0) & (place < count * frames)).astype(F32)
    ends_mask = jnp.concatenate([mask[:, :LANES], mask[:, window - LANES :]], axis=1)
    saved = {}

    def joined(name, value):
        inside = kept[name]
        quarter = LANES // 4
        lane = lax.broadcasted_iota(jnp.int32, (value.shape[0], LANES), 1)
        head = jnp.where(lane < 3 * quarter, value[:, :LANES], inside[:, :LANES])
        tail = jnp.where(lane >= quarter, value[:, LANES:], inside[:, window - LANES :])
        saved[name] = jnp.concatenate([head, inside[:, LANES : window - LANES], tail], axis=1)

    def keep(name, value):
        if isinstance(value, tuple):
            joined(name + "_h", value[0])
            joined(name + "_l", value[1])
        else:
            joined(name, value)

    ends_wave = decode(sizes, weights, ends, keep, ends_mask)
    slope_a, slope_u, slope_c, slope_m = (saved["slope_" + x] for x in "aucm")

    for r in range(2):
        columns = slice(r * LANES, (r + 1) * LANES)
        for side in range(2):
            piece = moved(ends_wave[r][:, side * LANES : (side + 1) * LANES], MARGIN)
            row = own_blocks * (1 + side)
            wave_b[row - 1 : row, columns] = jnp.where(
                lane >= LANES - 4, piece, wave_b[row - 1 : row, columns]
            )
            wave_b[row : row + 1, columns] = jnp.where(lane < 4, piece, wave_b[row : row + 1, columns])
    turns_h, turns_l = turns_ref[0:BLOCK], turns_ref[BLOCK:]
    coarse_bank, fine_bank = bank_ref[0 : 2 * BLOCK], bank_ref[2 * BLOCK :]
    line = [lines_ref[i : i + 1, :] for i in range(11)]
    hann, cos, sin, taper = line[0:4], line[4:7], line[7:10], line[10]

    row_count = own_blocks + 4
    start = own_blocks - 3
    parts = []
    for j in range(4):
        rows = jnp.concatenate(
            [wave_b[pl.ds(start + j, row_count), :], targ_b[pl.ds(start + j, row_count), :]], 0
        )
        parts.append(rows * hann[j])
    even_sum, odd_sum = parts[0] + parts[2], parts[1] + parts[3]
    pair0, pair1 = even_sum + odd_sum, even_sum - odd_sum
    part0, part1 = parts[0] - parts[2], parts[1] - parts[3]
    blocks_in = [
        pair0,
        part0 * cos[0] - part1 * sin[0],
        -part1 * cos[0] - part0 * sin[0],
        pair1 * cos[1],
        -pair1 * sin[1],
        part0 * cos[2] + part1 * sin[2],
        part1 * cos[2] - part0 * sin[2],
    ]

    hop = LANES // 4
    lane = lax.broadcasted_iota(jnp.int32, (1, LANES), 1)
    start_fine = own_blocks - 1
    for which, source in enumerate((wave_b, targ_b)):
        for s in range(4):
            base = (which * 4 + s) * row_count
            for r in range(2):
                here = source[pl.ds(start_fine, row_count), r * LANES : (r + 1) * LANES]
                if s:
                    there = source[pl.ds(start_fine + 1, row_count), r * LANES : (r + 1) * LANES]
                    here = jnp.where(
                        lane < LANES - s * hop,
                        pltpu.roll(here, LANES - s * hop, 1),
                        pltpu.roll(there, LANES - s * hop, 1),
                    )
                shifted[base : base + row_count, r * LANES : (r + 1) * LANES] = here
    spec = dot3(jnp.concatenate([*blocks_in, shifted[...] * taper], axis=0), turns_h, turns_l)
    rows = 2 * row_count
    bins = [spec[i * rows : (i + 1) * rows] for i in range(7)]
    real, imag = [bins[0][:, :LANES]], [bins[0][:, LANES:]]
    for first_bin, second_bin in (bins[1:3], bins[3:5], bins[5:7]):
        real.append(first_bin[:, :LANES] - second_bin[:, LANES:])
        imag.append(first_bin[:, LANES:] + second_bin[:, :LANES])
    real, imag = jnp.concatenate(real, axis=1), jnp.concatenate(imag, axis=1)
    spec_fine = spec[7 * rows :]
    real_fine, imag_fine = spec_fine[:, :LANES], spec_fine[:, LANES:]
    mel_fine = to_mel(real_fine * real_fine + imag_fine * imag_fine, fine_bank)
    level_fine = jnp.sqrt(mel_fine + 1.0)
    fine_rows = 4 * row_count
    level_wave_fine = level_fine[:fine_rows]
    row_fine = lax.broadcasted_iota(jnp.int32, (fine_rows, MELS), 0)
    frame_fine = (lax.rem(row_fine, row_count) - 1 + index * own_blocks) * 4 + row_fine // row_count
    slope_fine = jnp.where(frame_fine >= 0, (level_wave_fine - level_fine[fine_rows:]) / level_wave_fine, 0.0)
    mel = to_mel(real * real + imag * imag, coarse_bank)
    level = jnp.sqrt(mel + 1.0)
    level_wave = level[:row_count]
    frame = lax.broadcasted_iota(jnp.int32, (row_count, MELS), 0) + index * own_blocks - 3
    slope = jnp.where(frame >= 0, (level_wave - level[row_count:]) / level_wave, 0.0)
    push_fine = 2.0 * from_mel(slope_fine, fine_bank)
    push = 2.0 * from_mel(slope, coarse_bank)
    real, imag = real[:row_count] * push, imag[:row_count] * push
    wide = []
    for rho in range(4):
        columns = slice(rho * LANES, (rho + 1) * LANES)
        first_bin, second_bin = real[:, columns], imag[:, columns]
        wide.append(jnp.concatenate([first_bin, second_bin], axis=1))
        if rho:
            wide.append(jnp.concatenate([second_bin, -first_bin], axis=1))
    wide.append(
        jnp.concatenate([real_fine[:fine_rows] * push_fine, imag_fine[:fine_rows] * push_fine], 1)
    )
    back = dot3(jnp.concatenate(wide, axis=0), turns_h, turns_l, True)
    back_fine = back[7 * row_count :] * taper
    back = [back[i * row_count : (i + 1) * row_count] for i in range(7)]
    back0, back2 = back[0], back[3] * cos[1] - back[4] * sin[1]
    back1 = [
        back[1] * cos[0] - back[2] * sin[0] + back[5] * cos[2] - back[6] * sin[2],
        back[5] * sin[2] + back[6] * cos[2] - back[1] * sin[0] - back[2] * cos[0],
    ]
    fine = []
    for r in range(2):
        total = jnp.zeros((own_blocks, LANES), F32)
        for s in range(4):
            piece = back_fine[s * row_count : (s + 1) * row_count, r * LANES : (r + 1) * LANES]
            if s:
                piece = pltpu.roll(piece, s * hop, 1)
                total = total + jnp.where(
                    lane >= s * hop, piece[1 : 1 + own_blocks], piece[0:own_blocks]
                )
            else:
                total = total + piece[1 : 1 + own_blocks]
        fine.append(total)
    fine = jnp.concatenate(fine, axis=1)

    plus, minus = back0 + back2, back0 - back2
    backs = [
        plus + back1[0],
        minus + back1[1],
        plus - back1[0],
        minus - back1[1],
    ]
    coarse = jnp.zeros((own_blocks, BLOCK), F32)
    for j in range(4):
        coarse = coarse + (backs[j] * hann[j])[3 - j : 3 - j + own_blocks]

    own_rows = pl.ds(own_blocks, own_blocks)
    timed = 2.0 * (wave_b[own_rows, :] - targ_b[own_rows, :])

    streams = (timed, coarse, fine)
    totals = [jnp.sum(stream * stream) for stream in streams]
    lanes_b[...] = jnp.zeros_like(lanes_b)
    for i, stream in enumerate(streams):
        for b in range(own_blocks):
            for r in range(2):
                lanes_b[r, i : i + 1, b * LANES : (b + 1) * LANES] = stream[
                    b : b + 1, r * LANES : (r + 1) * LANES
                ]
    evens, odds = lanes_b[0], lanes_b[1]
    shifted_rows = [moved(odds if k % 2 else evens, MARGIN - (4 - k) // 2) for k in range(8)]
    views = [
        jnp.concatenate([shifted_rows[k][i : i + 1] for k in range(8)], axis=0) for i in range(STREAMS)
    ]
    threes = []
    for view in views:
        high = view.astype(BF16).astype(F32)
        threes.append(jnp.concatenate([high, high, view - high], axis=0).astype(BF16))
    slope_m, slope_u = slope_m * mask, slope_u * mask
    slope_a = slope_a * mask
    grad_mixed = [dot(out_back, three) * slope_m for three in threes]
    mixeds = [split(x) for x in grad_mixed]
    grad_inner = [apply(outer_back, pair) * slope_c for pair in mixeds]
    inners = [split(x) for x in grad_inner]
    spreads = [
        split(jnp.concatenate([moved(x[hidden:], 1), x, moved(x[:hidden], -1)], 0)) for x in grad_inner
    ]
    grad_upper = [
        x + apply(back_inner, pair) * slope_u for x, pair in zip(grad_mixed, spreads)
    ]
    uppers = [split(x) for x in grad_upper]
    low = lane < MARGIN
    slope_edge = jnp.where(low, slope_a[:, :LANES], slope_a[:, frames:])
    edges = []
    for i, value in enumerate(grad_upper):
        upper_ref[i * 2 * half : (i + 1) * 2 * half, :] = value
        head, tail = value[:, :LANES], value[:, frames:]
        both = jnp.concatenate(
            [jnp.where(low, head, tail), jnp.where(low, moved(head, -1), moved(tail, -1))], 0
        )
        turned = jnp.transpose(apply(up_back, split(both)) * slope_edge)
        edges.append(
            jnp.concatenate([turned[MARGIN - REACH : MARGIN], turned[MARGIN : MARGIN + REACH]], axis=1)
        )
    slope_ref[...] = slope_a

    def against(highs, lows, name):
        high, low = saved[name + "_h"], saved[name + "_l"]
        count = high.shape[0]
        wide = dot(highs, jnp.concatenate([high, low], axis=0), True)
        return wide[:, :count] + wide[:, count:] + dot(lows, high, True)

    def summed(pairs, name):
        rows = pairs[0][0].shape[0]
        highs, lows = (jnp.concatenate([pair[i] for pair in pairs], axis=0) for i in range(2))
        value = against(highs, lows, name)
        return [value[i * rows : (i + 1) * rows] for i in range(STREAMS)]

    def put(value, at, columns):
        rows = value.shape[0] // 2
        low, high = value[:rows], value[rows:]
        keep_ref[at : at + rows, columns] = jnp.where(odd_place, high, low)
        send_ref[at : at + rows, columns] = jnp.where(odd_place, low, high)

    step = half + hidden // 2
    for i, value in enumerate(summed(uppers, "a")):
        put(value, i * step, slice(0, 2 * channels))
    for i, value in enumerate(summed(inners, "e")):
        put(value[:hidden, : 3 * half] + value[hidden:, half:], i * step + half, slice(0, 3 * half))
    highs = jnp.concatenate([pair[0] for pair in mixeds], axis=0)
    lows = jnp.concatenate([pair[1] for pair in mixeds], axis=0)
    both = jnp.concatenate([saved["h_h"], saved["h_l"]], axis=0)
    first = dot(both, highs, True)
    value = first[: 2 * hidden] + first[2 * hidden :] + dot(saved["h_h"], lows, True)
    for i in range(STREAMS):
        columns = i * 2 * half
        put(
            value[:hidden, columns : columns + half]
            + value[hidden:, columns + half : columns + 2 * half],
            i * step + half,
            slice(3 * half, 4 * half),
        )
    taps = against(*split(jnp.concatenate(views, axis=0)), "g")
    for i in range(STREAMS):
        wblock[0:7, i * half : (i + 1) * half] = (
            taps[8 * i + 1 : 8 * i + 8, :half] + taps[8 * i : 8 * i + 7, half:]
        )
    lane = lax.broadcasted_iota(jnp.int32, (1, half), 1)
    sums = jnp.where(lane == 0, totals[0], jnp.where(lane == 1, totals[1], totals[2]))
    wblock[7:8, :] = jnp.zeros((1, 4 * half), F32)
    wblock[0:7, STREAMS * half :] = jnp.zeros((7, half), F32)
    wblock[7:8, STREAMS * half :] = sums
    edges = jnp.concatenate(edges, axis=0)
    for ref in (keep_ref, send_ref):
        ref[STREAMS * step : STREAMS * step + 8, :] = wblock[...]
        ref[STREAMS * step + 8 :, :] = edges


def combine_kernel(sizes, mine_ref, theirs_ref, weights_ref, aux_ref):
    half, hidden, samples = sizes
    step = half + hidden // 2
    rows = STREAMS * step
    total = mine_ref[0 : rows + 8, :] + theirs_ref[0 : rows + 8, :]
    line = total[rows + 7 : rows + 8, :]
    lane = lax.broadcasted_iota(jnp.int32, line.shape, 1) - STREAMS * half
    wanted = jnp.where(lane == 0, LOSS_WEIGHTS[0], jnp.where(lane == 1, LOSS_WEIGHTS[1], LOSS_WEIGHTS[2]))
    line = wanted / jnp.sqrt(line / samples + 1e-06)
    scale = [
        jnp.sum(jnp.where(lane == i, line, 0.0), axis=1, keepdims=True) for i in range(STREAMS)
    ]
    weights_ref[0:step, :] = sum(total[i * step : (i + 1) * step] * scale[i] for i in range(STREAMS))
    last = total[rows : rows + 8]
    out = sum(
        (pltpu.roll(last, (4 - i) * half % (4 * half), 1) if i else last) * scale[i]
        for i in range(STREAMS)
    )
    place = lax.broadcasted_iota(jnp.int32, out.shape, 0)
    lane = lax.broadcasted_iota(jnp.int32, out.shape, 1)
    weights_ref[step:, :] = jnp.where((place < 7) & (lane < half), out, 0.0)
    index = lax.axis_index("tm")
    step = lax.axis_size("tm") // 2
    low = lax.rem(index, step)
    edge_lane = lax.broadcasted_iota(jnp.int32, (1, LANES), 1)
    swap = ((low == 0) & (edge_lane >= LANES // 2)) | ((low == step - 1) & (edge_lane < LANES // 2))
    edges = jnp.where(swap, theirs_ref[rows + 8 :, :], mine_ref[rows + 8 :, :])
    aux_ref[0:REACH, :] = sum(edges[REACH * i : REACH * (i + 1)] * scale[i] for i in range(STREAMS))
    for i in range(STREAMS):
        aux_ref[8 + i : 9 + i, :] = jnp.broadcast_to(scale[i], (1, LANES))


def latent_kernel(channels, upper_ref, slope_ref, weight_ref, aux_ref, grad_ref, square):
    frames = grad_ref.shape[2]
    rows = upper_ref.shape[0] // STREAMS
    upper = sum(
        upper_ref[i * rows : (i + 1) * rows, :] * aux_ref[8 + i : 9 + i, 0:1] for i in range(STREAMS)
    )
    both = split(jnp.concatenate([upper, moved(upper, -1)], 0))
    grads = moved(apply(weight_ref[...], both) * slope_ref[...], -MARGIN)[:, :frames]
    square[...] = jnp.zeros_like(square)
    square[0:REACH, 0:channels] = aux_ref[0:REACH, channels:]
    square[LANES - REACH :, channels:] = aux_ref[0:REACH, 0:channels]
    turned = jnp.transpose(square[...])
    grad_ref[0, :, 0:LANES] = grads[:, :LANES] + turned[0:channels]
    grad_ref[0, :, LANES : frames - LANES] = grads[:, LANES : frames - LANES]
    grad_ref[0, :, frames - LANES :] = grads[:, frames - LANES :] + turned[channels:]


def final_kernel(sizes, mine_ref, far_ref, theirs_ref, theirs_far_ref, up_ref, inner_ref, outer_ref, out_ref):
    channels, half, hidden, params = sizes
    step = half + hidden // 2
    mine, theirs = mine_ref[...] + far_ref[...], theirs_ref[...] + theirs_far_ref[...]
    odd_place = lax.rem(lax.axis_index("tm"), 2) == 1
    low = jnp.where(odd_place, theirs[:step], mine[:step])
    high = jnp.where(odd_place, mine[:step], theirs[:step])
    out = mine[step:]
    squares = jnp.sum(low * low) + jnp.sum(high * high) + jnp.sum(out * out)
    factor = jnp.minimum(1.0, 1.0 / jnp.sqrt(jnp.full((1, 1), squares / params + 1e-06, F32)))
    low, high = low * factor, high * factor
    for r, part in enumerate((low, high)):
        up_ref[r] = part[0:half, 0:channels]
        up_ref[r + 2] = part[0:half, channels:]
    inner = jnp.concatenate([low[half:], high[half:]], axis=0)
    for j in range(3):
        inner_ref[j] = inner[:, j * half : (j + 1) * half]
    outer_ref[...] = inner[:, 3 * half :]
    out_ref[...] = (out * factor)[0:7, 0:half]


def run(kernel, out_shape, operands, scratch, name, mebibytes, left=0):
    spec = pl.BlockSpec(memory_space=VMEM)
    kept = len(operands) - left
    hbm = [pltpu.with_memory_space_constraint(x, pltpu.MemorySpace.HBM) for x in operands[kept:]]
    operands = [*operands[:kept], *hbm]
    stay = pl.BlockSpec(memory_space=pltpu.MemorySpace.HBM)
    return pl.pallas_call(
        kernel,
        out_shape=tuple(
            jax.ShapeDtypeStruct(*(x if isinstance(x[1], type) else (x, F32))) for x in out_shape
        ),
        in_specs=[spec] * (len(operands) - left) + [stay] * left,
        out_specs=tuple([spec] * len(out_shape)),
        scratch_shapes=scratch,
        compiler_params=pltpu.CompilerParams(vmem_limit_bytes=mebibytes << 20),
        name=name,
    )(*operands)


def local(latent, target, up_kernel, inner_kernel, outer_kernel, out_kernel):
    assert latent.shape[0] == 1
    channels, frames = latent.shape[1:]
    half, hidden = outer_kernel.shape
    window = frames + LANES
    blocks = frames // LANES
    count = lax.axis_size("tm")
    samples = target.shape[1] * count
    params = sum(x.size for x in (up_kernel, inner_kernel, outer_kernel, out_kernel))

    constants = tables()
    sizes = (channels, half, hidden, frames)
    weights = [up_kernel, inner_kernel, outer_kernel.T, out_kernel]
    forward = [
        ((2 * half, 6 * channels), BF16),
        ((2 * hidden, 12 * half), BF16),
        ((2 * half, 6 * hidden), BF16),
        ((8, 6 * half), BF16),
    ]
    own, own_latent, *made = run(
        lambda *refs: own_kernel(sizes, *refs),
        [
            (8 + 4 * blocks, LANES),
            (channels, frames),
            *forward,
            *kept_shapes(channels, half, hidden, window),
        ],
        [latent, target, *weights],
        [
            *[pltpu.VMEM(x.shape, F32) for x in weights],
            pltpu.VMEM(target.shape, F32),
            pltpu.VMEM((LANES, LANES), F32),
            pltpu.SemaphoreType.DMA((6,)),
        ],
        "own_decode",
        8,
        6,
    )
    backward = run(
        lambda *refs: backward_kernel(sizes, *refs),
        [
            ((channels, 12 * half), BF16),
            ((2 * half, 12 * hidden), BF16),
            ((2 * hidden, 6 * half), BF16),
            ((2 * half, 24), BF16),
            constants[0].shape,
            *[(x.shape, BF16) for x in constants[1:]],
        ],
        [*weights, own, *constants],
        [pltpu.VMEM((LANES, LANES), F32), pltpu.SemaphoreType.DMA((4,))],
        "backward_weights",
        4,
        4,
    )
    pairs = [(i, i ^ 1) for i in range(count) if i ^ 1 < count]
    first = lax.ppermute(own, "tm", pairs)
    pairs = [(i, i + 1 if i % 2 else i - 1) for i in range(count)]
    second = lax.ppermute(own, "tm", [(a, b) for a, b in pairs if 0 <= b < count])

    part = half + hidden // 2
    rows = STREAMS * part

    payload, sent, upper, slope = run(
        lambda *refs: main_kernel(sizes, *refs),
        [
            *[(rows + 8 + REACH * STREAMS, LANES)] * 2,
            (STREAMS * 2 * half, window),
            (channels, window),
        ],
        [own, first, second, own_latent, *made, *backward],
        [
            pltpu.VMEM((LANES, LANES), F32),
            pltpu.VMEM((8, 4 * half), F32),
            pltpu.VMEM((8 * (blocks + 4), BLOCK), F32),
            pltpu.VMEM((3 * blocks, BLOCK), F32),
            pltpu.VMEM((3 * blocks, BLOCK), F32),
            pltpu.VMEM((2, 8, window), F32),
        ],
        "losses",
        16,
    )

    index = lax.axis_index("tm")
    line = lax.broadcasted_iota(jnp.int32, payload.shape, 0)
    lane = lax.broadcasted_iota(jnp.int32, payload.shape, 1)
    step = 1
    while True:
        theirs = lax.ppermute(sent, "tm", [(i, i ^ step) for i in range(count)])
        if 2 * step == count:
            break
        low = index % step
        swap = ((low == 0) & (lane >= LANES // 2)) | ((low == step - 1) & (lane < LANES // 2))
        payload = jnp.where(
            line < rows + 8, payload + theirs, jnp.where(swap, theirs, payload)
        )
        sent = payload
        step *= 2

    weights, aux = run(
        lambda *refs: combine_kernel((half, hidden, samples), *refs),
        [(part + 8, LANES), (16, LANES)],
        [payload, theirs],
        [],
        "combine",
        2,
    )
    (latent_grad,) = run(
        lambda *refs: latent_kernel(channels, *refs),
        [latent.shape],
        [upper, slope, backward[0], aux],
        [pltpu.VMEM((LANES, LANES), F32)],
        "latent",
        4,
    )

    depth = lax.axis_size("dp")
    step = 1
    while 2 * step < depth:
        weights = weights + lax.ppermute(weights, "dp", [(i, i ^ step) for i in range(depth)])
        step *= 2
    places = [(d, t) for d in range(depth) for t in range(count)]

    def partner(far, near):
        pairs = [(d * count + t, (d ^ far) * count + (t ^ near)) for d, t in places]
        return lax.ppermute(weights, ("dp", "tm"), pairs)

    parts = [weights, partner(step, 0), partner(0, 1), partner(step, 1)]
    up, inner, outer, out = run(
        lambda *refs: final_kernel((channels, half, hidden, params), *refs),
        [up_kernel.shape, inner_kernel.shape, outer_kernel.shape[::-1], out_kernel.shape],
        parts,
        [],
        "final",
        2,
    )
    return (latent_grad, up, inner, outer.T, out)


def solution(mesh):
    for axis in ("dp", "tm"):
        size = mesh.shape[axis]
        assert size > 1 and size & (size - 1) == 0
    placed = (P("dp", None, "tm"), P("dp", "tm"), P(), P(), P(), P())
    return jax.shard_map(
        local,
        mesh=mesh,
        in_specs=placed,
        out_specs=(P("dp", None, "tm"), P(), P(), P(), P()),
        check_vma=False,
    )
```

```python
import jax
import jax.numpy as jnp
import numpy as np
from jax import lax
from jax.experimental import pallas as pl
from jax.experimental.pallas import tpu as pltpu
from jax.sharding import PartitionSpec as P

MELS = 64
WIN_COARSE = 1024
WIN_FINE = 256
LOSS_WEIGHTS = (0.25, 0.5, 0.5)
LANES = 128
BLOCK = 2 * LANES
STREAMS = 3
REACH = 3
MARGIN = LANES // 2
F32 = jnp.float32
BF16 = jnp.bfloat16
VMEM = pltpu.MemorySpace.VMEM


def hi_lo(table):
    high = table.astype(np.float32).astype(BF16)
    low = (table - high.astype(np.float64)).astype(np.float32).astype(BF16)
    return high, low


def mel_table(window):
    half = window // 2
    top = 2595.0 * np.log10(1.0 + 12000.0 / 700.0)
    points = (np.arange(MELS + 1) + 1.0) / (MELS + 2.0) * top
    centers = 700.0 * (10.0 ** (points / 2595.0) - 1.0) / 12000.0 * half
    spacing = np.maximum(centers[1:] - centers[:-1], 1.0)
    places = np.arange(half)[:, None]
    return np.maximum(0.0, 1.0 - np.abs(places - centers[None, :MELS]) / spacing[None, :])


def tables():
    order = np.concatenate([np.arange(0, BLOCK, 2), np.arange(1, BLOCK, 2)])
    angle = 2.0 * np.pi / BLOCK * ((order[:, None] * np.arange(LANES)[None, :]) % BLOCK)
    turns = np.concatenate([np.cos(angle), -np.sin(angle)], 1)
    coarse_mel = mel_table(WIN_COARSE)
    coarse_mel = np.concatenate([coarse_mel[rho::4] for rho in range(4)], 0)
    fine_mel = mel_table(WIN_FINE)
    hann = 0.5 - 0.5 * np.cos(2.0 * np.pi / WIN_COARSE * np.arange(WIN_COARSE))
    twist = 2.0 * np.pi / WIN_COARSE * np.arange(1, 4)[:, None] * order[None, :]
    taper = 0.5 - 0.5 * np.cos(2.0 * np.pi / WIN_FINE * order)[None, :]
    lines = [hann.reshape(4, BLOCK)[:, order], np.cos(twist), np.sin(twist), taper]
    lines = np.concatenate(lines + [np.zeros((5, BLOCK))], 0).astype(np.float32)
    deal = np.zeros((BLOCK, BLOCK), np.float32)
    deal[order, np.arange(BLOCK)] = 1.0
    banks = [np.concatenate(hi_lo(x), 1) for x in (coarse_mel, fine_mel)]
    return lines, np.concatenate(hi_lo(turns), 0), np.concatenate(banks, 0), deal.astype(BF16)


def split(x):
    high = x.astype(BF16)
    return high, (x - high.astype(F32)).astype(BF16)


def stacked(x):
    high = x.astype(BF16).astype(F32)
    return jnp.concatenate([high, x - high], axis=0).astype(BF16)


def dot(left, right, transposed=False):
    dims = (((1,), (1 if transposed else 0,)), ((), ()))
    return lax.dot_general(left, right, dims, preferred_element_type=F32)


def dot3(left, right_high, right_low, transposed=False):
    rows = left.shape[0]
    both = stacked(left)
    first = dot(both, right_high, transposed)
    second = dot(left.astype(BF16), right_low, transposed)
    return first[:rows] + first[rows:] + second


def to_mel(energy, bank):
    rows = energy.shape[0]
    both = dot(stacked(energy), bank)
    both = both[:rows] + both[rows:]
    return both[:, :MELS] + both[:, MELS:]


def from_mel(push, bank):
    rows = push.shape[0]
    both = dot(stacked(jnp.concatenate([push, push], axis=1)), bank, True)
    return both[:rows] + both[rows:]


def three_wide(weight):
    high = weight.astype(BF16).astype(F32)
    return jnp.concatenate([high, weight - high, high], axis=1).astype(BF16)


def apply(weight3, pair):
    high, low = pair
    return dot(weight3, jnp.concatenate([high, high, low], axis=0))


def elu_pair(x):
    slope = jnp.exp(jnp.minimum(x, 0.0))
    return jnp.where(x > 0, x, slope - 1.0), slope


def moved(x, by):
    return pltpu.roll(x, by % x.shape[1], 1)


def decode(sizes, weights, latent, keep, mask):
    half = sizes[1]
    activated, slope = elu_pair(latent)
    keep("slope_a", slope)
    both = jnp.concatenate([activated, moved(activated, 1)], 0)
    pair = split(both)
    keep("a", pair)
    upper = apply(weights["up"], pair) * mask
    rect, slope = elu_pair(upper)
    keep("slope_u", slope)
    pair = split(
        jnp.concatenate([moved(rect[half:], 1), rect, moved(rect[:half], -1)], 0)
    )
    keep("e", pair)
    hid, slope = elu_pair(apply(weights["inner"], pair))
    keep("slope_c", slope)
    pair = split(hid)
    keep("h", pair)
    mixed = (upper + apply(weights["outer"], pair)) * mask
    rect, slope = elu_pair(mixed)
    keep("slope_m", slope)
    pair = split(rect)
    keep("g", pair)
    taps = apply(weights["out"], pair)
    plus1, plus2, minus1, minus2 = (moved(taps, by) for by in (1, 2, -1, -2))
    return (
        (plus2[0:1] + plus1[2:3] + taps[4:5] + minus1[6:7]) * mask,
        (plus1[1:2] + taps[3:4] + minus1[5:6] + minus2[7:8]) * mask,
    )


KEPT = ("slope_a", "a_h", "a_l", "slope_u", "e_h", "e_l", "slope_c", "h_h", "h_l", "slope_m", "g_h", "g_l")


def kept_shapes(channels, half, hidden, window):
    rows = (channels, 2 * channels, 2 * half, 4 * half, 2 * hidden, 2 * hidden, 2 * half, 2 * half)
    shapes = []
    for i in range(4):
        shapes.append(((rows[2 * i], window), F32))
        shapes += [((rows[2 * i + 1], window), BF16)] * 2
    return shapes


def forward_weights(sizes, up, inner, outer, out, square):
    channels, half, hidden, _ = sizes
    weights = {}
    weights["up"] = three_wide(
        jnp.concatenate(
            [jnp.concatenate([up[r], up[r + 2]], axis=1) for r in range(2)], axis=0
        )
    )
    square[...] = jnp.zeros_like(square)
    for j in range(3):
        square[0:hidden, j * half : (j + 1) * half] = inner[j]
        square[hidden : 2 * hidden, (j + 1) * half : (j + 2) * half] = inner[j]
    weights["inner"] = three_wide(square[0 : 2 * hidden, :])
    square[...] = jnp.zeros_like(square)
    square[0:hidden, 0:half] = outer[...]
    square[hidden : 2 * hidden, half : 2 * half] = outer[...]
    weights["outer"] = three_wide(jnp.transpose(square[...])[0 : 2 * half, 0 : 2 * hidden])
    square[...] = jnp.zeros_like(square)
    square[1:8, 0:half] = out[...]
    square[0:7, half : 2 * half] = out[...]
    weights["out"] = three_wide(square[0:8, 0 : 2 * half])
    return weights


FORWARD = ("up", "inner", "outer", "out")


def backward_kernel(sizes, *refs):
    up, inner, outer, out = refs[:4]
    up_ref, inner_ref, outer_ref, out_ref = refs[9:13]
    square, sems = refs[17:]
    copies = [pltpu.make_async_copy(refs[5 + i], refs[13 + i], sems.at[i]) for i in range(4)]
    for copy in copies:
        copy.start()
    channels, half, hidden, _ = sizes
    for r in range(4):
        square[r * half : (r + 1) * half, 0:channels] = up[r]
        square[r * half : (r + 1) * half, channels:] = up[r]
    up_ref[...] = three_wide(jnp.transpose(square[...])[0:channels, :])
    square[...] = jnp.zeros_like(square)
    for j in range(3):
        square[(2 - j) * hidden : (3 - j) * hidden, 0:half] = inner[j]
        square[(3 - j) * hidden : (4 - j) * hidden, half : 2 * half] = inner[j]
    inner_ref[...] = three_wide(jnp.transpose(square[...])[0 : 2 * half, 0 : 4 * hidden])
    square[...] = jnp.zeros_like(square)
    square[0:hidden, 0:half] = outer[...]
    square[hidden : 2 * hidden, half : 2 * half] = outer[...]
    outer_ref[...] = three_wide(square[0 : 2 * hidden, 0 : 2 * half])
    square[...] = jnp.zeros_like(square)
    square[1:8, 0:half] = out[...]
    square[0:7, half : 2 * half] = out[...]
    out_ref[...] = three_wide(jnp.transpose(square[...])[0 : 2 * half, 0:8])
    for copy in copies:
        copy.wait()


def own_kernel(sizes, *refs):
    sources = refs[:6]
    packet_ref, latent_ref = refs[6:8]
    weight_refs = refs[8:12]
    kept = dict(zip(KEPT, refs[12:24]))
    up_ref, inner_ref, outer_ref, out_ref, target_ref, square, sems = refs[24:]
    channels, half, hidden, frames = sizes
    spaces = (latent_ref, target_ref, up_ref, inner_ref, outer_ref, out_ref)
    copies = []
    for i, (source, space) in enumerate(zip(sources, spaces)):
        if i == 0:
            source = source.at[0]
        copies.append(pltpu.make_async_copy(source, space, sems.at[i]))
    for copy in copies:
        copy.start()
    for copy in copies:
        copy.wait()
    weights = forward_weights(sizes, up_ref, inner_ref, outer_ref, out_ref, square)
    for name, ref in zip(FORWARD, weight_refs):
        ref[...] = weights[name]

    def keep(name, value):
        if isinstance(value, tuple):
            kept[name + "_h"][...], kept[name + "_l"][...] = value
        else:
            kept[name][...] = value

    latent = latent_ref[...]
    spread = moved(jnp.concatenate([latent, jnp.zeros((channels, LANES), F32)], 1), MARGIN)
    wave = jnp.concatenate(decode(sizes, weights, spread, keep, 1.0), 0)
    wave = moved(wave, -MARGIN)
    blocks = frames // LANES
    packet_ref[0:8, 0:channels] = jnp.transpose(latent[:, 0:LANES])[0:8]
    packet_ref[0:8, channels:] = jnp.transpose(latent[:, frames - LANES :])[LANES - 8 :]
    for r in range(2):
        for b in range(blocks):
            packet_ref[8 + r * blocks + b : 9 + r * blocks + b, :] = wave[
                r : r + 1, b * LANES : (b + 1) * LANES
            ]
    for row in range(2 * blocks):
        at = 8 + 2 * blocks + row
        packet_ref[at : at + 1, :] = target_ref[:, row * LANES : (row + 1) * LANES]


def main_kernel(sizes, *refs):
    own_ref, first_ref, second_ref, latent_ref = refs[:4]
    weights = {name: ref[...] for name, ref in zip(FORWARD, refs[4:8])}
    kept = dict(zip(KEPT, refs[8:20]))
    up_back, back_inner, outer_back, out_back = (ref[...] for ref in refs[20:24])
    lines_ref, turns_ref, bank_ref, deal_ref = refs[24:28]
    keep_ref, send_ref, upper_ref, slope_ref = refs[28:32]
    (square, wblock, shifted, wave_b, targ_b, lanes_b) = refs[32:38]
    channels, half, hidden, frames = sizes
    window = frames + LANES
    own_blocks = frames // LANES
    index = lax.axis_index("tm")
    count = lax.axis_size("tm")
    odd_place = lax.rem(index, 2) == 1

    first, second = first_ref[...], second_ref[...]
    left = jnp.where(odd_place, first, second)
    right = jnp.where(odd_place, second, first)
    for side, packet in enumerate((left, own_ref[...], right)):
        rows = slice(side * own_blocks, (side + 1) * own_blocks)
        for r in range(2):
            columns = slice(r * LANES, (r + 1) * LANES)
            at = 8 + r * own_blocks
            wave_b[rows, columns] = packet[at : at + own_blocks]
            for b in range(own_blocks):
                at = 8 + 2 * own_blocks + 2 * b + r
                row = side * own_blocks + b
                targ_b[row : row + 1, columns] = packet[at : at + 1]
    whole = targ_b[...]
    high = whole.astype(BF16).astype(F32)
    middle = (whole - high).astype(BF16).astype(F32)
    dealt = dot(
        jnp.concatenate([high, middle, whole - high - middle], axis=0).astype(BF16), deal_ref[...]
    )
    size = targ_b.shape[0]
    targ_b[...] = dealt[:size] + dealt[size : 2 * size] + dealt[2 * size :]
    square[...] = jnp.zeros_like(square)
    square[MARGIN - 8 : MARGIN, 0:channels] = left[0:8, channels:]
    square[MARGIN : MARGIN + 8, channels:] = right[0:8, 0:channels]
    turned = jnp.transpose(square[...])
    lane = lax.broadcasted_iota(jnp.int32, (1, LANES), 1)
    ends = jnp.concatenate(
        [
            jnp.where(lane < MARGIN, turned[0:channels], moved(latent_ref[:, 0:LANES], MARGIN)),
            jnp.where(
                lane < MARGIN, moved(latent_ref[:, frames - LANES :], MARGIN), turned[channels:]
            ),
        ],
        axis=1,
    )
    place = lax.broadcasted_iota(jnp.int32, (1, window), 1) + index * frames - MARGIN
    mask = ((place >= 0) & (place < count * frames)).astype(F32)
    ends_mask = jnp.concatenate([mask[:, :LANES], mask[:, window - LANES :]], axis=1)
    saved = {}

    def joined(name, value):
        inside = kept[name]
        quarter = LANES // 4
        lane = lax.broadcasted_iota(jnp.int32, (value.shape[0], LANES), 1)
        head = jnp.where(lane < 3 * quarter, value[:, :LANES], inside[:, :LANES])
        tail = jnp.where(lane >= quarter, value[:, LANES:], inside[:, window - LANES :])
        saved[name] = jnp.concatenate([head, inside[:, LANES : window - LANES], tail], axis=1)

    def keep(name, value):
        if isinstance(value, tuple):
            joined(name + "_h", value[0])
            joined(name + "_l", value[1])
        else:
            joined(name, value)

    ends_wave = decode(sizes, weights, ends, keep, ends_mask)
    slope_a, slope_u, slope_c, slope_m = (saved["slope_" + x] for x in "aucm")

    for r in range(2):
        columns = slice(r * LANES, (r + 1) * LANES)
        for side in range(2):
            piece = moved(ends_wave[r][:, side * LANES : (side + 1) * LANES], MARGIN)
            row = own_blocks * (1 + side)
            wave_b[row - 1 : row, columns] = jnp.where(
                lane >= LANES - 4, piece, wave_b[row - 1 : row, columns]
            )
            wave_b[row : row + 1, columns] = jnp.where(lane < 4, piece, wave_b[row : row + 1, columns])
    turns_h, turns_l = turns_ref[0:BLOCK], turns_ref[BLOCK:]
    coarse_bank, fine_bank = bank_ref[0 : 2 * BLOCK], bank_ref[2 * BLOCK :]
    line = [lines_ref[i : i + 1, :] for i in range(11)]
    hann, cos, sin, taper = line[0:4], line[4:7], line[7:10], line[10]

    row_count = own_blocks + 4
    start = own_blocks - 3
    parts = []
    for j in range(4):
        rows = jnp.concatenate(
            [wave_b[pl.ds(start + j, row_count), :], targ_b[pl.ds(start + j, row_count), :]], 0
        )
        parts.append(rows * hann[j])
    even_sum, odd_sum = parts[0] + parts[2], parts[1] + parts[3]
    pair0, pair1 = even_sum + odd_sum, even_sum - odd_sum
    part0, part1 = parts[0] - parts[2], parts[1] - parts[3]
    blocks_in = [
        pair0,
        part0 * cos[0] - part1 * sin[0],
        -part1 * cos[0] - part0 * sin[0],
        pair1 * cos[1],
        -pair1 * sin[1],
        part0 * cos[2] + part1 * sin[2],
        part1 * cos[2] - part0 * sin[2],
    ]

    hop = LANES // 4
    lane = lax.broadcasted_iota(jnp.int32, (1, LANES), 1)
    start_fine = own_blocks - 1
    for which, source in enumerate((wave_b, targ_b)):
        for s in range(4):
            base = (which * 4 + s) * row_count
            for r in range(2):
                here = source[pl.ds(start_fine, row_count), r * LANES : (r + 1) * LANES]
                if s:
                    there = source[pl.ds(start_fine + 1, row_count), r * LANES : (r + 1) * LANES]
                    here = jnp.where(
                        lane < LANES - s * hop,
                        pltpu.roll(here, LANES - s * hop, 1),
                        pltpu.roll(there, LANES - s * hop, 1),
                    )
                shifted[base : base + row_count, r * LANES : (r + 1) * LANES] = here
    spec = dot3(jnp.concatenate([*blocks_in, shifted[...] * taper], axis=0), turns_h, turns_l)
    rows = 2 * row_count
    bins = [spec[i * rows : (i + 1) * rows] for i in range(7)]
    real, imag = [bins[0][:, :LANES]], [bins[0][:, LANES:]]
    for first_bin, second_bin in (bins[1:3], bins[3:5], bins[5:7]):
        real.append(first_bin[:, :LANES] - second_bin[:, LANES:])
        imag.append(first_bin[:, LANES:] + second_bin[:, :LANES])
    real, imag = jnp.concatenate(real, axis=1), jnp.concatenate(imag, axis=1)
    spec_fine = spec[7 * rows :]
    real_fine, imag_fine = spec_fine[:, :LANES], spec_fine[:, LANES:]
    mel_fine = to_mel(real_fine * real_fine + imag_fine * imag_fine, fine_bank)
    level_fine = jnp.sqrt(mel_fine + 1.0)
    fine_rows = 4 * row_count
    level_wave_fine = level_fine[:fine_rows]
    row_fine = lax.broadcasted_iota(jnp.int32, (fine_rows, MELS), 0)
    frame_fine = (lax.rem(row_fine, row_count) - 1 + index * own_blocks) * 4 + row_fine // row_count
    slope_fine = jnp.where(frame_fine >= 0, (level_wave_fine - level_fine[fine_rows:]) / level_wave_fine, 0.0)
    mel = to_mel(real * real + imag * imag, coarse_bank)
    level = jnp.sqrt(mel + 1.0)
    level_wave = level[:row_count]
    frame = lax.broadcasted_iota(jnp.int32, (row_count, MELS), 0) + index * own_blocks - 3
    slope = jnp.where(frame >= 0, (level_wave - level[row_count:]) / level_wave, 0.0)
    push_fine = 2.0 * from_mel(slope_fine, fine_bank)
    push = 2.0 * from_mel(slope, coarse_bank)
    real, imag = real[:row_count] * push, imag[:row_count] * push
    wide = []
    for rho in range(4):
        columns = slice(rho * LANES, (rho + 1) * LANES)
        first_bin, second_bin = real[:, columns], imag[:, columns]
        wide.append(jnp.concatenate([first_bin, second_bin], axis=1))
        if rho:
            wide.append(jnp.concatenate([second_bin, -first_bin], axis=1))
    wide.append(
        jnp.concatenate([real_fine[:fine_rows] * push_fine, imag_fine[:fine_rows] * push_fine], 1)
    )
    back = dot3(jnp.concatenate(wide, axis=0), turns_h, turns_l, True)
    back_fine = back[7 * row_count :] * taper
    back = [back[i * row_count : (i + 1) * row_count] for i in range(7)]
    back0, back2 = back[0], back[3] * cos[1] - back[4] * sin[1]
    back1 = [
        back[1] * cos[0] - back[2] * sin[0] + back[5] * cos[2] - back[6] * sin[2],
        back[5] * sin[2] + back[6] * cos[2] - back[1] * sin[0] - back[2] * cos[0],
    ]
    fine = []
    for r in range(2):
        total = jnp.zeros((own_blocks, LANES), F32)
        for s in range(4):
            piece = back_fine[s * row_count : (s + 1) * row_count, r * LANES : (r + 1) * LANES]
            if s:
                piece = pltpu.roll(piece, s * hop, 1)
                total = total + jnp.where(
                    lane >= s * hop, piece[1 : 1 + own_blocks], piece[0:own_blocks]
                )
            else:
                total = total + piece[1 : 1 + own_blocks]
        fine.append(total)
    fine = jnp.concatenate(fine, axis=1)

    plus, minus = back0 + back2, back0 - back2
    backs = [
        plus + back1[0],
        minus + back1[1],
        plus - back1[0],
        minus - back1[1],
    ]
    coarse = jnp.zeros((own_blocks, BLOCK), F32)
    for j in range(4):
        coarse = coarse + (backs[j] * hann[j])[3 - j : 3 - j + own_blocks]

    own_rows = pl.ds(own_blocks, own_blocks)
    timed = 2.0 * (wave_b[own_rows, :] - targ_b[own_rows, :])

    streams = (timed, coarse, fine)
    totals = [jnp.sum(stream * stream) for stream in streams]
    lanes_b[...] = jnp.zeros_like(lanes_b)
    for i, stream in enumerate(streams):
        for b in range(own_blocks):
            for r in range(2):
                lanes_b[r, i : i + 1, b * LANES : (b + 1) * LANES] = stream[
                    b : b + 1, r * LANES : (r + 1) * LANES
                ]
    evens, odds = lanes_b[0], lanes_b[1]
    shifted_rows = [moved(odds if k % 2 else evens, MARGIN - (4 - k) // 2) for k in range(8)]
    views = [
        jnp.concatenate([shifted_rows[k][i : i + 1] for k in range(8)], axis=0) for i in range(STREAMS)
    ]
    threes = []
    for view in views:
        high = view.astype(BF16).astype(F32)
        threes.append(jnp.concatenate([high, high, view - high], axis=0).astype(BF16))
    slope_m, slope_u = slope_m * mask, slope_u * mask
    slope_a = slope_a * mask
    grad_mixed = [dot(out_back, three) * slope_m for three in threes]
    mixeds = [split(x) for x in grad_mixed]
    grad_inner = [apply(outer_back, pair) * slope_c for pair in mixeds]
    inners = [split(x) for x in grad_inner]
    spreads = [
        split(jnp.concatenate([moved(x[hidden:], 1), x, moved(x[:hidden], -1)], 0)) for x in grad_inner
    ]
    grad_upper = [
        x + apply(back_inner, pair) * slope_u for x, pair in zip(grad_mixed, spreads)
    ]
    uppers = [split(x) for x in grad_upper]
    low = lane < MARGIN
    slope_edge = jnp.where(low, slope_a[:, :LANES], slope_a[:, frames:])
    edges = []
    for i, value in enumerate(grad_upper):
        upper_ref[i * 2 * half : (i + 1) * 2 * half, :] = value
        head, tail = value[:, :LANES], value[:, frames:]
        both = jnp.concatenate(
            [jnp.where(low, head, tail), jnp.where(low, moved(head, -1), moved(tail, -1))], 0
        )
        turned = jnp.transpose(apply(up_back, split(both)) * slope_edge)
        edges.append(
            jnp.concatenate([turned[MARGIN - REACH : MARGIN], turned[MARGIN : MARGIN + REACH]], axis=1)
        )
    slope_ref[...] = slope_a

    def against(highs, lows, name):
        high, low = saved[name + "_h"], saved[name + "_l"]
        count = high.shape[0]
        wide = dot(highs, jnp.concatenate([high, low], axis=0), True)
        return wide[:, :count] + wide[:, count:] + dot(lows, high, True)

    def summed(pairs, name):
        rows = pairs[0][0].shape[0]
        highs, lows = (jnp.concatenate([pair[i] for pair in pairs], axis=0) for i in range(2))
        value = against(highs, lows, name)
        return [value[i * rows : (i + 1) * rows] for i in range(STREAMS)]

    def put(value, at, columns):
        rows = value.shape[0] // 2
        low, high = value[:rows], value[rows:]
        keep_ref[at : at + rows, columns] = jnp.where(odd_place, high, low)
        send_ref[at : at + rows, columns] = jnp.where(odd_place, low, high)

    step = half + hidden // 2
    for i, value in enumerate(summed(uppers, "a")):
        put(value, i * step, slice(0, 2 * channels))
    for i, value in enumerate(summed(inners, "e")):
        put(value[:hidden, : 3 * half] + value[hidden:, half:], i * step + half, slice(0, 3 * half))
    highs = jnp.concatenate([pair[0] for pair in mixeds], axis=0)
    lows = jnp.concatenate([pair[1] for pair in mixeds], axis=0)
    both = jnp.concatenate([saved["h_h"], saved["h_l"]], axis=0)
    first = dot(both, highs, True)
    value = first[: 2 * hidden] + first[2 * hidden :] + dot(saved["h_h"], lows, True)
    for i in range(STREAMS):
        columns = i * 2 * half
        put(
            value[:hidden, columns : columns + half]
            + value[hidden:, columns + half : columns + 2 * half],
            i * step + half,
            slice(3 * half, 4 * half),
        )
    taps = against(*split(jnp.concatenate(views, axis=0)), "g")
    for i in range(STREAMS):
        wblock[0:7, i * half : (i + 1) * half] = (
            taps[8 * i + 1 : 8 * i + 8, :half] + taps[8 * i : 8 * i + 7, half:]
        )
    lane = lax.broadcasted_iota(jnp.int32, (1, half), 1)
    sums = jnp.where(lane == 0, totals[0], jnp.where(lane == 1, totals[1], totals[2]))
    wblock[7:8, :] = jnp.zeros((1, 4 * half), F32)
    wblock[0:7, STREAMS * half :] = jnp.zeros((7, half), F32)
    wblock[7:8, STREAMS * half :] = sums
    edges = jnp.concatenate(edges, axis=0)
    for ref in (keep_ref, send_ref):
        ref[STREAMS * step : STREAMS * step + 8, :] = wblock[...]
        ref[STREAMS * step + 8 :, :] = edges


def combine_kernel(sizes, mine_ref, theirs_ref, weights_ref, aux_ref):
    half, hidden, samples = sizes
    step = half + hidden // 2
    rows = STREAMS * step
    total = mine_ref[0 : rows + 8, :] + theirs_ref[0 : rows + 8, :]
    line = total[rows + 7 : rows + 8, :]
    lane = lax.broadcasted_iota(jnp.int32, line.shape, 1) - STREAMS * half
    wanted = jnp.where(lane == 0, LOSS_WEIGHTS[0], jnp.where(lane == 1, LOSS_WEIGHTS[1], LOSS_WEIGHTS[2]))
    line = wanted / jnp.sqrt(line / samples + 1e-06)
    scale = [
        jnp.sum(jnp.where(lane == i, line, 0.0), axis=1, keepdims=True) for i in range(STREAMS)
    ]
    weights_ref[0:step, :] = sum(total[i * step : (i + 1) * step] * scale[i] for i in range(STREAMS))
    last = total[rows : rows + 8]
    out = sum(
        (pltpu.roll(last, (4 - i) * half % (4 * half), 1) if i else last) * scale[i]
        for i in range(STREAMS)
    )
    place = lax.broadcasted_iota(jnp.int32, out.shape, 0)
    lane = lax.broadcasted_iota(jnp.int32, out.shape, 1)
    weights_ref[step:, :] = jnp.where((place < 7) & (lane < half), out, 0.0)
    index = lax.axis_index("tm")
    step = lax.axis_size("tm") // 2
    low = lax.rem(index, step)
    edge_lane = lax.broadcasted_iota(jnp.int32, (1, LANES), 1)
    swap = ((low == 0) & (edge_lane >= LANES // 2)) | ((low == step - 1) & (edge_lane < LANES // 2))
    edges = jnp.where(swap, theirs_ref[rows + 8 :, :], mine_ref[rows + 8 :, :])
    aux_ref[0:REACH, :] = sum(edges[REACH * i : REACH * (i + 1)] * scale[i] for i in range(STREAMS))
    for i in range(STREAMS):
        aux_ref[8 + i : 9 + i, :] = jnp.broadcast_to(scale[i], (1, LANES))


def latent_kernel(channels, upper_ref, slope_ref, weight_ref, aux_ref, grad_ref, square):
    frames = grad_ref.shape[2]
    rows = upper_ref.shape[0] // STREAMS
    upper = sum(
        upper_ref[i * rows : (i + 1) * rows, :] * aux_ref[8 + i : 9 + i, 0:1] for i in range(STREAMS)
    )
    both = split(jnp.concatenate([upper, moved(upper, -1)], 0))
    grads = moved(apply(weight_ref[...], both) * slope_ref[...], -MARGIN)[:, :frames]
    square[...] = jnp.zeros_like(square)
    square[0:REACH, 0:channels] = aux_ref[0:REACH, channels:]
    square[LANES - REACH :, channels:] = aux_ref[0:REACH, 0:channels]
    turned = jnp.transpose(square[...])
    grad_ref[0, :, 0:LANES] = grads[:, :LANES] + turned[0:channels]
    grad_ref[0, :, LANES : frames - LANES] = grads[:, LANES : frames - LANES]
    grad_ref[0, :, frames - LANES :] = grads[:, frames - LANES :] + turned[channels:]


def final_kernel(sizes, mine_ref, far_ref, theirs_ref, theirs_far_ref, up_ref, inner_ref, outer_ref, out_ref):
    channels, half, hidden, params = sizes
    step = half + hidden // 2
    mine, theirs = mine_ref[...] + far_ref[...], theirs_ref[...] + theirs_far_ref[...]
    odd_place = lax.rem(lax.axis_index("tm"), 2) == 1
    low = jnp.where(odd_place, theirs[:step], mine[:step])
    high = jnp.where(odd_place, mine[:step], theirs[:step])
    out = mine[step:]
    squares = jnp.sum(low * low) + jnp.sum(high * high) + jnp.sum(out * out)
    factor = jnp.minimum(1.0, 1.0 / jnp.sqrt(jnp.full((1, 1), squares / params + 1e-06, F32)))
    low, high = low * factor, high * factor
    for r, part in enumerate((low, high)):
        up_ref[r] = part[0:half, 0:channels]
        up_ref[r + 2] = part[0:half, channels:]
    inner = jnp.concatenate([low[half:], high[half:]], axis=0)
    for j in range(3):
        inner_ref[j] = inner[:, j * half : (j + 1) * half]
    outer_ref[...] = inner[:, 3 * half :]
    out_ref[...] = (out * factor)[0:7, 0:half]


def run(kernel, out_shape, operands, scratch, name, mebibytes, left=0):
    spec = pl.BlockSpec(memory_space=VMEM)
    kept = len(operands) - left
    hbm = [pltpu.with_memory_space_constraint(x, pltpu.MemorySpace.HBM) for x in operands[kept:]]
    operands = [*operands[:kept], *hbm]
    stay = pl.BlockSpec(memory_space=pltpu.MemorySpace.HBM)
    return pl.pallas_call(
        kernel,
        out_shape=tuple(
            jax.ShapeDtypeStruct(*(x if isinstance(x[1], type) else (x, F32))) for x in out_shape
        ),
        in_specs=[spec] * (len(operands) - left) + [stay] * left,
        out_specs=tuple([spec] * len(out_shape)),
        scratch_shapes=scratch,
        compiler_params=pltpu.CompilerParams(vmem_limit_bytes=mebibytes << 20),
        name=name,
    )(*operands)


def local(latent, target, up_kernel, inner_kernel, outer_kernel, out_kernel):
    assert latent.shape[0] == 1
    channels, frames = latent.shape[1:]
    half, hidden = outer_kernel.shape
    window = frames + LANES
    blocks = frames // LANES
    count = lax.axis_size("tm")
    samples = target.shape[1] * count
    params = sum(x.size for x in (up_kernel, inner_kernel, outer_kernel, out_kernel))

    constants = tables()
    sizes = (channels, half, hidden, frames)
    weights = [up_kernel, inner_kernel, outer_kernel.T, out_kernel]
    forward = [
        ((2 * half, 6 * channels), BF16),
        ((2 * hidden, 12 * half), BF16),
        ((2 * half, 6 * hidden), BF16),
        ((8, 6 * half), BF16),
    ]
    own, own_latent, *made = run(
        lambda *refs: own_kernel(sizes, *refs),
        [
            (8 + 4 * blocks, LANES),
            (channels, frames),
            *forward,
            *kept_shapes(channels, half, hidden, window),
        ],
        [latent, target, *weights],
        [
            *[pltpu.VMEM(x.shape, F32) for x in weights],
            pltpu.VMEM(target.shape, F32),
            pltpu.VMEM((LANES, LANES), F32),
            pltpu.SemaphoreType.DMA((6,)),
        ],
        "own_decode",
        8,
        6,
    )
    backward = run(
        lambda *refs: backward_kernel(sizes, *refs),
        [
            ((channels, 12 * half), BF16),
            ((2 * half, 12 * hidden), BF16),
            ((2 * hidden, 6 * half), BF16),
            ((2 * half, 24), BF16),
            constants[0].shape,
            *[(x.shape, BF16) for x in constants[1:]],
        ],
        [*weights, own, *constants],
        [pltpu.VMEM((LANES, LANES), F32), pltpu.SemaphoreType.DMA((4,))],
        "backward_weights",
        4,
        4,
    )
    pairs = [(i, i ^ 1) for i in range(count) if i ^ 1 < count]
    first = lax.ppermute(own, "tm", pairs)
    pairs = [(i, i + 1 if i % 2 else i - 1) for i in range(count)]
    second = lax.ppermute(own, "tm", [(a, b) for a, b in pairs if 0 <= b < count])

    part = half + hidden // 2
    rows = STREAMS * part

    payload, sent, upper, slope = run(
        lambda *refs: main_kernel(sizes, *refs),
        [
            *[(rows + 8 + REACH * STREAMS, LANES)] * 2,
            (STREAMS * 2 * half, window),
            (channels, window),
        ],
        [own, first, second, own_latent, *made, *backward],
        [
            pltpu.VMEM((LANES, LANES), F32),
            pltpu.VMEM((8, 4 * half), F32),
            pltpu.VMEM((8 * (blocks + 4), BLOCK), F32),
            pltpu.VMEM((3 * blocks, BLOCK), F32),
            pltpu.VMEM((3 * blocks, BLOCK), F32),
            pltpu.VMEM((2, 8, window), F32),
        ],
        "losses",
        16,
    )

    index = lax.axis_index("tm")
    line = lax.broadcasted_iota(jnp.int32, payload.shape, 0)
    lane = lax.broadcasted_iota(jnp.int32, payload.shape, 1)

    def exchange(x, mask):
        return lax.ppermute(x, "tm", [(i, i ^ mask) for i in range(count)])

    def merge(mine, theirs, passed, step):
        low = index % step
        swap = ((low == 0) & (lane >= LANES // 2)) | ((low == step - 1) & (lane < LANES // 2))
        return jnp.where(line < rows + 8, mine + theirs, jnp.where(swap, theirs, passed))

    if count < 8:
        payload = merge(payload, exchange(sent, 1), payload, 1)
        step = 2
    else:
        near, across, far = exchange(sent, 1), exchange(payload, 2), exchange(sent, 3)
        low = index % 2
        swap = ((low == 0) & (lane >= LANES // 2)) | ((low == 1) & (lane < LANES // 2))
        payload = jnp.where(
            line < rows + 8, (payload + near) + (across + far), jnp.where(swap, far, near)
        )
        step = 4
    while True:
        theirs = exchange(payload, step)
        if 2 * step == count:
            break
        payload = merge(payload, theirs, payload, step)
        step *= 2

    weights, aux = run(
        lambda *refs: combine_kernel((half, hidden, samples), *refs),
        [(part + 8, LANES), (16, LANES)],
        [payload, theirs],
        [],
        "combine",
        2,
    )
    (latent_grad,) = run(
        lambda *refs: latent_kernel(channels, *refs),
        [latent.shape],
        [upper, slope, backward[0], aux],
        [pltpu.VMEM((LANES, LANES), F32)],
        "latent",
        4,
    )

    depth = lax.axis_size("dp")
    step = 1
    while 2 * step < depth:
        weights = weights + lax.ppermute(weights, "dp", [(i, i ^ step) for i in range(depth)])
        step *= 2
    places = [(d, t) for d in range(depth) for t in range(count)]

    def partner(far, near):
        pairs = [(d * count + t, (d ^ far) * count + (t ^ near)) for d, t in places]
        return lax.ppermute(weights, ("dp", "tm"), pairs)

    parts = [weights, partner(step, 0), partner(0, 1), partner(step, 1)]
    up, inner, outer, out = run(
        lambda *refs: final_kernel((channels, half, hidden, params), *refs),
        [up_kernel.shape, inner_kernel.shape, outer_kernel.shape[::-1], out_kernel.shape],
        parts,
        [],
        "final",
        2,
    )
    return (latent_grad, up, inner, outer.T, out)


def solution(mesh):
    for axis in ("dp", "tm"):
        size = mesh.shape[axis]
        assert size > 1 and size & (size - 1) == 0
    placed = (P("dp", None, "tm"), P("dp", "tm"), P(), P(), P(), P())
    return jax.shard_map(
        local,
        mesh=mesh,
        in_specs=placed,
        out_specs=(P("dp", None, "tm"), P(), P(), P(), P()),
        check_vma=False,
    )
```
